32 devices in a mesh: dp: 8 (over z, x), fsdp: 4 (over y, core).
Axes of the slice: x: 2, y: 2, z: 4, core: 2. Of those that a mesh axis runs over, the one named last changes fastest.
Arguments:
- inputs: bfloat16 [32, 1024, 512], P(('dp', 'fsdp')), may hold values from -6 to 6
- noisy_ids: int32 [32, 1024], P(('dp', 'fsdp')), may hold values from 0 to 26
- timesteps: int32 [32, 4], P(('dp', 'fsdp')), may hold values from 0 to 999
- doc_lens: int32 [32, 4], P(('dp', 'fsdp')), may hold values from 0 to 1024, as said below
- cotangent: bfloat16 [32, 1024, 512], P(('dp', 'fsdp')), may hold values from -6 to 6
- params: float32 [3296768], P(('dp', 'fsdp'))
- momentum: float32 [3296768], P(('dp', 'fsdp'))
- average: float32 [3296768], P(('dp', 'fsdp'))
Outputs:
- activations: bfloat16 [32, 1024, 512], P(('dp', 'fsdp'))
- input_grad: float32 [32, 1024, 512], P(('dp', 'fsdp'))
- new_params: float32 [3296768], P(('dp', 'fsdp'))
- new_momentum: float32 [3296768], P(('dp', 'fsdp'))
- new_average: float32 [3296768], P(('dp', 'fsdp'))
- params_low: bfloat16 [3296768], P(('dp', 'fsdp'))
The draws below stay inside these ranges and needn't reach their ends.
Inputs may be any that keep to these rules, and one draw needn't show every extreme that they name: Each row is either long, with doc_lens[r] = [L, 0, 0, 0] and L from 512 to 1024, or short, with every entry from 128 to 256. In every draw some row is long with L = 1024 and some short row has a slot of exactly 256.
All inputs are finite; a program needn't handle non-finite values.
Results may differ from the reference program's by a relative error of at most 0.011.
Values may be sent and summed in bfloat16 or wider, within the bound.
A program may use at most 192 MiB of HBM per device.

```python
import math
import jax
import jax.numpy as jnp
from jax import lax

D = 512
HEADS = 8
FF = 2048
VOCAB = 27
STEPS = 1000
TDIM = 256
S = 1024
PACK = 4
ROWS = 32
TOKENS = 32768
PARAMS = 3296768


def layout_drawn(model_width, hidden, time_dim, vocab_size):
    shapes = [(model_width, 3 * model_width), (model_width, model_width), (model_width, hidden), (hidden, model_width), (time_dim, model_width), (vocab_size, model_width), (8, model_width), (hidden,)]
    starts = []
    offset = 0
    for member_shape in shapes:
        starts.append(offset)
        offset = offset + math.prod(member_shape)
    return (shapes, starts)


def segment_scales(member_scales):
    shapes, starts = layout_drawn(D, FF, TDIM, VOCAB)
    positions = jnp.arange(PARAMS)
    scales = jnp.full((PARAMS,), 0.1, jnp.float32)
    for member_shape, member_start, member_scale in zip(shapes, starts, member_scales):
        inside = (positions >= member_start) & (positions < member_start + math.prod(member_shape))
        scales = jnp.where(inside, jnp.float32(member_scale), scales)
    return scales


def weight_field(key):
    shapes, starts = layout_drawn(D, FF, TDIM, VOCAB)
    scales = segment_scales([D ** (-0.5), 0.5, D ** (-0.5), FF ** (-0.5), TDIM ** (-0.5), 1.0, 0.3, 0.3])
    noise_draw = jax.random.truncated_normal(jax.random.fold_in(key, 11), -3.0, 3.0, (PARAMS,), jnp.float32)
    positions = jnp.arange(PARAMS)
    vector_start = starts[6]
    gain_mask = (positions >= vector_start) & (positions < vector_start + D) | (positions >= vector_start + 2 * D) & (positions < vector_start + 3 * D)
    gain_vals = 1.0 + 0.3 * jax.random.uniform(jax.random.fold_in(key, 12), (PARAMS,), jnp.float32, -1.0, 1.0)
    return jnp.where(gain_mask, gain_vals, scales * noise_draw)


def draw_params(key, part):
    return weight_field(jax.random.fold_in(key, 1))


def draw_average(key, part):
    return weight_field(jax.random.fold_in(key, 5))


def draw_momentum(key, part):
    scales = segment_scales([0.2, 0.05, 0.5, 0.5, 0.5, 0.2, 1.0, 0.5])
    noise_draw = jax.random.truncated_normal(jax.random.fold_in(key, 3), -3.0, 3.0, (PARAMS,), jnp.float32)
    return scales * noise_draw


def draw_doc_lens(key, part):
    slot_len = S // PACK
    keys_list = jax.random.split(key, 5)
    long_flags = jax.random.randint(keys_list[0], (ROWS,), 0, 2)
    forced_long = jax.random.randint(keys_list[1], (), 0, ROWS)
    forced_short = (forced_long + 1 + jax.random.randint(keys_list[2], (), 0, ROWS - 1)) % ROWS
    row_ids = jnp.arange(ROWS)
    long_flags = jnp.where(row_ids == forced_long, 1, jnp.where(row_ids == forced_short, 0, long_flags))
    long_lens = jax.random.randint(keys_list[3], (ROWS,), S // 2, S + 1)
    long_lens = jnp.where(row_ids == forced_long, S, long_lens)
    short_lens = jax.random.randint(keys_list[4], (ROWS, PACK), slot_len // 2, slot_len + 1)
    first_col = jnp.arange(PACK)[None, :] == 0
    short_lens = jnp.where((row_ids[:, None] == forced_short) & first_col, slot_len, short_lens)
    long_rows = jnp.where(first_col, long_lens[:, None], 0)
    return jnp.where(long_flags[:, None] == 1, long_rows, short_lens).astype(jnp.int32)


def with_ends(values, key, smallest, top_value):
    dims = values.shape
    place = [jax.random.randint(jax.random.fold_in(key, axis), (), 0, dims[axis]) for axis in range(len(dims))]
    values = values.at[tuple(place)].set(smallest)
    longest = dims.index(max(dims))
    place[longest] = (place[longest] + 1) % dims[longest]
    return values.at[tuple(place)].set(top_value)


def block_levels(stream_key, shape, cuts, smallest, largest):
    def one(dim, shards_of):
        steps = jax.random.uniform(jax.random.fold_in(jax.random.fold_in(stream_key, 6), dim), (shards_of,), jnp.float32, smallest / len(cuts), largest / len(cuts))
        return jnp.repeat(jnp.exp(steps), shape[dim] // shards_of).reshape((-1,) + (1,) * (len(shape) - dim - 1))

    loudness = one(*cuts[0])
    for cut in cuts[1:]:
        loudness = loudness * one(*cut)
    return loudness


def gaussian(own_key, shape, scale, limit, cuts=(), kind=jnp.bfloat16):
    factor_of = block_levels(own_key, shape, cuts, -0.22, 0.18) if cuts else 1.0
    entries = jax.random.normal(own_key, shape, jnp.float32) * scale * factor_of
    return jnp.minimum(jnp.maximum(entries, -limit), limit).astype(kind)


def setup_inputs(seed: int = 0) -> dict:
    streams_of = jax.random.split(jax.random.key(seed), 9)
    return {
        "inputs": gaussian(streams_of[0], (ROWS, S, D), 1.0, 6.0, ((0, 32),)),
        "noisy_ids": with_ends(jax.random.randint(streams_of[1], (ROWS, S), 0, VOCAB), jax.random.fold_in(streams_of[1], 1), 0, VOCAB - 1).astype(jnp.int32),
        "timesteps": with_ends(jax.random.randint(streams_of[2], (ROWS, PACK), 0, STEPS), jax.random.fold_in(streams_of[2], 1), 0, STEPS - 1).astype(jnp.int32),
        "doc_lens": draw_doc_lens(jax.random.fold_in(streams_of[8], 71), 0),
        "cotangent": gaussian(streams_of[4], (ROWS, S, D), 1.0, 6.0, ((0, 32),)),
        "params": draw_params(jax.random.fold_in(streams_of[8], 71), 0),
        "momentum": draw_momentum(jax.random.fold_in(streams_of[8], 71), 0),
        "average": draw_average(jax.random.fold_in(streams_of[8], 71), 0),
    }


@jax.custom_vjp
def low(v):
    return lax.optimization_barrier(v.astype(jnp.bfloat16)).astype(jnp.float32)

@jax.custom_vjp
def low_back(v):
    return v

def low_keep(v):
    return (low(v), None)

def low_pass(kept, grad):
    return (grad,)

def back_keep(v):
    return (v, None)

def back_low(kept, grad):
    return (low(grad),)
low.defvjp(low_keep, low_pass)
low_back.defvjp(back_keep, back_low)
EPSILON = 1e-05
MOMENTUM_RATE = 0.9
LEARN_RATE = 0.02
AVERAGE_RATE = 0.8
HIGHEST_PRECISION = lax.Precision.HIGHEST

def layout(model_width, hidden, time_dim, vocab_size):
    shapes = [(model_width, 3 * model_width), (model_width, model_width), (model_width, hidden), (hidden, model_width), (time_dim, model_width), (vocab_size, model_width), (8, model_width), (hidden,)]
    starts = []
    offset = 0
    for member_shape in shapes:
        starts.append(offset)
        offset = offset + math.prod(member_shape)
    return (shapes, starts, offset)

def matmul(left, right):
    return jnp.dot(left, right, precision=HIGHEST_PRECISION)

def layer_norm(stream, norm_gain, norm_bias):
    row_mean = lax.optimization_barrier(jnp.mean(stream, axis=-1, keepdims=True))
    centered = stream - row_mean
    row_var = lax.optimization_barrier(jnp.mean(centered * centered, axis=-1, keepdims=True))
    return centered * lax.rsqrt(row_var + EPSILON) * norm_gain + norm_bias

def row_layout(doc_lens, seq_len):
    pack_count = doc_lens.shape[-1]
    slot_len = seq_len // pack_count
    position = jnp.arange(seq_len, dtype=jnp.int32)
    slot_of = jnp.where(doc_lens[..., 1:2] == 0, 0, position // slot_len).astype(jnp.int32)
    inside = position - slot_of * slot_len
    slot_hot = slot_of[..., None] == jnp.arange(pack_count, dtype=jnp.int32)
    doc_length = lax.optimization_barrier(jnp.sum(jnp.where(slot_hot, doc_lens[..., None, :], 0), axis=-1))
    return (slot_of, slot_hot, inside < doc_length)

def time_features(step_pos, time_dim):
    half_dim = time_dim // 2
    freqs = jnp.exp(-math.log(10000.0) * jnp.arange(half_dim, dtype=jnp.float32) / half_dim)
    angles = step_pos.astype(jnp.float32)[..., None] * freqs
    return jnp.concatenate([jnp.sin(angles), jnp.cos(angles)], axis=-1)

def row_forward(weights, row_input, row_ids, row_steps, row_lens):
    shapes, starts, total_len = layout(D, FF, TDIM, VOCAB)
    pieces = [weights[member_start:member_start + math.prod(member_shape)].reshape(member_shape) for member_shape, member_start in zip(shapes, starts)]
    w_qkv, w_out, w_up, w_down, w_time, char_table, vectors, up_bias = pieces
    seq_len = row_input.shape[0]
    head_dim = D // HEADS
    slot_of, slot_hot, is_valid = row_layout(row_lens, seq_len)
    step_pos = lax.optimization_barrier(jnp.sum(jnp.where(slot_hot, row_steps[None, :], 0), axis=-1))
    features = low(time_features(step_pos, TDIM))
    side_sum = low_back(jnp.take(char_table, row_ids, axis=0) + matmul(features, w_time))
    resid0 = row_input + side_sum
    attn_in = low(layer_norm(resid0, vectors[0], vectors[1]))
    qkv_bias = jnp.concatenate([vectors[4], jnp.zeros_like(vectors[4]), vectors[5]])
    proj_qkv = low(low_back(matmul(attn_in, w_qkv) + qkv_bias))
    queries = proj_qkv[:, :D].reshape(seq_len, HEADS, head_dim)
    keys_all = proj_qkv[:, D:2 * D].reshape(seq_len, HEADS, head_dim)
    values = proj_qkv[:, 2 * D:].reshape(seq_len, HEADS, head_dim)
    scores = low_back(jnp.einsum('qhd,khd->hqk', queries, keys_all, precision=HIGHEST_PRECISION) * head_dim ** (-0.5))
    allowed = (slot_of[:, None] == slot_of[None, :]) & is_valid[None, :]
    scores = jnp.where(allowed[None], scores, -1e+30)
    attn_probs = jax.nn.softmax(scores, axis=-1)
    attended = jnp.einsum('hqk,khd->qhd', low(attn_probs), values, precision=HIGHEST_PRECISION).reshape(seq_len, D)
    attended = low(low_back(attended))
    resid1 = resid0 + low_back(matmul(attended, w_out) + vectors[6])
    ffn_in = low(layer_norm(resid1, vectors[2], vectors[3]))
    pre_act = low_back(matmul(ffn_in, w_up) + up_bias)
    activated = low(jax.nn.gelu(pre_act, approximate=False))
    return resid1 + low_back(matmul(activated, w_down) + vectors[7])

def reference(inputs, noisy_ids, timesteps, doc_lens, cotangent, params, momentum, average):
    weights = params.astype(jnp.bfloat16).astype(jnp.float32)
    row_inputs = inputs.astype(jnp.float32)

    def forward(weights, row_inputs):
        row_step = jax.checkpoint(row_forward)
        return lax.map(lambda member: row_step(weights, *member), (row_inputs, noisy_ids, timesteps, doc_lens))
    output, pullback = jax.vjp(forward, weights, row_inputs)
    is_valid = row_layout(doc_lens, S)[2]
    cot_eff = cotangent.astype(jnp.float32) * is_valid[..., None].astype(jnp.float32)
    grad_weights, input_grad = pullback(cot_eff)
    gradient = grad_weights * (1.0 / math.sqrt(TOKENS))
    new_momentum = MOMENTUM_RATE * momentum + gradient
    new_params = params - LEARN_RATE * (gradient + MOMENTUM_RATE * new_momentum)
    new_average = AVERAGE_RATE * average + (1.0 - AVERAGE_RATE) * new_params
    return (output.astype(jnp.bfloat16), input_grad, new_params, new_momentum, new_average, new_params.astype(jnp.bfloat16))
```

```python
from functools import partial
import math

import jax
import jax.numpy as jnp
from jax import lax
from jax.experimental import pallas as pl
from jax.experimental.pallas import tpu as pltpu
from jax.sharding import PartitionSpec as P

D = 512
HEADS = 8
FF = 2048
VOCAB = 27
TDIM = 256


EPSILON = 1e-05
MOMENTUM_RATE = 0.9
LEARN_RATE = 0.02
AVERAGE_RATE = 0.8


def layout(model_width, hidden, time_dim, vocab_size):
    shapes = [
        (model_width, 3 * model_width),
        (model_width, model_width),
        (model_width, hidden),
        (hidden, model_width),
        (time_dim, model_width),
        (vocab_size, model_width),
        (8, model_width),
        (hidden,),
    ]
    starts = []
    offset = 0
    for member_shape in shapes:
        starts.append(offset)
        offset = offset + math.prod(member_shape)
    return (shapes, starts, offset)


def unpack(gathered):
    shapes, starts, total_len = layout(D, FF, TDIM, VOCAB)
    return [
        gathered[member_start : member_start + math.prod(member_shape)].reshape(member_shape)
        for member_shape, member_start in zip(shapes, starts)
    ]


def layer_norm(stream, norm_gain, norm_bias):
    row_mean = jnp.mean(stream, axis=-1, keepdims=True)
    centered = stream - row_mean
    row_var = jnp.mean(centered * centered, axis=-1, keepdims=True)
    return centered * lax.rsqrt(row_var + EPSILON) * norm_gain + norm_bias


def row_layout(doc_lens, seq_len):
    pack_count = doc_lens.shape[-1]
    slot_len = seq_len // pack_count
    position = jnp.arange(seq_len, dtype=jnp.int32)
    slot_of = jnp.where(doc_lens[..., 1:2] == 0, 0, position // slot_len)
    inside = position - slot_of * slot_len
    slot_hot = slot_of[..., None] == jnp.arange(pack_count, dtype=jnp.int32)
    doc_length = jnp.sum(jnp.where(slot_hot, doc_lens[..., None, :], 0), axis=-1)
    return (slot_of, slot_hot, inside < doc_length)


def time_features(step_pos, time_dim):
    half_dim = time_dim // 2
    freqs = jnp.exp(-math.log(10000.0) * jnp.arange(half_dim, dtype=jnp.float32) / half_dim)
    angles = step_pos.astype(jnp.float32)[..., None] * freqs
    return jnp.concatenate([jnp.sin(angles), jnp.cos(angles)], axis=-1)


MESH = pl.DeviceIdType.MESH
ROW = 512
TILE = 16
BF = jnp.bfloat16
F32 = jnp.float32


class Plan:
    def __init__(self, ndp, nfs, total):
        self.nx, self.ny, self.nc = 2, nfs // 2, 2
        self.nz = ndp // 2
        self.count = ndp * nfs
        self.share = total // self.count
        self.total = total
        self.starts = [self.start(i) for i in range(self.count)]
        ends = [-(-((i + 1) * self.share) // ROW) for i in range(self.count)]
        need = max(e - s for e, s in zip(ends, self.starts))
        self.rows = -(-need // 32) * 32
        self.half = self.rows // 2
        self.padded = max(self.starts) + self.rows

    def start(self, i):
        return ((i * self.share) // (ROW * TILE)) * TILE

    def index(self, z, x, y, c):
        return ((z * self.nx + x) * self.ny + y) * self.nc + c


class Place:
    def __init__(self, plan):
        d = lax.axis_index("dp")
        f = lax.axis_index("fsdp")
        self.plan = plan
        self.z, self.x = d // plan.nx, d % plan.nx
        self.y, self.c = f // plan.nc, f % plan.nc

    def dev(self, z=None, x=None, y=None, c=None):
        z = self.z if z is None else z
        x = self.x if x is None else x
        y = self.y if y is None else y
        c = self.c if c is None else c
        return (z * self.plan.nx + x, y * self.plan.nc + c)

    @property
    def X(self):
        return self.dev(x=1 - self.x)

    @property
    def Y(self):
        return self.dev(y=1 - self.y)

    @property
    def C(self):
        return self.dev(c=1 - self.c)


def greet(place, nz):
    bar = pltpu.get_barrier_semaphore()
    for dev in (place.X, place.Y, place.C):
        pl.semaphore_signal(bar, inc=1, device_id=dev, device_id_type=MESH)
    for s in range(1, nz):
        pl.semaphore_signal(bar, inc=1, device_id=place.dev(z=(place.z + s) % nz), device_id_type=MESH)
    pl.semaphore_wait(bar, 3 + nz - 1)


def rcopy(src, dst, ss, rs, dev):
    return pltpu.make_async_remote_copy(src_ref=src, dst_ref=dst, send_sem=ss, recv_sem=rs, device_id=dev, device_id_type=MESH)


AG_KINDS = 13


def gather_events(plan, layers, g, zs, zr, ps, pr):
    p = Place(plan)
    z, x, y, c, nz, h, n = p.z, p.x, p.y, p.c, plan.nz, plan.half, plan.rows
    A, B, W = pl.ds(0, h), pl.ds(h, h), pl.ds(0, n)

    def at(r, xx, yy, part):
        return g.at[r, xx, yy, c, part]

    def zcopy(r, j, up):
        ref = g.at[r, x, y, c, (A, B)[j]]
        return rcopy(ref, ref, zs.at[r, j, 0 if up else 1], zr.at[r, j], p.dev(z=z + 1 if up else z - 1))

    def cp(r, k):
        table = {
            0: (at(r, x, y, A), p.X), 1: (at(r, x, y, B), p.Y),
            2: (at(r, x, y, A), p.Y), 3: (at(r, x, y, B), p.X),
            4: (at(r, 1 - x, y, A), p.Y), 5: (at(r, x, 1 - y, B), p.X),
            6: (at(r, x, y, W), p.C), 7: (at(r, 1 - x, y, A), p.C), 8: (at(r, x, 1 - y, B), p.C),
            9: (at(r, x, 1 - y, A), p.C), 10: (at(r, 1 - x, 1 - y, A), p.C),
            11: (at(r, 1 - x, y, B), p.C), 12: (at(r, 1 - x, 1 - y, B), p.C),
        }
        ref, dev = table[k]
        return rcopy(ref, ref, ps.at[r, k], pr.at[r, k], dev)

    def stage0(r):
        for j in (0, 1):
            if r < nz - 1:
                @pl.when(z == r)
                def _(): zcopy(r, j, True).start()
            if r > 0:
                @pl.when(z == r)
                def _(): zcopy(r, j, False).start()

    def stage1(r):
        for j in (0, 1):
            @pl.when(z != r)
            def _(): zcopy(r, j, True).wait_recv()
            if r < nz - 1:
                @pl.when((z > r) & (z < nz - 1))
                def _(): zcopy(r, j, True).start()
            if r > 0:
                @pl.when((z < r) & (z > 0))
                def _(): zcopy(r, j, False).start()
            cp(r, j).start()
        for k in (2, 3, 6):
            cp(r, k).start()

    def stage2(r):
        cp(r, 0).wait_recv()
        cp(r, 4).start()
        cp(r, 7).start()
        cp(r, 1).wait_recv()
        cp(r, 5).start()
        cp(r, 8).start()

    def stage3(r):
        for k, kk in ((2, 9), (4, 10), (3, 11), (5, 12)):
            cp(r, k).wait_recv()
            cp(r, kk).start()

    def stage4(r):
        for k in range(6, 13):
            cp(r, k).wait_recv()

    def drain():
        for r in layers:
            for j in (0, 1):
                if r < nz - 1:
                    @pl.when((z >= r) & (z < nz - 1))
                    def _(): zcopy(r, j, True).wait_send()
                if r > 0:
                    @pl.when((z <= r) & (z > 0))
                    def _(): zcopy(r, j, False).wait_send()
            for k in range(AG_KINDS):
                cp(r, k).wait_send()

    return [stage0, stage1, stage2, stage3, stage4], drain


def pipelined(stages, layers):
    order = []
    for t in range(len(layers) + len(stages) - 1):
        for s in reversed(range(len(stages))):
            j = t - s
            if 0 <= j < len(layers):
                order.append((stages[s], layers[j]))
    return order


def gather_scratch(plan):
    nz = plan.nz
    D = pltpu.SemaphoreType.DMA
    return [D((nz, 2, 2)), D((nz, 2)), D((nz, AG_KINDS)), D((nz, AG_KINDS))]


def assemble(plan, g, out, write=None):
    n = plan.rows
    for i in range(plan.count):
        cc = i % 2; yy = (i // 2) % 2; xx = (i // 4) % 2; zz = i // 8
        s = plan.starts[i]
        e = plan.starts[i + 1] if i + 1 < plan.count else plan.padded
        head = g[zz, xx, yy, cc, 0:TILE, :]
        if i:
            j = i - 1
            d = s - plan.starts[j]
            if d < n:
                head = head + g[j // 8, (j // 4) % 2, (j // 2) % 2, j % 2, d:d + TILE, :]
        out[s:s + TILE, :] = head
        if e - s > TILE:
            out[s + TILE:e, :] = g[zz, xx, yy, cc, TILE:e - s, :]


def gather_all(plan, chunk, cid):
    nz, n = plan.nz, plan.rows
    layers = list(range(nz))

    def kern(chunk_ref, out_ref, g, zs, zr, ps, pr, ls):
        p = Place(plan)
        greet(p, nz)
        cpy = pltpu.make_async_copy(chunk_ref, g.at[p.z, p.x, p.y, p.c], ls)
        cpy.start(); cpy.wait()
        stages, drain = gather_events(plan, layers, g, zs, zr, ps, pr)
        for st, r in pipelined(stages, layers):
            st(r)
        assemble(plan, g, out_ref)
        drain()

    return pl.pallas_call(
        kern, out_shape=jax.ShapeDtypeStruct((plan.padded, ROW), BF),
        in_specs=[pl.BlockSpec(memory_space=pltpu.VMEM)],
        out_specs=pl.BlockSpec(memory_space=pltpu.VMEM),
        scratch_shapes=[pltpu.VMEM((nz, 2, 2, 2, n, ROW), BF)] + gather_scratch(plan) + [pltpu.SemaphoreType.DMA],
        compiler_params=pltpu.CompilerParams(collective_id=cid, has_side_effects=True, vmem_limit_bytes=60 << 20),
        name="gather_all",
    )(chunk)


def reduce_events(plan, layers, src, cb, pa, pb, p2, zb, cs, cr, ps, pr, zs, zr):
    p = Place(plan)
    z, x, y, c, nz, h, n = p.z, p.x, p.y, p.c, plan.nz, plan.half, plan.rows

    def rows(r, xx, yy, cc):
        i = plan.index(r, xx, yy, cc)
        return pl.ds(pl.multiple_of(((i * plan.share) // (ROW * TILE)) * TILE, TILE), n)

    def ccopy(r, xx, yy):
        return rcopy(src.at[rows(r, xx, yy, 1 - c)], cb.at[r, xx, yy], cs.at[r, xx, yy], cr.at[r, xx, yy], p.C)

    def cp(r, k):
        table = {
            0: (cb.at[r, :, 1 - y, pl.ds(0, h)], pa.at[r], p.Y),
            1: (cb.at[r, 1 - x, :, pl.ds(h, h)], pb.at[r], p.X),
            2: (pa.at[r, 1 - x], p2.at[r, pl.ds(0, h)], p.X),
            3: (pb.at[r, 1 - y], p2.at[r, pl.ds(h, h)], p.Y),
        }
        s, d, dev = table[k]
        return rcopy(s, d, ps.at[r, k], pr.at[r, k], dev)

    def zcopy(r):
        return rcopy(p2.at[r], zb.at[z], zs.at[r], zr.at[z], p.dev(z=r))

    def zwait(s):
        return rcopy(p2.at[0], zb.at[s], zs.at[0], zr.at[s], p.dev(z=s))

    def stage0(r):
        for xx in (0, 1):
            for yy in (0, 1):
                ccopy(r, xx, yy).start()

    def stage1(r):
        for xx in (0, 1):
            for yy in (0, 1):
                ccopy(r, xx, yy).wait_recv()
                cb[r, xx, yy] = (cb[r, xx, yy].astype(F32) + src[rows(r, xx, yy, c), :].astype(F32)).astype(BF)
        cp(r, 0).start()
        cp(r, 1).start()

    def stage2(r):
        cp(r, 0).wait_recv()
        for xx in (0, 1):
            pa[r, xx] = (pa[r, xx].astype(F32) + cb[r, xx, y, 0:h].astype(F32)).astype(BF)
        cp(r, 2).start()
        cp(r, 1).wait_recv()
        for yy in (0, 1):
            pb[r, yy] = (pb[r, yy].astype(F32) + cb[r, x, yy, h:n].astype(F32)).astype(BF)
        cp(r, 3).start()

    def stage3(r):
        cp(r, 2).wait_recv()
        p2[r, 0:h] = (p2[r, 0:h].astype(F32) + pa[r, x].astype(F32)).astype(BF)
        cp(r, 3).wait_recv()
        p2[r, h:n] = (p2[r, h:n].astype(F32) + pb[r, y].astype(F32)).astype(BF)
        @pl.when(z != r)
        def _(): zcopy(r).start()

    def finish(out, mine):
        out[...] = p2[mine].astype(F32)
        for s in range(nz):
            @pl.when(z != s)
            def _():
                zwait(s).wait_recv()
                out[...] += zb[s].astype(F32)

    def drain():
        for r in layers:
            for xx in (0, 1):
                for yy in (0, 1):
                    ccopy(r, xx, yy).wait_send()
            for k in range(4):
                cp(r, k).wait_send()
            @pl.when(z != r)
            def _(): zcopy(r).wait_send()

    return [stage0, stage1, stage2, stage3], finish, drain


def reduce_scratch(plan):
    nz, n, h = plan.nz, plan.rows, plan.half
    D = pltpu.SemaphoreType.DMA
    return [pltpu.VMEM((nz, 2, 2, n, ROW), BF), pltpu.VMEM((nz, 2, h, ROW), BF), pltpu.VMEM((nz, 2, h, ROW), BF),
            pltpu.VMEM((nz, n, ROW), BF), pltpu.VMEM((nz, n, ROW), BF),
            D((nz, 2, 2)), D((nz, 2, 2)), D((nz, 4)), D((nz, 4)), D((nz,)), D((nz,))]


def reduce_all(plan, src, cid):
    nz, n = plan.nz, plan.rows
    layers = list(range(1, nz)) + [0]

    def kern(src_ref, out_ref, *rest):
        p = Place(plan)
        greet(p, nz)
        stages, finish, drain = reduce_events(plan, layers, src_ref, *rest)
        for st, r in pipelined(stages, layers):
            st(r)
        finish(out_ref, p.z)
        drain()

    return pl.pallas_call(
        kern, out_shape=jax.ShapeDtypeStruct((n, ROW), F32),
        in_specs=[pl.BlockSpec(memory_space=pltpu.VMEM)],
        out_specs=pl.BlockSpec(memory_space=pltpu.VMEM),
        scratch_shapes=reduce_scratch(plan),
        compiler_params=pltpu.CompilerParams(collective_id=cid, has_side_effects=True, vmem_limit_bytes=60 << 20),
        name="reduce_all",
    )(src)


def block_scores(query_block, keys_all, slot_of, is_valid, row_start, block_rows, score_scale):
    scores = (
        jnp.einsum("rqhd,rkhd->rhqk", query_block, keys_all, preferred_element_type=jnp.float32)
        * score_scale
    )
    allowed = (
        slot_of[:, row_start : row_start + block_rows, None] == slot_of[:, None, :]
    ) & is_valid[:, None, :]
    return jnp.where(allowed[:, None], scores, -1e30)


def attention_forward(queries, keys_all, values, slot_of, is_valid):
    row_count, seq_len, head_count, head_dim = queries.shape
    block_rows = min(512, seq_len)
    score_scale = head_dim ** (-0.5)
    outputs = []
    totals = []
    for block_index in range(seq_len // block_rows):
        row_start = block_index * block_rows
        query_block = queries[:, row_start : row_start + block_rows]
        scores = block_scores(
            query_block, keys_all, slot_of, is_valid, row_start, block_rows, score_scale
        )
        row_max = jnp.max(scores, axis=-1, keepdims=True)
        exp_scores = jnp.exp(scores - row_max)
        row_total = jnp.sum(exp_scores, axis=-1, keepdims=True)
        attn_probs = (exp_scores / row_total).astype(jnp.bfloat16)
        outputs.append(
            jnp.einsum("rhqk,rkhd->rqhd", attn_probs, values, preferred_element_type=jnp.float32)
        )
        totals.append((row_max + jnp.log(row_total))[..., 0])
    return (jnp.concatenate(outputs, axis=1).astype(jnp.bfloat16), jnp.concatenate(totals, axis=2))


def attention_backward(queries, keys_all, values, log_total, d_attended, slot_of, is_valid):
    row_count, seq_len, head_count, head_dim = queries.shape
    block_rows = min(512, seq_len)
    score_scale = head_dim ** (-0.5)
    grad_queries = []
    grad_keys = jnp.zeros(queries.shape, jnp.float32)
    grad_values = jnp.zeros(queries.shape, jnp.float32)
    for block_index in range(seq_len // block_rows):
        row_start = block_index * block_rows
        query_block = queries[:, row_start : row_start + block_rows]
        scores = block_scores(
            query_block, keys_all, slot_of, is_valid, row_start, block_rows, score_scale
        )
        attn_probs = jnp.exp(scores - log_total[:, :, row_start : row_start + block_rows, None])
        d_out_block = d_attended[:, row_start : row_start + block_rows]
        grad_values = grad_values + jnp.einsum(
            "rhqk,rqhd->rkhd",
            attn_probs.astype(jnp.bfloat16),
            d_out_block,
            preferred_element_type=jnp.float32,
        )
        d_probs = jnp.einsum(
            "rqhd,rkhd->rhqk", d_out_block, values, preferred_element_type=jnp.float32
        )
        d_scores = (
            attn_probs * (d_probs - jnp.sum(attn_probs * d_probs, axis=-1, keepdims=True))
        ).astype(jnp.bfloat16)
        grad_queries.append(
            jnp.einsum("rhqk,rkhd->rqhd", d_scores, keys_all, preferred_element_type=jnp.float32)
            * score_scale
        )
        grad_keys = (
            grad_keys
            + jnp.einsum(
                "rhqk,rqhd->rkhd", d_scores, query_block, preferred_element_type=jnp.float32
            )
            * score_scale
        )
    return (jnp.concatenate(grad_queries, axis=1), grad_keys, grad_values)


def forward_pass(pieces, inputs, noisy_ids, timesteps, doc_lens):
    w_qkv, w_out, w_up, w_down, w_time, char_table, vectors, up_bias = pieces
    row_count, seq_len, model_width = inputs.shape
    head_dim = model_width // HEADS
    tokens_here = row_count * seq_len
    slot_of, slot_hot, is_valid = row_layout(doc_lens, seq_len)
    step_pos = jnp.sum(jnp.where(slot_hot, timesteps[:, None, :], 0), axis=-1)
    features = (
        time_features(step_pos, w_time.shape[0])
        .astype(jnp.bfloat16)
        .reshape(tokens_here, w_time.shape[0])
    )
    vocab_size = char_table.shape[0]
    one_hot = (
        noisy_ids.reshape(tokens_here, 1) == jnp.arange(vocab_size, dtype=jnp.int32)[None, :]
    ).astype(jnp.bfloat16)
    side_sum = jnp.dot(one_hot, char_table, preferred_element_type=jnp.float32) + jnp.dot(
        features, w_time, preferred_element_type=jnp.float32
    )
    resid0 = inputs.reshape(tokens_here, model_width).astype(jnp.float32) + side_sum
    vector_rows = vectors.astype(jnp.float32)
    attn_in = layer_norm(resid0, vector_rows[0], vector_rows[1]).astype(jnp.bfloat16)
    qkv_bias = jnp.concatenate([vector_rows[4], jnp.zeros_like(vector_rows[4]), vector_rows[5]])
    proj_qkv = (jnp.dot(attn_in, w_qkv, preferred_element_type=jnp.float32) + qkv_bias).astype(
        jnp.bfloat16
    )
    proj_qkv = proj_qkv.reshape(row_count, seq_len, 3, HEADS, head_dim)
    queries = proj_qkv[:, :, 0]
    keys_all = proj_qkv[:, :, 1]
    values = proj_qkv[:, :, 2]
    attended, log_total = attention_forward(queries, keys_all, values, slot_of, is_valid)
    attended_flat = attended.reshape(tokens_here, model_width)
    resid1 = resid0 + (
        jnp.dot(attended_flat, w_out, preferred_element_type=jnp.float32) + vector_rows[6]
    )
    ffn_in = layer_norm(resid1, vector_rows[2], vector_rows[3]).astype(jnp.bfloat16)
    pre_act = jnp.dot(ffn_in, w_up, preferred_element_type=jnp.float32) + up_bias.astype(
        jnp.float32
    )
    activated = jax.nn.gelu(pre_act, approximate=False).astype(jnp.bfloat16)
    output = resid1 + (
        jnp.dot(activated, w_down, preferred_element_type=jnp.float32) + vector_rows[7]
    )
    saved_state = (
        one_hot,
        features,
        resid0,
        attn_in,
        queries,
        keys_all,
        values,
        log_total,
        attended_flat,
        resid1,
        ffn_in,
        pre_act,
        activated,
        is_valid,
        slot_of,
    )
    return (output, saved_state)


def backward_pass(pieces, saved_state, cot_eff, total_len):
    w_qkv, w_out, w_up, w_down, w_time, char_table, vectors, up_bias = pieces
    (
        one_hot,
        features,
        resid0,
        attn_in,
        queries,
        keys_all,
        values,
        log_total,
        attended_flat,
        resid1,
        ffn_in,
        pre_act,
        activated,
        is_valid,
        slot_of,
    ) = saved_state
    row_count, seq_len, head_count, head_dim = queries.shape
    tokens_here, model_width = resid0.shape
    vector_rows = vectors.astype(jnp.float32)
    d_ffn = cot_eff.astype(jnp.bfloat16)
    grad_down = jnp.einsum("nf,nd->fd", activated, d_ffn, preferred_element_type=jnp.float32)
    grad_down_bias = jnp.sum(d_ffn.astype(jnp.float32), axis=0)
    d_act = jnp.einsum("nd,fd->nf", d_ffn, w_down, preferred_element_type=jnp.float32)
    unused_act, gelu_pull = jax.vjp(partial(jax.nn.gelu, approximate=False), pre_act)
    d_pre = gelu_pull(d_act)[0].astype(jnp.bfloat16)
    grad_up = jnp.einsum("nd,nf->df", ffn_in, d_pre, preferred_element_type=jnp.float32)
    grad_up_bias = jnp.sum(d_pre.astype(jnp.float32), axis=0)
    d_norm_second = jnp.einsum("nf,df->nd", d_pre, w_up, preferred_element_type=jnp.float32)
    unused_norm, norm_pull = jax.vjp(layer_norm, resid1, vector_rows[2], vector_rows[3])
    d_resid_norm, grad_gain_second, grad_bias_second = norm_pull(d_norm_second)
    d_resid1 = cot_eff + d_resid_norm
    d_branch = d_resid1.astype(jnp.bfloat16)
    grad_out = jnp.einsum("nd,ne->de", attended_flat, d_branch, preferred_element_type=jnp.float32)
    grad_out_bias = jnp.sum(d_branch.astype(jnp.float32), axis=0)
    d_attended = jnp.einsum(
        "ne,de->nd", d_branch, w_out, preferred_element_type=jnp.float32
    ).astype(jnp.bfloat16)
    d_attended = d_attended.reshape(row_count, seq_len, head_count, head_dim)
    grad_q, grad_k, grad_v = attention_backward(
        queries, keys_all, values, log_total, d_attended, slot_of, is_valid
    )
    d_qkv = (
        jnp.stack([grad_q, grad_k, grad_v], axis=2)
        .reshape(tokens_here, 3 * model_width)
        .astype(jnp.bfloat16)
    )
    grad_qkv = jnp.einsum("nd,ne->de", attn_in, d_qkv, preferred_element_type=jnp.float32)
    column_sums = jnp.sum(d_qkv.astype(jnp.float32), axis=0)
    d_norm_first = jnp.einsum("ne,de->nd", d_qkv, w_qkv, preferred_element_type=jnp.float32)
    unused_first, first_pull = jax.vjp(layer_norm, resid0, vector_rows[0], vector_rows[1])
    d_resid_first, grad_gain_first, grad_bias_first = first_pull(d_norm_first)
    input_grad = d_resid1 + d_resid_first
    d_side = input_grad.astype(jnp.bfloat16)
    grad_time = jnp.einsum("nt,nd->td", features, d_side, preferred_element_type=jnp.float32)
    grad_char = jnp.einsum("nv,nd->vd", one_hot, d_side, preferred_element_type=jnp.float32)
    grad_vectors = jnp.stack(
        [
            grad_gain_first,
            grad_bias_first,
            grad_gain_second,
            grad_bias_second,
            column_sums[:model_width],
            column_sums[2 * model_width :],
            grad_out_bias,
            grad_down_bias,
        ]
    )
    members = [
        grad_qkv,
        grad_out,
        grad_up,
        grad_down,
        grad_time,
        grad_char,
        grad_vectors,
        grad_up_bias,
    ]
    grad_flat = jnp.concatenate([member.astype(BF).reshape(-1) for member in members]).reshape(-1, ROW)
    grad_flat = jnp.pad(grad_flat, ((0, total_len - grad_flat.shape[0]), (0, 0)))
    return (grad_flat, input_grad)


def offset_in_chunk(plan, nfs):
    i = lax.axis_index("dp") * nfs + lax.axis_index("fsdp")
    return i * plan.share - ((i * plan.share) // (ROW * TILE)) * (TILE * ROW)


def shards(inputs, noisy_ids, timesteps, doc_lens, cotangent, params, momentum, average):
    ndp, nfs = lax.axis_size("dp"), lax.axis_size("fsdp")
    device_count = ndp * nfs
    row_count, seq_len, model_width = inputs.shape
    plan = Plan(ndp, nfs, params.shape[0] * device_count)
    offset = offset_in_chunk(plan, nfs)
    chunk = lax.dynamic_update_slice(
        jnp.zeros((plan.rows * ROW,), BF), params.astype(BF), (offset,)
    ).reshape(plan.rows, ROW)
    gathered = gather_all(plan, chunk, 0)
    pieces = unpack(gathered.reshape(-1))
    output, saved = forward_pass(pieces, inputs, noisy_ids, timesteps, doc_lens)
    is_valid = saved[13].reshape(row_count * seq_len, 1).astype(jnp.float32)
    cot_eff = cotangent.astype(jnp.float32).reshape(row_count * seq_len, model_width) * is_valid
    grad_rows, input_grad = backward_pass(pieces, saved, cot_eff, plan.padded)
    owned = reduce_all(plan, grad_rows, 1)
    owned_grad = lax.dynamic_slice(owned.reshape(-1), (offset,), (plan.share,))
    gradient = owned_grad * (1.0 / math.sqrt(row_count * seq_len * device_count))
    new_momentum = MOMENTUM_RATE * momentum + gradient
    new_params = params - LEARN_RATE * (gradient + MOMENTUM_RATE * new_momentum)
    new_average = AVERAGE_RATE * average + (1.0 - AVERAGE_RATE) * new_params
    return (
        output.reshape(row_count, seq_len, model_width).astype(jnp.bfloat16),
        input_grad.reshape(row_count, seq_len, model_width),
        new_params,
        new_momentum,
        new_average,
        new_params.astype(jnp.bfloat16),
    )


def solution(mesh):
    in_specs = (
        P(("dp", "fsdp"), None, None),
        P(("dp", "fsdp"), None),
        P(("dp", "fsdp"), None),
        P(("dp", "fsdp"), None),
        P(("dp", "fsdp"), None, None),
        P(("dp", "fsdp")),
        P(("dp", "fsdp")),
        P(("dp", "fsdp")),
    )
    out_specs = (
        P(("dp", "fsdp"), None, None),
        P(("dp", "fsdp"), None, None),
        P(("dp", "fsdp")),
        P(("dp", "fsdp")),
        P(("dp", "fsdp")),
        P(("dp", "fsdp")),
    )
    return jax.shard_map(shards, mesh=mesh, in_specs=in_specs, out_specs=out_specs, check_vma=False)
```

```python
import math

import jax
import jax.numpy as jnp
from jax import lax
from jax.experimental import pallas as pl
from jax.experimental.pallas import tpu as pltpu
from jax.sharding import PartitionSpec as P

MOMENTUM_RATE = 0.9
LEARN_RATE = 0.02
AVERAGE_RATE = 0.8
EPSILON = 1e-5
MESH = pl.DeviceIdType.MESH
ROW = 512
TILE = 16
BF = jnp.bfloat16
F32 = jnp.float32


class Plan:
    def __init__(self, ndp, nfs, total):
        self.nx, self.ny, self.nc = 2, nfs // 2, 2
        self.nz = ndp // 2
        self.count = ndp * nfs
        self.share = total // self.count
        self.total = total
        self.starts = [self.start(i) for i in range(self.count)]
        ends = [-(-((i + 1) * self.share) // ROW) for i in range(self.count)]
        need = max(e - s for e, s in zip(ends, self.starts))
        self.rows = -(-need // 32) * 32
        self.half = self.rows // 2
        self.padded = max(self.starts) + self.rows

    def start(self, i):
        return ((i * self.share) // (ROW * TILE)) * TILE

    def index(self, z, x, y, c):
        return ((z * self.nx + x) * self.ny + y) * self.nc + c


class Place:
    def __init__(self, plan):
        d = lax.axis_index("dp")
        f = lax.axis_index("fsdp")
        self.plan = plan
        self.z, self.x = d // plan.nx, d % plan.nx
        self.y, self.c = f // plan.nc, f % plan.nc

    def dev(self, z=None, x=None, y=None, c=None):
        z = self.z if z is None else z
        x = self.x if x is None else x
        y = self.y if y is None else y
        c = self.c if c is None else c
        return (z * self.plan.nx + x, y * self.plan.nc + c)

    @property
    def X(self):
        return self.dev(x=1 - self.x)

    @property
    def Y(self):
        return self.dev(y=1 - self.y)

    @property
    def C(self):
        return self.dev(c=1 - self.c)


def greet(place, nz):
    bar = pltpu.get_barrier_semaphore()
    for dev in (place.X, place.Y, place.C):
        pl.semaphore_signal(bar, inc=1, device_id=dev, device_id_type=MESH)
    for s in range(1, nz):
        pl.semaphore_signal(bar, inc=1, device_id=place.dev(z=(place.z + s) % nz), device_id_type=MESH)
    pl.semaphore_wait(bar, 3 + nz - 1)


def rcopy(src, dst, ss, rs, dev):
    return pltpu.make_async_remote_copy(src_ref=src, dst_ref=dst, send_sem=ss, recv_sem=rs, device_id=dev, device_id_type=MESH)


AG_KINDS = 13


def gather_events(plan, layers, g, zs, zr, ps, pr):
    p = Place(plan)
    z, x, y, c, nz, h, n = p.z, p.x, p.y, p.c, plan.nz, plan.half, plan.rows
    A, B, W = pl.ds(0, h), pl.ds(h, h), pl.ds(0, n)

    def at(r, xx, yy, part):
        return g.at[r, xx, yy, c, part]

    def zcopy(r, j, up):
        ref = g.at[r, x, y, c, (A, B)[j]]
        return rcopy(ref, ref, zs.at[r, j, 0 if up else 1], zr.at[r, j], p.dev(z=z + 1 if up else z - 1))

    def cp(r, k):
        table = {
            0: (at(r, x, y, A), p.X), 1: (at(r, x, y, B), p.Y),
            2: (at(r, x, y, A), p.Y), 3: (at(r, x, y, B), p.X),
            4: (at(r, 1 - x, y, A), p.Y), 5: (at(r, x, 1 - y, B), p.X),
            6: (at(r, x, y, W), p.C), 7: (at(r, 1 - x, y, A), p.C), 8: (at(r, x, 1 - y, B), p.C),
            9: (at(r, x, 1 - y, A), p.C), 10: (at(r, 1 - x, 1 - y, A), p.C),
            11: (at(r, 1 - x, y, B), p.C), 12: (at(r, 1 - x, 1 - y, B), p.C),
        }
        ref, dev = table[k]
        return rcopy(ref, ref, ps.at[r, k], pr.at[r, k], dev)

    def stage0(r):
        for j in (0, 1):
            if r < nz - 1:
                @pl.when(z == r)
                def _(): zcopy(r, j, True).start()
            if r > 0:
                @pl.when(z == r)
                def _(): zcopy(r, j, False).start()

    def stage1(r):
        for j in (0, 1):
            @pl.when(z != r)
            def _(): zcopy(r, j, True).wait_recv()
            if r < nz - 1:
                @pl.when((z > r) & (z < nz - 1))
                def _(): zcopy(r, j, True).start()
            if r > 0:
                @pl.when((z < r) & (z > 0))
                def _(): zcopy(r, j, False).start()
            cp(r, j).start()
        for k in (2, 3, 6):
            cp(r, k).start()

    def stage2(r):
        cp(r, 0).wait_recv()
        cp(r, 4).start()
        cp(r, 7).start()
        cp(r, 1).wait_recv()
        cp(r, 5).start()
        cp(r, 8).start()

    def stage3(r):
        for k, kk in ((2, 9), (4, 10), (3, 11), (5, 12)):
            cp(r, k).wait_recv()
            cp(r, kk).start()

    def stage4(r):
        for k in range(6, 13):
            cp(r, k).wait_recv()

    def drain():
        for r in layers:
            for j in (0, 1):
                if r < nz - 1:
                    @pl.when((z >= r) & (z < nz - 1))
                    def _(): zcopy(r, j, True).wait_send()
                if r > 0:
                    @pl.when((z <= r) & (z > 0))
                    def _(): zcopy(r, j, False).wait_send()
            for k in range(AG_KINDS):
                cp(r, k).wait_send()

    return [stage0, stage1, stage2, stage3, stage4], drain


def pipelined(stages, layers):
    order = []
    for t in range(len(layers) + len(stages) - 1):
        for s in reversed(range(len(stages))):
            j = t - s
            if 0 <= j < len(layers):
                order.append((stages[s], layers[j]))
    return order


def gather_scratch(plan):
    nz = plan.nz
    D = pltpu.SemaphoreType.DMA
    return [D((nz, 2, 2)), D((nz, 2)), D((nz, AG_KINDS)), D((nz, AG_KINDS))]


def assemble(plan, g, out, write=None):
    n = plan.rows
    for i in range(plan.count):
        cc = i % 2; yy = (i // 2) % 2; xx = (i // 4) % 2; zz = i // 8
        s = plan.starts[i]
        e = plan.starts[i + 1] if i + 1 < plan.count else plan.padded
        head = g[zz, xx, yy, cc, 0:TILE, :]
        if i:
            j = i - 1
            d = s - plan.starts[j]
            if d < n:
                head = head + g[j // 8, (j // 4) % 2, (j // 2) % 2, j % 2, d:d + TILE, :]
        out[s:s + TILE, :] = head
        if e - s > TILE:
            out[s + TILE:e, :] = g[zz, xx, yy, cc, TILE:e - s, :]


def gather_all(plan, chunk, cid):
    nz, n = plan.nz, plan.rows
    layers = list(range(nz))

    def kern(chunk_ref, out_ref, g, zs, zr, ps, pr, ls):
        p = Place(plan)
        greet(p, nz)
        cpy = pltpu.make_async_copy(chunk_ref, g.at[p.z, p.x, p.y, p.c], ls)
        cpy.start(); cpy.wait()
        stages, drain = gather_events(plan, layers, g, zs, zr, ps, pr)
        for st, r in pipelined(stages, layers):
            st(r)
        assemble(plan, g, out_ref)
        drain()

    return pl.pallas_call(
        kern, out_shape=jax.ShapeDtypeStruct((plan.padded, ROW), BF),
        in_specs=[pl.BlockSpec(memory_space=pltpu.VMEM)],
        out_specs=pl.BlockSpec(memory_space=pltpu.VMEM),
        scratch_shapes=[pltpu.VMEM((nz, 2, 2, 2, n, ROW), BF)] + gather_scratch(plan) + [pltpu.SemaphoreType.DMA],
        compiler_params=pltpu.CompilerParams(collective_id=cid, has_side_effects=True, vmem_limit_bytes=60 << 20),
        name="gather_all",
    )(chunk)


def reduce_events(plan, layers, src, cb, pa, pb, p2, zb, cs, cr, ps, pr, zs, zr):
    p = Place(plan)
    z, x, y, c, nz, h, n = p.z, p.x, p.y, p.c, plan.nz, plan.half, plan.rows

    def rows(r, xx, yy, cc):
        i = plan.index(r, xx, yy, cc)
        return pl.ds(pl.multiple_of(((i * plan.share) // (ROW * TILE)) * TILE, TILE), n)

    def ccopy(r, xx, yy):
        return rcopy(src.at[rows(r, xx, yy, 1 - c)], cb.at[r, xx, yy], cs.at[r, xx, yy], cr.at[r, xx, yy], p.C)

    def cp(r, k):
        table = {
            0: (cb.at[r, :, 1 - y, pl.ds(0, h)], pa.at[r], p.Y),
            1: (cb.at[r, 1 - x, :, pl.ds(h, h)], pb.at[r], p.X),
            2: (pa.at[r, 1 - x], p2.at[r, pl.ds(0, h)], p.X),
            3: (pb.at[r, 1 - y], p2.at[r, pl.ds(h, h)], p.Y),
        }
        s, d, dev = table[k]
        return rcopy(s, d, ps.at[r, k], pr.at[r, k], dev)

    def zcopy(r):
        return rcopy(p2.at[r], zb.at[z], zs.at[r], zr.at[z], p.dev(z=r))

    def zwait(s):
        return rcopy(p2.at[0], zb.at[s], zs.at[0], zr.at[s], p.dev(z=s))

    def stage0(r):
        for xx in (0, 1):
            for yy in (0, 1):
                ccopy(r, xx, yy).start()

    def stage1(r):
        for xx in (0, 1):
            for yy in (0, 1):
                ccopy(r, xx, yy).wait_recv()
                cb[r, xx, yy] = (cb[r, xx, yy].astype(F32) + src[rows(r, xx, yy, c), :].astype(F32)).astype(BF)
        cp(r, 0).start()
        cp(r, 1).start()

    def stage2(r):
        cp(r, 0).wait_recv()
        for xx in (0, 1):
            pa[r, xx] = (pa[r, xx].astype(F32) + cb[r, xx, y, 0:h].astype(F32)).astype(BF)
        cp(r, 2).start()
        cp(r, 1).wait_recv()
        for yy in (0, 1):
            pb[r, yy] = (pb[r, yy].astype(F32) + cb[r, x, yy, h:n].astype(F32)).astype(BF)
        cp(r, 3).start()

    def stage3(r):
        cp(r, 2).wait_recv()
        p2[r, 0:h] = (p2[r, 0:h].astype(F32) + pa[r, x].astype(F32)).astype(BF)
        cp(r, 3).wait_recv()
        p2[r, h:n] = (p2[r, h:n].astype(F32) + pb[r, y].astype(F32)).astype(BF)
        @pl.when(z != r)
        def _(): zcopy(r).start()

    def finish(out, mine):
        out[...] = p2[mine].astype(F32)
        for s in range(nz):
            @pl.when(z != s)
            def _():
                zwait(s).wait_recv()
                out[...] += zb[s].astype(F32)

    def drain():
        for r in layers:
            for xx in (0, 1):
                for yy in (0, 1):
                    ccopy(r, xx, yy).wait_send()
            for k in range(4):
                cp(r, k).wait_send()
            @pl.when(z != r)
            def _(): zcopy(r).wait_send()

    return [stage0, stage1, stage2, stage3], finish, drain


def reduce_scratch(plan):
    nz, n, h = plan.nz, plan.rows, plan.half
    D = pltpu.SemaphoreType.DMA
    return [pltpu.VMEM((nz, 2, 2, n, ROW), BF), pltpu.VMEM((nz, 2, h, ROW), BF), pltpu.VMEM((nz, 2, h, ROW), BF),
            pltpu.VMEM((nz, n, ROW), BF), pltpu.VMEM((nz, n, ROW), BF),
            D((nz, 2, 2)), D((nz, 2, 2)), D((nz, 4)), D((nz, 4)), D((nz,)), D((nz,))]


def reduce_all(plan, src, cid):
    nz, n = plan.nz, plan.rows
    layers = list(range(1, nz)) + [0]

    def kern(src_ref, out_ref, *rest):
        p = Place(plan)
        greet(p, nz)
        stages, finish, drain = reduce_events(plan, layers, src_ref, *rest)
        for st, r in pipelined(stages, layers):
            st(r)
        finish(out_ref, p.z)
        drain()

    return pl.pallas_call(
        kern, out_shape=jax.ShapeDtypeStruct((n, ROW), F32),
        in_specs=[pl.BlockSpec(memory_space=pltpu.VMEM)],
        out_specs=pl.BlockSpec(memory_space=pltpu.VMEM),
        scratch_shapes=reduce_scratch(plan),
        compiler_params=pltpu.CompilerParams(collective_id=cid, has_side_effects=True, vmem_limit_bytes=60 << 20),
        name="reduce_all",
    )(src)

T = 1024
D = 512
BLK = 256
NB = T // BLK
PAIRS = 4
ROW_O, ROW_UP, ROW_DOWN, ROW_T, ROW_C, ROW_V = 1536, 2048, 4096, 6144, 6400, 6427
TAIL = 48
SCALE = 0.125
VMEM_LIMIT = 63 << 20


def mm(a, b):
    return lax.dot_general(a, b, (((1,), (0,)), ((), ())), preferred_element_type=F32)


def mm_nt(a, b):
    return lax.dot_general(a, b, (((1,), (1,)), ((), ())), preferred_element_type=F32)


def mm_tn(a, b):
    return lax.dot_general(a, b, (((0,), (0,)), ((), ())), preferred_element_type=F32)


def norm(h):
    mean = jnp.mean(h, axis=-1, keepdims=True)
    cen = h - mean
    inv = lax.rsqrt(jnp.mean(cen * cen, axis=-1, keepdims=True) + EPSILON)
    return cen * inv, inv


def norm_back(dn, n, inv):
    return (dn - jnp.mean(dn, axis=-1, keepdims=True) - n * jnp.mean(dn * n, axis=-1, keepdims=True)) * inv


def valid_len(lens, b):
    long = lens[0, 1] == 0
    return jnp.where(long, lens[0, 0] - b * BLK, lens[0, b])


def lane_half(par):
    lane = lax.broadcasted_iota(jnp.int32, (1, 128), 1)
    return (lane >= 64) if par else (lane < 64)


def key_bias(lens, qb):
    long = lens[0, 1] == 0
    cols = []
    it = lax.broadcasted_iota(jnp.int32, (BLK, 1), 0)
    for kb in range(NB):
        thr = jnp.where(long | (qb == kb), valid_len(lens, kb), 0)
        cols.append(jnp.where(it < thr, 0.0, -1e30).astype(F32))
    return jnp.concatenate(cols, axis=0)


def unpack(w, base, n, wf, to):
    for j in range(4):
        wf[j, 0:512 * n, :] = w[base:base + 512 * n, 128 * j:128 * j + 128].astype(F32)
    for c in range(n):
        for j in range(4):
            to[c, :, 128 * j:128 * j + 128] = wf[j, pl.ds(c, 512, stride=n), :].astype(BF)


def put(wf, c, n, val):
    for j in range(4):
        wf[j, pl.ds(c, 512, stride=n), :] = val[:, 128 * j:128 * j + 128]


def take(wf, n, out, base):
    for j in range(4):
        out[base:base + 512 * n, 128 * j:128 * j + 128] = wf[j, 0:512 * n, :].astype(BF)


def fwd_body(lens, x, ids, feat, w, resid0, attn_in, qkv, attended, lse, wf, wq, ft):
    unpack(w, 0, 3, wf, wq)
    ctab = w[ROW_C:ROW_C + 32, :]
    vecs = w[ROW_C + 16:ROW_C + TAIL, :].astype(F32)
    o = ROW_V - ROW_C - 16
    g1, b1, bq, bv = vecs[o:o + 1], vecs[o + 1:o + 2], vecs[o + 4:o + 5], vecs[o + 5:o + 6]
    ft[...] = mm(feat[...], w[ROW_T:ROW_T + 256, :])
    long = lens[0, 1] == 0

    def block(b, _):
        r0 = pl.multiple_of(b * BLK, BLK)
        rows = pl.ds(r0, BLK)
        oh = (lax.broadcasted_iota(jnp.int32, (32, BLK), 0) == ids[0:1, rows]).astype(F32).astype(BF)
        side = mm_tn(oh, ctab)
        slot = jnp.where(long, 0, b)
        h = x[rows, :].astype(F32) + (side + ft[pl.ds(slot, 1), :])
        resid0[rows, :] = h
        n, _i = norm(h)
        a = (n * g1 + b1).astype(BF)
        attn_in[rows, :] = a
        for c in range(3):
            pr = mm(a, wq[c])
            if c == 0:
                pr = pr + bq
            if c == 2:
                pr = pr + bv
            pr = pr.astype(BF)
            for j in range(4):
                qkv[4 * c + j, rows, :] = pr[:, 128 * j:128 * j + 128]
        return 0

    lax.fori_loop(0, NB, block, 0)

    ones = jnp.ones((T, 128), BF)

    def attend(i, _):
        pair, qb = lax.div(i, NB), lax.rem(i, NB)
        rows = pl.ds(pl.multiple_of(qb * BLK, BLK), BLK)
        q = qkv[pair, rows, :] * jnp.asarray(SCALE, BF)
        k = qkv[PAIRS + pair]
        va = jnp.concatenate([qkv[2 * PAIRS + pair], ones], axis=1)
        bias = key_bias(lens, qb)
        outs = []
        for par in (0, 1):
            qm = jnp.where(lane_half(par), q, jnp.zeros_like(q))
            s = mm_nt(k, qm) + bias
            m = jnp.max(s, axis=0, keepdims=True)
            e = jnp.exp(s - m)
            l = jnp.sum(e, axis=0, keepdims=True)
            lse[pl.ds(2 * pair + par, 1), rows] = m + jnp.log(l)
            oa = mm_tn(e.astype(BF), va)
            outs.append(oa[:, :128] / oa[:, 128:])
        attended[pair, rows, :] = jnp.where(lane_half(0), outs[0], outs[1]).astype(BF)
        return 0

    lax.fori_loop(0, PAIRS * NB, attend, 0)


def vm():
    return pl.BlockSpec(memory_space=pltpu.VMEM)


def sm():
    return pl.BlockSpec(memory_space=pltpu.SMEM)


def forward(lens, x, ids, feat, w):
    S = jax.ShapeDtypeStruct
    return pl.pallas_call(
        fwd_body,
        out_shape=[S((T, D), F32), S((T, D), BF), S((12, T, 128), BF), S((PAIRS, T, 128), BF), S((8, T), F32)],
        in_specs=[sm()] + [vm()] * 4, out_specs=[vm()] * 5,
        scratch_shapes=[pltpu.VMEM((4, 1536, 128), F32), pltpu.VMEM((3, D, D), BF), pltpu.VMEM((8, D), F32)],
        compiler_params=pltpu.CompilerParams(vmem_limit_bytes=VMEM_LIMIT),
        name="forward",
    )(lens, x, ids, feat, w)


def phi_parts(v):
    cdf = 0.5 * (1.0 + lax.erf(v * (2.0 ** -0.5)))
    pdf = jnp.exp(v * v * -0.5) * (1.0 / math.sqrt(2.0 * math.pi))
    return cdf, pdf


def mid_body(lens, resid0, attended, cot, w, out, dres, datt, grads, small, wf, wu, act, dpre, fin, dbr, dff):
    unpack(w, ROW_UP, 4, wf, wu)
    vecs = w[ROW_C + 16:ROW_C + TAIL, :].astype(F32)
    o = ROW_V - ROW_C - 16
    g2, b2, bo, bd = vecs[o + 2:o + 3], vecs[o + 3:o + 4], vecs[o + 6:o + 7], vecs[o + 7:o + 8]
    small[...] = jnp.zeros_like(small)

    def block(b, _):
        rows = pl.ds(pl.multiple_of(b * BLK, BLK), BLK)
        att = jnp.concatenate([attended[j, rows, :] for j in range(PAIRS)], axis=1)
        h = resid0[rows, :] + (mm(att, w[ROW_O:ROW_O + 512, :]) + bo)
        n, inv = norm(h)
        f = (n * g2 + b2).astype(BF)
        fin[rows, :] = f
        ok = lax.broadcasted_iota(jnp.int32, (BLK, 1), 0) < valid_len(lens, b)
        do = jnp.where(ok, cot[rows, :].astype(F32), 0.0)
        d = do.astype(BF)
        dff[rows, :] = d
        small[0:1, :] += jnp.sum(do, axis=0, keepdims=True)
        acc = h + bd
        e2 = jnp.zeros((BLK, D), F32)
        for c in range(4):
            pre = mm(f, wu[c]) + vecs[o + 8 + c:o + 9 + c]
            cdf, pdf = phi_parts(pre)
            a = (pre * cdf).astype(BF)
            wd = w[ROW_DOWN + 512 * c:ROW_DOWN + 512 * c + 512, :]
            dp = (mm_nt(d, wd) * (cdf + pre * pdf)).astype(BF)
            act[c, rows, :] = a
            dpre[c, rows, :] = dp
            small[4 + c:5 + c, :] += jnp.sum(dp.astype(F32), axis=0, keepdims=True)
            acc = acc + mm(a, wd)
            e2 = e2 + mm_nt(dp, wu[c])
        out[rows, :] = acc.astype(BF)
        small[1:2, :] += jnp.sum(e2 * n, axis=0, keepdims=True)
        small[2:3, :] += jnp.sum(e2, axis=0, keepdims=True)
        dr = do + norm_back(e2 * g2, n, inv)
        dres[rows, :] = dr
        db = dr.astype(BF)
        dbr[rows, :] = db
        small[3:4, :] += jnp.sum(db.astype(F32), axis=0, keepdims=True)
        da = mm_nt(db, w[ROW_O:ROW_O + 512, :]).astype(BF)
        for j in range(PAIRS):
            datt[j, rows, :] = da[:, 128 * j:128 * j + 128]
        return 0

    lax.fori_loop(0, NB, block, 0)

    def wgrad(c, _):
        base = pl.multiple_of(ROW_DOWN - ROW_O + 512 * c, 512)
        grads[pl.ds(base, 512), :] = mm_tn(act[c], dff[...]).astype(BF)
        put(wf, c, 4, mm_tn(fin[...], dpre[c]))
        return 0

    for c in range(4):
        wgrad(c, 0)
    take(wf, 4, grads, ROW_UP - ROW_O)
    for j in range(PAIRS):
        grads[128 * j:128 * j + 128, :] = mm_tn(attended[j], dbr[...]).astype(BF)


def middle(lens, resid0, attended, cot, w):
    S = jax.ShapeDtypeStruct
    V = pltpu.VMEM
    return pl.pallas_call(
        mid_body,
        out_shape=[S((T, D), BF), S((T, D), F32), S((PAIRS, T, 128), BF), S((ROW_T - ROW_O, D), BF), S((8, D), F32)],
        in_specs=[sm()] + [vm()] * 4, out_specs=[vm()] * 5,
        scratch_shapes=[V((4, 2048, 128), F32), V((4, D, D), BF), V((4, T, D), BF), V((4, T, D), BF), V((T, D), BF), V((T, D), BF), V((T, D), BF)],
        compiler_params=pltpu.CompilerParams(vmem_limit_bytes=VMEM_LIMIT),
        name="middle",
    )(lens, resid0, attended, cot, w)


def bwd_body(lens, qkv, lse, datt, attn_in, resid0, dres, ids, feat, w, small, gin, ga, gt, dqkv, accv, wf, wq, slots, cacc):
    unpack(w, 0, 3, wf, wq)
    vecs = w[ROW_C + 16:ROW_C + TAIL, :].astype(F32)
    o = ROW_V - ROW_C - 16
    g1 = vecs[o:o + 1]
    long = lens[0, 1] == 0

    def attend(i, _):
        pair, qb = lax.div(i, NB), lax.rem(i, NB)
        rows = pl.ds(pl.multiple_of(qb * BLK, BLK), BLK)
        q = qkv[pair, rows, :] * jnp.asarray(SCALE, BF)
        k = qkv[PAIRS + pair]
        v = qkv[2 * PAIRS + pair]
        do = datt[pair, rows, :]
        bias = key_bias(lens, qb)
        dqs = []

        @pl.when(qb == 0)
        def _():
            accv[...] = jnp.zeros_like(accv)

        for par in (0, 1):
            half = lane_half(par)
            qm = jnp.where(half, q, jnp.zeros_like(q))
            dm = jnp.where(half, do, jnp.zeros_like(do))
            p = jnp.exp(mm_nt(k, qm) + bias - lse[pl.ds(2 * pair + par, 1), rows])
            dp = mm_nt(v, dm)
            delta = jnp.sum(p * dp, axis=0, keepdims=True)
            ds = (p * (dp - delta)).astype(BF)
            accv[1] += mm(p.astype(BF), dm)
            accv[0] += mm(ds, qm)
            dqs.append(mm_tn(ds, k))
        dqkv[pair, rows, :] = (jnp.where(lane_half(0), dqs[0], dqs[1]) * SCALE).astype(BF)

        @pl.when(qb == NB - 1)
        def _():
            dqkv[PAIRS + pair] = accv[0].astype(BF)
            dqkv[2 * PAIRS + pair] = accv[1].astype(BF)
        return 0

    lax.fori_loop(0, PAIRS * NB, attend, 0)

    cols = []
    for c in range(3):
        dq = jnp.concatenate([dqkv[4 * c + j] for j in range(4)], axis=1)
        put(wf, c, 3, mm_tn(attn_in[...], dq))
        if c != 1:
            cols.append(jnp.sum(dq.astype(F32), axis=0, keepdims=True))
    take(wf, 3, ga, 0)
    slots[...] = jnp.zeros_like(slots)
    cacc[...] = jnp.zeros_like(cacc)

    def block(b, _):
        rows = pl.ds(pl.multiple_of(b * BLK, BLK), BLK)
        e1 = jnp.zeros((BLK, D), F32)
        for c in range(3):
            dq = jnp.concatenate([dqkv[4 * c + j, rows, :] for j in range(4)], axis=1)
            e1 = e1 + mm_nt(dq, wq[c])
        n, inv = norm(resid0[rows, :])
        slots[8:9, :] += jnp.sum(e1 * n, axis=0, keepdims=True)
        slots[9:10, :] += jnp.sum(e1, axis=0, keepdims=True)
        g = dres[rows, :] + norm_back(e1 * g1, n, inv)
        gin[rows, :] = g
        ds = g.astype(BF)
        oh = (lax.broadcasted_iota(jnp.int32, (32, BLK), 0) == ids[0:1, rows]).astype(F32).astype(BF)
        cacc[0:32, :] += mm(oh, ds)
        slot = jnp.where(long, 0, b)
        slots[pl.ds(slot, 1), :] += jnp.sum(ds.astype(F32), axis=0, keepdims=True)
        return 0

    lax.fori_loop(0, NB, block, 0)
    f = feat[...].astype(F32)
    gt[0:256, :] = lax.dot_general(f, slots[0:8, :], (((0,), (0,)), ((), ())), precision=lax.Precision.HIGHEST, preferred_element_type=F32).astype(BF)
    o = ROW_V - ROW_C
    cacc[o:o + 2, :] = slots[8:10, :]
    cacc[o + 2:o + 4, :] = small[1:3, :]
    cacc[o + 4:o + 5, :] = cols[0]
    cacc[o + 5:o + 6, :] = cols[1]
    cacc[o + 6:o + 7, :] = small[3:4, :]
    cacc[o + 7:o + 8, :] = small[0:1, :]
    cacc[o + 8:o + 12, :] = small[4:8, :]
    gt[256:256 + TAIL, :] = cacc[...].astype(BF)


def backward(lens, qkv, lse, datt, attn_in, resid0, dres, ids, feat, w, small):
    S = jax.ShapeDtypeStruct
    V = pltpu.VMEM
    return pl.pallas_call(
        bwd_body,
        out_shape=[S((T, D), F32), S((ROW_O, D), BF), S((256 + TAIL, D), BF)],
        in_specs=[sm()] + [vm()] * 10, out_specs=[vm()] * 3,
        scratch_shapes=[V((12, T, 128), BF), V((2, T, 128), F32), V((4, 1536, 128), F32), V((3, D, D), BF), V((16, D), F32), V((TAIL, D), F32)],
        compiler_params=pltpu.CompilerParams(vmem_limit_bytes=VMEM_LIMIT),
        name="backward",
    )(lens, qkv, lse, datt, attn_in, resid0, dres, ids, feat, w, small)


def time_features(steps):
    half = 128
    freqs = jnp.exp(-math.log(10000.0) * jnp.arange(half, dtype=F32) / half)
    ang = steps.astype(F32).reshape(4, 1) * freqs
    f = jnp.concatenate([jnp.sin(ang), jnp.cos(ang)], axis=-1).astype(BF)
    return jnp.pad(f, ((0, 4), (0, 0)))


def step(inputs, ids, timesteps, lens, cot, w):
    x = inputs.reshape(T, D)
    feat = time_features(timesteps)
    resid0, attn_in, qkv, attended, lse = forward(lens, x, ids, feat, w)
    out, dres, datt, gmid, small = middle(lens, resid0, attended, cot.reshape(T, D), w)
    gin, ga, gt = backward(lens, qkv, lse, datt, attn_in, resid0, dres, ids, feat, w, small)
    return out, gin, ga, gmid, gt


def offset_in_chunk(plan, nfs):
    i = lax.axis_index("dp") * nfs + lax.axis_index("fsdp")
    return i * plan.share - lax.div(i * plan.share, ROW * TILE) * (TILE * ROW)


def shards(inputs, noisy_ids, timesteps, doc_lens, cotangent, params, momentum, average):
    ndp, nfs = lax.axis_size("dp"), lax.axis_size("fsdp")
    device_count = ndp * nfs
    row_count, seq_len, model_width = inputs.shape
    plan = Plan(ndp, nfs, params.shape[0] * device_count)
    offset = offset_in_chunk(plan, nfs)
    chunk = lax.dynamic_update_slice(
        jnp.zeros((plan.rows * ROW,), BF), params.astype(BF), (offset,)
    ).reshape(plan.rows, ROW)
    weights = gather_all(plan, chunk, 0)
    output, input_grad, ga, gmid, gt = step(
        inputs, noisy_ids, timesteps, doc_lens, cotangent, weights
    )
    rows = jnp.concatenate([ga, gmid, gt], axis=0)
    if plan.padded > rows.shape[0]:
        rows = jnp.pad(rows, ((0, plan.padded - rows.shape[0]), (0, 0)))
    owned = reduce_all(plan, rows[: plan.padded], 1)
    owned_grad = lax.dynamic_slice(owned.reshape(-1), (offset,), (plan.share,))
    gradient = owned_grad * (1.0 / math.sqrt(row_count * seq_len * device_count))
    new_momentum = MOMENTUM_RATE * momentum + gradient
    new_params = params - LEARN_RATE * (gradient + MOMENTUM_RATE * new_momentum)
    new_average = AVERAGE_RATE * average + (1.0 - AVERAGE_RATE) * new_params
    return (
        output.reshape(row_count, seq_len, model_width),
        input_grad.reshape(row_count, seq_len, model_width),
        new_params,
        new_momentum,
        new_average,
        new_params.astype(BF),
    )


def solution(mesh):
    rows = ("dp", "fsdp")
    in_specs = (
        P(rows, None, None),
        P(rows, None),
        P(rows, None),
        P(rows, None),
        P(rows, None, None),
        P(rows),
        P(rows),
        P(rows),
    )
    out_specs = (P(rows, None, None), P(rows, None, None), P(rows), P(rows), P(rows), P(rows))
    return jax.shard_map(shards, mesh=mesh, in_specs=in_specs, out_specs=out_specs, check_vma=False)
```

```python
import math

import jax
import jax.numpy as jnp
from jax import lax
from jax.experimental import pallas as pl
from jax.experimental.pallas import tpu as pltpu
from jax.sharding import PartitionSpec as P

MOMENTUM_RATE = 0.9
LEARN_RATE = 0.02
AVERAGE_RATE = 0.8
EPSILON = 1e-5
MESH = pl.DeviceIdType.MESH
BF = jnp.bfloat16
F32 = jnp.float32
ROW = 512
TILE = 16
T = 1024
D = 512
BLK = 256
NB = T // BLK
PAIRS = 4
SCALE = 0.125
ROW_O, ROW_UP, ROW_DOWN, ROW_T, ROW_C, ROW_V = 1536, 2048, 4096, 6144, 6400, 6427
TAIL = 48
AG_KINDS = 13
RS_KINDS = 6
HOOKS = NB + PAIRS * NB


class Plan:
    def __init__(self, ndp, nfs, total):
        self.nx, self.ny, self.nc = 2, 2, nfs // 2
        self.nz = ndp // 2
        self.count = ndp * nfs
        self.share = total // self.count
        self.starts = [((i * self.share) // (ROW * TILE)) * TILE for i in range(self.count)]
        ends = [-(-((i + 1) * self.share) // ROW) for i in range(self.count)]
        need = max(e - s for e, s in zip(ends, self.starts))
        self.rows = max(2, -(-need // TILE)) * TILE
        self.half = -(-self.rows // (2 * TILE)) * TILE
        self.padded = max(max(self.starts) + self.rows, ROW_C + TAIL)
        layer = self.count // self.nz
        last = self.nz - 1
        self.lo = next(r for r in range(self.nz) if self.starts[r * layer] >= ROW_O)
        first = next(i for i in range(self.count) if self.starts[i] + self.rows > ROW_T)
        self.only = first >= self.count - self.nc
        self.hi = last if self.only else first // layer - 1
        self.early = list(range(self.lo)) + list(range(last if self.only else self.hi + 1, self.nz))
        self.late = list(range(self.lo, self.hi + 1))

    def early_pick(self, r, cx, cy):
        if self.only and r == self.nz - 1:
            return cx * cy == 1
        return True

    def late_pick(self, r, cx, cy):
        if self.only and r == self.nz - 1:
            return cx * cy == 0
        return True


class Place:
    def __init__(self, plan):
        d = lax.axis_index("dp")
        f = lax.axis_index("fsdp")
        self.plan = plan
        two = jnp.int32(2)
        self.z, self.x = lax.div(d, two), lax.rem(d, two)
        self.y, self.c = lax.div(f, two), lax.rem(f, two)
        self.X = self.dev(x=1 - self.x)
        self.Y = self.dev(y=1 - self.y)
        self.C = self.dev(c=1 - self.c)

    def dev(self, z=None, x=None, y=None, c=None):
        z = self.z if z is None else z
        x = self.x if x is None else x
        y = self.y if y is None else y
        c = self.c if c is None else c
        return (z * 2 + x, y * 2 + c)

    def partners(self):
        nz = self.plan.nz
        others = [self.dev(z=lax.rem(self.z + s, jnp.int32(nz))) for s in range(1, nz)]
        return [self.X, self.Y, self.C] + others

    def far(self, r):
        return jnp.abs(self.z - r)


def signal_all(place, sem):
    for dev in place.partners():
        pl.semaphore_signal(sem, inc=1, device_id=dev, device_id_type=MESH)


def wait_all(place, sem):
    pl.semaphore_wait(sem, 3 + place.plan.nz - 1)


def rcopy(src, dst, ss, rs, dev):
    return pltpu.make_async_remote_copy(
        src_ref=src, dst_ref=dst, send_sem=ss, recv_sem=rs, device_id=dev, device_id_type=MESH
    )


def when(*conds):
    real = [c for c in conds if c is not True]

    def run(f):
        if not real:
            return f()
        c = real[0]
        for other in real[1:]:
            c = c & other
        return pl.when(c)(f)

    return run


class Gather:
    def __init__(self, p, g, zs, zr, ps, pr):
        self.p, self.g, self.zs, self.zr, self.ps, self.pr = p, g, zs, zr, ps, pr
        h, n = p.plan.half, p.plan.rows
        self.parts = (pl.ds(0, h), pl.ds(h, n - h), pl.ds(0, n))

    def zcopy(self, r, j, up):
        p = self.p
        ref = self.g.at[r, p.x, p.y, p.c, self.parts[j]]
        return rcopy(ref, ref, self.zs.at[r, j, 0 if up else 1], self.zr.at[r, j], p.dev(z=p.z + 1 if up else p.z - 1))

    def cp(self, r, k):
        p = self.p
        a, b, w = self.parts
        x, y = p.x, p.y
        cx, cy, part, dev = (
            (x, y, a, p.X), (x, y, b, p.Y), (x, y, a, p.Y), (x, y, b, p.X),
            (1 - x, y, a, p.Y), (x, 1 - y, b, p.X), (x, y, w, p.C), (1 - x, y, a, p.C), (x, 1 - y, b, p.C),
            (x, 1 - y, a, p.C), (1 - x, 1 - y, a, p.C), (1 - x, y, b, p.C), (1 - x, 1 - y, b, p.C),
        )[k]
        ref = self.g.at[r, cx, cy, p.c, part]
        return rcopy(ref, ref, self.ps.at[r, k], self.pr.at[r, k], dev)

    def stage(self, s, r, pick):
        p = self.p
        z, x, y, nz = p.z, p.x, p.y, p.plan.nz
        if s == 0:
            for j in (0, 1):
                if r < nz - 1:
                    when(z == r, pick(r, x, y))(lambda: self.zcopy(r, j, True).start())
                if r > 0:
                    when(z == r, pick(r, x, y))(lambda: self.zcopy(r, j, False).start())
        if s == 1:
            for j in (0, 1):
                when(z != r, pick(r, x, y))(lambda: self.zcopy(r, j, True).wait_recv())
                if 0 < r < nz - 1 or r == 0:
                    when(z > r, z < nz - 1, pick(r, x, y))(lambda: self.zcopy(r, j, True).start())
                if r > 0:
                    when(z < r, z > 0, pick(r, x, y))(lambda: self.zcopy(r, j, False).start())
                when(pick(r, x, y))(lambda: self.cp(r, j).start())

            def rest():
                for k in (2, 3, 6):
                    self.cp(r, k).start()

            when(pick(r, x, y))(rest)
        if s == 2:
            for k, a, b, cx, cy in ((0, 4, 7, 1 - x, y), (1, 5, 8, x, 1 - y)):
                def go():
                    self.cp(r, k).wait_recv()
                    self.cp(r, a).start()
                    self.cp(r, b).start()

                when(pick(r, cx, cy))(go)
        if s == 3:
            for k, a, cx, cy in ((2, 9, x, 1 - y), (4, 10, 1 - x, 1 - y), (3, 11, 1 - x, y), (5, 12, 1 - x, 1 - y)):
                def go():
                    self.cp(r, k).wait_recv()
                    self.cp(r, a).start()

                when(pick(r, cx, cy))(go)
        if s == 4:
            for ks, cx, cy in (((6,), x, y), ((7, 11), 1 - x, y), ((8, 9), x, 1 - y), ((10, 12), 1 - x, 1 - y)):
                def go():
                    for k in ks:
                        self.cp(r, k).wait_recv()

                when(pick(r, cx, cy))(go)

    def drain(self):
        z, nz = self.p.z, self.p.plan.nz
        for r in range(nz):
            for j in (0, 1):
                if r < nz - 1:
                    when(z >= r, z < nz - 1)(lambda: self.zcopy(r, j, True).wait_send())
                if r > 0:
                    when(z <= r, z > 0)(lambda: self.zcopy(r, j, False).wait_send())
            for k in range(AG_KINDS):
                self.cp(r, k).wait_send()


class Reduce:
    def __init__(self, p, src, g, cs, cr, ps, pr, zs, zr):
        self.p, self.src, self.g = p, src, g
        self.cs, self.cr, self.ps, self.pr, self.zs, self.zr = cs, cr, ps, pr, zs, zr
        self.h, self.n = p.plan.half, p.plan.rows
        self.a, self.b = pl.ds(0, self.h), pl.ds(self.h, self.n - self.h)

    def rows(self, r, xx, yy, cc):
        plan = self.p.plan
        i = ((r * 2 + xx) * 2 + yy) * 2 + cc
        return pl.ds(pl.multiple_of(lax.div(i * plan.share, jnp.int32(ROW * TILE)) * TILE, TILE), self.n)

    def cb(self, r, xx, yy, *rest):
        return self.g.at[(r, xx, yy, 0) + rest]

    def pa(self, r, xx):
        return self.g.at[r, 0, xx, 1, self.a]

    def pb(self, r, yy):
        return self.g.at[r, 0, yy, 1, self.b]

    def p2(self, r, *rest):
        return self.g.at[(r, 1, 0, 1) + rest]

    def zb(self, s):
        return self.g.at[s, 1, 1, 1]

    def ccopy(self, r, xx, yy):
        p = self.p
        return rcopy(
            self.src.at[self.rows(r, xx, yy, 1 - p.c)], self.cb(r, xx, yy),
            self.cs.at[r, xx, yy], self.cr.at[r, xx, yy], p.C,
        )

    def cp(self, r, k):
        p = self.p
        x, y = p.x, p.y
        s, d, dev = (
            (self.cb(r, 0, 1 - y, self.a), self.pa(r, 0), p.Y),
            (self.cb(r, 1, 1 - y, self.a), self.pa(r, 1), p.Y),
            (self.cb(r, 1 - x, 0, self.b), self.pb(r, 0), p.X),
            (self.cb(r, 1 - x, 1, self.b), self.pb(r, 1), p.X),
            (self.pa(r, 1 - x), self.p2(r, self.a), p.X),
            (self.pb(r, 1 - y), self.p2(r, self.b), p.Y),
        )[k]
        return rcopy(s, d, self.ps.at[r, k], self.pr.at[r, k], dev)

    def zcopy(self, r):
        p = self.p
        return rcopy(self.p2(r), self.zb(p.z), self.zs.at[r], self.zr.at[p.z], p.dev(z=r))

    def zwait(self, s):
        rcopy(self.p2(0), self.zb(s), self.zs.at[0], self.zr.at[s], self.p.dev(z=s)).wait_recv()

    def stage(self, s, r, pick):
        p = self.p
        z, x, y = p.z, p.x, p.y
        both = [(xx, yy) for xx in (0, 1) for yy in (0, 1)]
        if s == 0:
            for xx, yy in both:
                when(pick(r, xx, yy))(lambda: self.ccopy(r, xx, yy).start())
        if s == 1:
            for xx, yy in both:
                def go():
                    self.ccopy(r, xx, yy).wait_recv()
                    ref = self.cb(r, xx, yy)
                    ref[...] = ref[...] + self.src[self.rows(r, xx, yy, p.c), :]

                when(pick(r, xx, yy))(go)
            for q in (0, 1):
                when(pick(r, q, 1 - y))(lambda: self.cp(r, q).start())
                when(pick(r, 1 - x, q))(lambda: self.cp(r, 2 + q).start())
        if s == 2:
            for q in (0, 1):
                def goa():
                    self.cp(r, q).wait_recv()
                    ref = self.pa(r, q)
                    ref[...] = ref[...] + self.cb(r, q, y, self.a)[...]

                when(pick(r, q, y))(goa)
            when(pick(r, 1 - x, y))(lambda: self.cp(r, 4).start())
            for q in (0, 1):
                def gob():
                    self.cp(r, 2 + q).wait_recv()
                    ref = self.pb(r, q)
                    ref[...] = ref[...] + self.cb(r, x, q, self.b)[...]

                when(pick(r, x, q))(gob)
            when(pick(r, x, 1 - y))(lambda: self.cp(r, 5).start())
        if s == 3:
            def fin():
                self.cp(r, 4).wait_recv()
                ref = self.p2(r, self.a)
                ref[...] = ref[...] + self.pa(r, x)[...]
                self.cp(r, 5).wait_recv()
                ref = self.p2(r, self.b)
                ref[...] = ref[...] + self.pb(r, y)[...]

            when(pick(r, x, y))(fin)
            when(pick(r, x, y), z != r)(lambda: self.zcopy(r).start())

    def finish(self, out):
        z = self.p.z
        out[...] = self.p2(z)[...].astype(F32)
        for s in range(self.p.plan.nz):
            def go():
                self.zwait(s)
                out[...] += self.zb(s)[...].astype(F32)

            when(z != s)(go)

    def drain(self):
        for r in range(self.p.plan.nz):
            for xx in (0, 1):
                for yy in (0, 1):
                    self.ccopy(r, xx, yy).wait_send()
            for k in range(RS_KINDS):
                self.cp(r, k).wait_send()
            when(self.p.z != r)(lambda: self.zcopy(r).wait_send())


def pipelined(stages, layers):
    order = []
    for t in range(len(layers) + len(stages) - 1):
        for s in reversed(range(len(stages))):
            if 0 <= t - s < len(layers):
                order.append((stages[s], layers[t - s]))
    return order


def assemble(plan, g, lo, hi, store):
    for i in range(plan.count):
        at = lambda k: (k // 8, (k // 4) % 2, (k // 2) % 2, k % 2)
        s = plan.starts[i]
        e = plan.starts[i + 1] if i + 1 < plan.count else plan.padded
        if lo <= s < hi:
            head = g[at(i) + (slice(0, TILE),)]
            if i and s - plan.starts[i - 1] < plan.rows:
                d = s - plan.starts[i - 1]
                head = head + g[at(i - 1) + (slice(d, d + TILE),)]
            store(s, s + TILE, head)
        a, b = max(s + TILE, lo), min(e, hi, s + plan.rows)
        if b > a:
            store(a, b, g[at(i) + (slice(a - s, b - s),)])


def mm(a, b):
    return lax.dot_general(a, b, (((1,), (0,)), ((), ())), preferred_element_type=F32)


def mm_nt(a, b):
    return lax.dot_general(a, b, (((1,), (1,)), ((), ())), preferred_element_type=F32)


def mm_tn(a, b):
    return lax.dot_general(a, b, (((0,), (0,)), ((), ())), preferred_element_type=F32)


def norm(h):
    mean = jnp.mean(h, axis=-1, keepdims=True)
    cen = h - mean
    inv = lax.rsqrt(jnp.mean(cen * cen, axis=-1, keepdims=True) + EPSILON)
    return cen * inv, inv


def norm_back(dn, n, inv):
    return (dn - jnp.mean(dn, axis=-1, keepdims=True) - n * jnp.mean(dn * n, axis=-1, keepdims=True)) * inv


def valid_len(lens, b):
    long = lens[0, 1] == 0
    short = lens[0, 0]
    for k in range(1, NB):
        short = jnp.where(b == k, lens[0, k], short)
    return jnp.where(long, lens[0, 0] - b * BLK, short)


def lane_half(par):
    lane = lax.broadcasted_iota(jnp.int32, (1, 128), 1)
    return (lane >= 64) if par else (lane < 64)


def key_bias(lens, qb):
    long = lens[0, 1] == 0
    cols = []
    it = lax.broadcasted_iota(jnp.int32, (BLK, 1), 0)
    for kb in range(NB):
        thr = jnp.where(long | (qb == kb), valid_len(lens, kb), 0)
        cols.append(jnp.where(it < thr, 0.0, -1e30).astype(F32))
    return jnp.concatenate(cols, axis=0)


def lanes(j):
    return slice(128 * j, 128 * j + 128)


def spread(wf, base):
    def store(a, b, val):
        for j in range(4):
            wf[j, a - base:b - base, :] = val[:, lanes(j)].astype(F32)
    return store


def regroup(wf, n, to):
    for c in range(n):
        for j in range(4):
            to[c, :, lanes(j)] = wf[j, pl.ds(c, 512, stride=n), :].astype(BF)


def put(wf, c, n, val):
    for j in range(4):
        wf[j, pl.ds(c, 512, stride=n), :] = val[:, lanes(j)]


def take(wf, n, out, base):
    for j in range(4):
        out[base:base + 512 * n, lanes(j)] = wf[j, 0:512 * n, :].astype(BF)


def phi_parts(v):
    cdf = 0.5 * (1.0 + lax.erf(v * (2.0 ** -0.5)))
    pdf = jnp.exp(v * v * -0.5) * (1.0 / math.sqrt(2.0 * math.pi))
    return cdf, pdf


def block_rows(b):
    return pl.ds(pl.multiple_of(b * BLK, BLK), BLK)


def body(plan, lens, ids, feat, x_hbm, cot_hbm, chunk_hbm, out_hbm, gin_hbm, own,
         g, src, wf, wq, wu, wo, wd, vec, xs, cs, resid0, attn_in, qkv, attended, lse, ft,
         act, dpre, fin, dff, dbr, dres, datt, dqkv, accv, slots, small, cacc,
         zs, zr, ps, pr, rcs, rcr, rps, rpr, rzs, rzr, ready, ins, outs, gins):
    p = Place(plan)
    nz = plan.nz
    gather = Gather(p, g, zs, zr, ps, pr)
    loads = [
        pltpu.make_async_copy(chunk_hbm, g.at[p.z, p.x, p.y, p.c], ins.at[0]),
        pltpu.make_async_copy(x_hbm, xs, ins.at[1]),
        pltpu.make_async_copy(cot_hbm, cs, ins.at[2]),
    ]
    for cpy in loads:
        cpy.start()
    bar = pltpu.get_barrier_semaphore()
    signal_all(p, bar)
    wait_all(p, bar)
    loads[0].wait()

    for r in plan.early:
        gather.stage(0, r, plan.early_pick)
    for t in range(nz + 3):
        for s in (4, 3, 2, 1):
            for r in plan.early:
                if 0 <= t - (s - 1) < nz:
                    when(p.far(r) == t - (s - 1))(lambda: gather.stage(s, r, plan.early_pick))
    for r in plan.late:
        gather.stage(0, r, plan.late_pick)

    def gather_hook(i):
        for s in (1, 2, 3, 4):
            for r in plan.late:
                start = lax.div(9 * p.far(r) + 2, jnp.int32(2)) + (0, 0, 3, 6, 7)[s]
                when(i == jnp.minimum(start, HOOKS))(lambda: gather.stage(s, r, plan.late_pick))

    assemble(plan, g, 0, ROW_O, spread(wf, 0))
    regroup(wf, 3, wq)

    def tail_store(a, b, val):
        vec[a - ROW_T:b - ROW_T, :] = val

    assemble(plan, g, ROW_T, ROW_C + TAIL, tail_store)
    ctab = vec[256:288, :]
    vecs = vec[272:304, :].astype(F32)
    v0 = ROW_V - ROW_C - 16
    g1, b1, g2, b2, bq, bv, bo, bd = (vecs[v0 + k:v0 + k + 1] for k in range(8))
    ft[...] = mm(feat[...], vec[0:256, :])
    long = lens[0, 1] == 0
    loads[1].wait()

    def embed(b, _):
        gather_hook(b)
        rows = block_rows(b)
        oh = (lax.broadcasted_iota(jnp.int32, (32, BLK), 0) == ids[0:1, rows]).astype(F32).astype(BF)
        side = mm_tn(oh, ctab)
        slot = jnp.where(long, 0, b)
        h = xs[rows, :].astype(F32) + (side + ft[pl.ds(slot, 1), :])
        resid0[rows, :] = h
        n, _i = norm(h)
        a = (n * g1 + b1).astype(BF)
        attn_in[rows, :] = a
        for c in range(3):
            pr_ = mm(a, wq[c])
            if c == 0:
                pr_ = pr_ + bq
            if c == 2:
                pr_ = pr_ + bv
            pr_ = pr_.astype(BF)
            for j in range(4):
                qkv[4 * c + j, rows, :] = pr_[:, lanes(j)]
        return 0

    lax.fori_loop(0, NB, embed, 0)
    ones = jnp.ones((T, 128), BF)

    def attend(i, _):
        gather_hook(i + NB)
        pair, qb = lax.div(i, NB), lax.rem(i, NB)
        rows = block_rows(qb)
        q = qkv[pair, rows, :] * jnp.asarray(SCALE, BF)
        k = qkv[PAIRS + pair]
        va = jnp.concatenate([qkv[2 * PAIRS + pair], ones], axis=1)
        bias = key_bias(lens, qb)
        heads = []
        for par in (0, 1):
            qm = jnp.where(lane_half(par), q, jnp.zeros_like(q))
            s = mm_nt(k, qm) + bias
            m = jnp.max(s, axis=0, keepdims=True)
            e = jnp.exp(s - m)
            l = jnp.sum(e, axis=0, keepdims=True)
            lse[pl.ds(2 * pair + par, 1), rows] = m + jnp.log(l)
            oa = mm_tn(e.astype(BF), va)
            heads.append(oa[:, :128] / oa[:, 128:])
        attended[pair, rows, :] = jnp.where(lane_half(0), heads[0], heads[1]).astype(BF)
        return 0

    lax.fori_loop(0, PAIRS * NB, attend, 0)
    gather_hook(HOOKS)

    def wo_store(a, b, val):
        wo[a - ROW_O:b - ROW_O, :] = val

    def wd_store(a, b, val):
        wd[a - ROW_DOWN:b - ROW_DOWN, :] = val

    assemble(plan, g, ROW_O, ROW_UP, wo_store)
    assemble(plan, g, ROW_UP, ROW_DOWN, spread(wf, ROW_UP))
    assemble(plan, g, ROW_DOWN, ROW_T, wd_store)
    regroup(wf, 4, wu)
    gather.drain()
    signal_all(p, ready)
    small[...] = jnp.zeros_like(small)
    loads[2].wait()

    def feed(b, _):
        rows = block_rows(b)
        att = jnp.concatenate([attended[j, rows, :] for j in range(PAIRS)], axis=1)
        h = resid0[rows, :] + (mm(att, wo[...]) + bo)
        n, inv = norm(h)
        f = (n * g2 + b2).astype(BF)
        fin[rows, :] = f
        ok = lax.broadcasted_iota(jnp.int32, (BLK, 1), 0) < valid_len(lens, b)
        do = jnp.where(ok, cs[rows, :].astype(F32), 0.0)
        d = do.astype(BF)
        dff[rows, :] = d
        small[0:1, :] += jnp.sum(do, axis=0, keepdims=True)
        acc = h + bd
        e2 = jnp.zeros((BLK, D), F32)
        for c in range(4):
            pre = mm(f, wu[c]) + vecs[v0 + 8 + c:v0 + 9 + c]
            cdf, pdf = phi_parts(pre)
            a = (pre * cdf).astype(BF)
            wdc = wd[512 * c:512 * c + 512, :]
            dp = (mm_nt(d, wdc) * (cdf + pre * pdf)).astype(BF)
            act[c, rows, :] = a
            dpre[c, rows, :] = dp
            small[4 + c:5 + c, :] += jnp.sum(dp.astype(F32), axis=0, keepdims=True)
            acc = acc + mm(a, wdc)
            e2 = e2 + mm_nt(dp, wu[c])
        xs[rows, :] = acc.astype(BF)
        pltpu.make_async_copy(xs.at[rows], out_hbm.at[rows], outs.at[b]).start()
        small[1:2, :] += jnp.sum(e2 * n, axis=0, keepdims=True)
        small[2:3, :] += jnp.sum(e2, axis=0, keepdims=True)
        dr = do + norm_back(e2 * g2, n, inv)
        dres[rows, :] = dr
        db = dr.astype(BF)
        dbr[rows, :] = db
        small[3:4, :] += jnp.sum(db.astype(F32), axis=0, keepdims=True)
        da = mm_nt(db, wo[...]).astype(BF)
        for j in range(PAIRS):
            datt[j, rows, :] = da[:, lanes(j)]
        return 0

    lax.fori_loop(0, NB, feed, 0)
    for c in range(4):
        src[ROW_DOWN + 512 * c:ROW_DOWN + 512 * c + 512, :] = mm_tn(act[c], dff[...]).astype(BF)
        put(wf, c, 4, mm_tn(fin[...], dpre[c]))
    take(wf, 4, src, ROW_UP)
    for j in range(PAIRS):
        src[ROW_O + 128 * j:ROW_O + 128 * j + 128, :] = mm_tn(attended[j], dbr[...]).astype(BF)

    reduce = Reduce(p, src, g, rcs, rcr, rps, rpr, rzs, rzr)
    wait_all(p, ready)
    for r in plan.late:
        reduce.stage(0, r, plan.late_pick)

    def reduce_hook(i):
        for k, r in enumerate(plan.late):
            for s, at in ((1, 1 + 3 * k), (2, 4 + 3 * k), (3, 6 + 3 * k)):
                when(i == min(at, PAIRS * NB))(lambda: reduce.stage(s, r, plan.late_pick))

    def attend_back(i, _):
        reduce_hook(i)
        pair, qb = lax.div(i, NB), lax.rem(i, NB)
        rows = block_rows(qb)
        q = qkv[pair, rows, :] * jnp.asarray(SCALE, BF)
        k = qkv[PAIRS + pair]
        v = qkv[2 * PAIRS + pair]
        do = datt[pair, rows, :]
        bias = key_bias(lens, qb)
        dqs = []

        @pl.when(qb == 0)
        def _():
            accv[...] = jnp.zeros_like(accv)

        for par in (0, 1):
            half = lane_half(par)
            qm = jnp.where(half, q, jnp.zeros_like(q))
            dm = jnp.where(half, do, jnp.zeros_like(do))
            pp = jnp.exp(mm_nt(k, qm) + bias - lse[pl.ds(2 * pair + par, 1), rows])
            dp = mm_nt(v, dm)
            delta = jnp.sum(pp * dp, axis=0, keepdims=True)
            ds = (pp * (dp - delta)).astype(BF)
            accv[1] += mm(pp.astype(BF), dm)
            accv[0] += mm(ds, qm)
            dqs.append(mm_tn(ds, k))
        dqkv[pair, rows, :] = (jnp.where(lane_half(0), dqs[0], dqs[1]) * SCALE).astype(BF)

        @pl.when(qb == NB - 1)
        def _():
            dqkv[PAIRS + pair] = accv[0].astype(BF)
            dqkv[2 * PAIRS + pair] = accv[1].astype(BF)
        return 0

    lax.fori_loop(0, PAIRS * NB, attend_back, 0)
    reduce_hook(PAIRS * NB)

    cols = []
    for c in range(3):
        dq = jnp.concatenate([dqkv[4 * c + j] for j in range(4)], axis=1)
        put(wf, c, 3, mm_tn(attn_in[...], dq))
        if c != 1:
            cols.append(jnp.sum(dq.astype(F32), axis=0, keepdims=True))
    take(wf, 3, src, 0)
    heads = [r for r in plan.early if r < plan.lo]
    tails = [r for r in plan.early if r >= plan.lo]
    for r in heads:
        reduce.stage(0, r, plan.early_pick)
    slots[...] = jnp.zeros_like(slots)
    cacc[...] = jnp.zeros_like(cacc)

    def embed_back(b, _):
        rows = block_rows(b)

        @pl.when(b == 1)
        def _():
            for r in heads:
                reduce.stage(1, r, plan.early_pick)

        e1 = jnp.zeros((BLK, D), F32)
        for c in range(3):
            dq = jnp.concatenate([dqkv[4 * c + j, rows, :] for j in range(4)], axis=1)
            e1 = e1 + mm_nt(dq, wq[c])
        n, inv = norm(resid0[rows, :])
        slots[8:9, :] += jnp.sum(e1 * n, axis=0, keepdims=True)
        slots[9:10, :] += jnp.sum(e1, axis=0, keepdims=True)
        gi = dres[rows, :] + norm_back(e1 * g1, n, inv)
        resid0[rows, :] = gi
        pltpu.make_async_copy(resid0.at[rows], gin_hbm.at[rows], gins.at[b]).start()
        ds = gi.astype(BF)
        oh = (lax.broadcasted_iota(jnp.int32, (32, BLK), 0) == ids[0:1, rows]).astype(F32).astype(BF)
        cacc[0:32, :] += mm(oh, ds)
        slots[pl.ds(b, 1), :] = jnp.sum(ds.astype(F32), axis=0, keepdims=True)
        return 0

    lax.fori_loop(0, NB, embed_back, 0)
    per = slots[0:8, :]
    total = jnp.sum(per, axis=0, keepdims=True)
    first = lax.broadcasted_iota(jnp.int32, (8, 1), 0) == 0
    per = jnp.where(long, jnp.where(first, total, 0.0), per)
    src[ROW_T:ROW_C, :] = lax.dot_general(
        feat[...].astype(F32), per, (((0,), (0,)), ((), ())),
        precision=lax.Precision.HIGHEST, preferred_element_type=F32,
    ).astype(BF)
    o = ROW_V - ROW_C
    cacc[o:o + 2, :] = slots[8:10, :]
    cacc[o + 2:o + 4, :] = small[1:3, :]
    cacc[o + 4:o + 5, :] = cols[0]
    cacc[o + 5:o + 6, :] = cols[1]
    cacc[o + 6:o + 7, :] = small[3:4, :]
    cacc[o + 7:o + 8, :] = small[0:1, :]
    cacc[o + 8:o + 12, :] = small[4:8, :]
    src[ROW_C:ROW_C + TAIL, :] = cacc[...].astype(BF)
    if plan.padded > ROW_C + TAIL:
        src[ROW_C + TAIL:plan.padded, :] = jnp.zeros((plan.padded - ROW_C - TAIL, ROW), BF)

    for r in tails:
        reduce.stage(0, r, plan.early_pick)
    for r in heads:
        reduce.stage(2, r, plan.early_pick)
    for r in tails:
        reduce.stage(1, r, plan.early_pick)
    for r in heads:
        reduce.stage(3, r, plan.early_pick)
    for s in (2, 3):
        for r in tails:
            reduce.stage(s, r, plan.early_pick)
    reduce.finish(own)
    reduce.drain()
    for b in range(NB):
        rows = pl.ds(b * BLK, BLK)
        pltpu.make_async_copy(xs.at[rows], out_hbm.at[rows], outs.at[b]).wait()
        pltpu.make_async_copy(resid0.at[rows], gin_hbm.at[rows], gins.at[b]).wait()


def layer(plan, lens, ids, feat, x, cot, chunk):
    S = jax.ShapeDtypeStruct
    V = pltpu.VMEM
    DM = pltpu.SemaphoreType.DMA
    nz, n = plan.nz, plan.rows
    vm = pl.BlockSpec(memory_space=pltpu.VMEM)
    hb = pl.BlockSpec(memory_space=pl.ANY)

    def kernel(*refs):
        body(plan, *refs)

    return pl.pallas_call(
        kernel,
        out_shape=[S((T, D), BF), S((T, D), F32), S((n, ROW), F32)],
        in_specs=[pl.BlockSpec(memory_space=pltpu.SMEM), vm, vm, hb, hb, hb],
        out_specs=[hb, hb, vm],
        scratch_shapes=[
            V((nz, 2, 2, 2, n, ROW), BF), V((plan.padded, ROW), BF), V((4, 2048, 128), F32),
            V((3, D, D), BF), V((4, D, D), BF), V((D, D), BF), V((2048, D), BF), V((256 + TAIL, D), BF),
            V((T, D), BF), V((T, D), BF), V((T, D), F32), V((T, D), BF), V((12, T, 128), BF),
            V((PAIRS, T, 128), BF), V((8, T), F32), V((8, D), F32),
            V((4, T, D), BF), V((4, T, D), BF), V((T, D), BF), V((T, D), BF), V((T, D), BF), V((T, D), F32),
            V((PAIRS, T, 128), BF), V((12, T, 128), BF), V((2, T, 128), F32), V((16, D), F32), V((8, D), F32),
            V((TAIL, D), F32),
            DM((nz, 2, 2)), DM((nz, 2)), DM((nz, AG_KINDS)), DM((nz, AG_KINDS)),
            DM((nz, 2, 2)), DM((nz, 2, 2)), DM((nz, RS_KINDS)), DM((nz, RS_KINDS)), DM((nz,)), DM((nz,)),
            pltpu.SemaphoreType.REGULAR, DM((3,)), DM((NB,)), DM((NB,)),
        ],
        compiler_params=pltpu.CompilerParams(
            collective_id=0, has_side_effects=True, vmem_limit_bytes=67043328
        ),
        name="layer",
    )(lens, ids, feat, x, cot, chunk)


def time_features(steps):
    half = 128
    freqs = jnp.exp(-math.log(10000.0) * jnp.arange(half, dtype=F32) / half)
    ang = steps.astype(F32).reshape(4, 1) * freqs
    f = jnp.concatenate([jnp.sin(ang), jnp.cos(ang)], axis=-1).astype(BF)
    return jnp.pad(f, ((0, 4), (0, 0)))


def shards(inputs, noisy_ids, timesteps, doc_lens, cotangent, params, momentum, average):
    ndp, nfs = lax.axis_size("dp"), lax.axis_size("fsdp")
    device_count = ndp * nfs
    row_count, seq_len, model_width = inputs.shape
    plan = Plan(ndp, nfs, params.shape[0] * device_count)
    i = lax.axis_index("dp") * nfs + lax.axis_index("fsdp")
    offset = lax.rem(i * plan.share, ROW * TILE)
    chunk = lax.dynamic_update_slice(
        jnp.zeros((plan.rows * ROW,), BF), params.astype(BF), (offset,)
    ).reshape(plan.rows, ROW)
    output, input_grad, owned = layer(
        plan, doc_lens, noisy_ids, time_features(timesteps),
        inputs.reshape(T, D), cotangent.reshape(T, D), chunk,
    )
    owned_grad = lax.dynamic_slice(owned.reshape(-1), (offset,), (plan.share,))
    gradient = owned_grad * (1.0 / math.sqrt(row_count * seq_len * device_count))
    new_momentum = MOMENTUM_RATE * momentum + gradient
    new_params = params - LEARN_RATE * (gradient + MOMENTUM_RATE * new_momentum)
    new_average = AVERAGE_RATE * average + (1.0 - AVERAGE_RATE) * new_params
    return (
        output.reshape(row_count, seq_len, model_width),
        input_grad.reshape(row_count, seq_len, model_width),
        new_params,
        new_momentum,
        new_average,
        new_params.astype(BF),
    )


def solution(mesh):
    rows = ("dp", "fsdp")
    in_specs = (
        P(rows, None, None), P(rows, None), P(rows, None), P(rows, None), P(rows, None, None),
        P(rows), P(rows), P(rows),
    )
    out_specs = (P(rows, None, None), P(rows, None, None), P(rows), P(rows), P(rows), P(rows))
    return jax.shard_map(shards, mesh=mesh, in_specs=in_specs, out_specs=out_specs, check_vma=False)
```

```python
import math

import jax
import jax.numpy as jnp
from jax import lax
from jax.experimental import pallas as pl
from jax.experimental.pallas import tpu as pltpu
from jax.sharding import PartitionSpec as P

MOMENTUM_RATE = 0.9
LEARN_RATE = 0.02
AVERAGE_RATE = 0.8
EPSILON = 1e-5
MESH = pl.DeviceIdType.MESH
BF = jnp.bfloat16
F32 = jnp.float32
ROW = 512
TILE = 16
T = 1024
D = 512
BLK = 256
NB = T // BLK
PAIRS = 4
SCALE = 0.125
ROW_O, ROW_UP, ROW_DOWN, ROW_T, ROW_C, ROW_V = 1536, 2048, 4096, 6144, 6400, 6427
TAIL = 48
AG_KINDS = 13
RS_KINDS = 6
HOOKS = NB + PAIRS * NB


class Plan:
    def __init__(self, ndp, nfs, total):
        self.nx, self.ny, self.nc = 2, 2, nfs // 2
        self.nz = ndp // 2
        self.count = ndp * nfs
        self.share = total // self.count
        self.starts = [((i * self.share) // (ROW * TILE)) * TILE for i in range(self.count)]
        ends = [-(-((i + 1) * self.share) // ROW) for i in range(self.count)]
        need = max(e - s for e, s in zip(ends, self.starts))
        self.rows = max(2, -(-need // TILE)) * TILE
        self.half = -(-self.rows // (2 * TILE)) * TILE
        self.padded = max(max(self.starts) + self.rows, ROW_C + TAIL)
        layer = self.count // self.nz
        last = self.nz - 1
        self.lo = next(r for r in range(self.nz) if self.starts[r * layer] >= ROW_O)
        first = next(i for i in range(self.count) if self.starts[i] + self.rows > ROW_T)
        self.only = first >= self.count - self.nc
        self.hi = last if self.only else first // layer - 1
        self.early = list(range(self.lo)) + list(range(last if self.only else self.hi + 1, self.nz))
        self.late = list(range(self.lo, self.hi + 1))
        self.ends = [r for r in self.early if r >= self.lo]
        self.owners = [i for i in range(self.count) if self.starts[i] + self.rows > ROW_T]
        self.slices = PAIRS if self.lo == 1 else 1
        self.units = [(r, None) for r in range(self.lo, self.nz)]
        self.body_units = len(self.units)
        for j in range(self.slices):
            self.units += [(r, None if self.slices == 1 else j) for r in range(self.lo)]

    def slice_units(self, j):
        return range(self.body_units + j * self.lo, self.body_units + (j + 1) * self.lo)

    def early_pick(self, r, cx, cy):
        if self.only and r == self.nz - 1:
            return cx * cy == 1
        return True

    def late_pick(self, r, cx, cy):
        if self.only and r == self.nz - 1:
            return cx * cy == 0
        return True


class Place:
    def __init__(self, plan):
        d = lax.axis_index("dp")
        f = lax.axis_index("fsdp")
        self.plan = plan
        two = jnp.int32(2)
        self.z, self.x = lax.div(d, two), lax.rem(d, two)
        self.y, self.c = lax.div(f, two), lax.rem(f, two)
        self.X = self.dev(x=1 - self.x)
        self.Y = self.dev(y=1 - self.y)
        self.C = self.dev(c=1 - self.c)

    def dev(self, z=None, x=None, y=None, c=None):
        z = self.z if z is None else z
        x = self.x if x is None else x
        y = self.y if y is None else y
        c = self.c if c is None else c
        return (z * 2 + x, y * 2 + c)

    def here(self):
        return ((self.z * 2 + self.x) * 2 + self.y) * 2 + self.c

    def partners(self):
        nz = self.plan.nz
        others = [self.dev(z=lax.rem(self.z + s, jnp.int32(nz))) for s in range(1, nz)]
        return [self.X, self.Y, self.C] + others

    def far(self, r):
        return jnp.abs(self.z - r)


def signal_all(place, sem):
    for dev in place.partners():
        pl.semaphore_signal(sem, inc=1, device_id=dev, device_id_type=MESH)


def wait_all(place, sem):
    pl.semaphore_wait(sem, 3 + place.plan.nz - 1)


def rcopy(src, dst, ss, rs, dev):
    return pltpu.make_async_remote_copy(
        src_ref=src, dst_ref=dst, send_sem=ss, recv_sem=rs, device_id=dev, device_id_type=MESH
    )


def when(*conds):
    real = [c for c in conds if c is not True]

    def run(f):
        if not real:
            return f()
        c = real[0]
        for other in real[1:]:
            c = c & other
        return pl.when(c)(f)

    return run


class Gather:
    def __init__(self, p, g, zs, zr, ps, pr):
        self.p, self.g, self.zs, self.zr, self.ps, self.pr = p, g, zs, zr, ps, pr
        h, n = p.plan.half, p.plan.rows
        self.parts = (pl.ds(0, h), pl.ds(h, n - h), pl.ds(0, n))

    def zcopy(self, r, j, up):
        p = self.p
        ref = self.g.at[r, p.x, p.y, p.c, self.parts[j]]
        return rcopy(ref, ref, self.zs.at[r, j, 0 if up else 1], self.zr.at[r, j], p.dev(z=p.z + 1 if up else p.z - 1))

    def cp(self, r, k):
        p = self.p
        a, b, w = self.parts
        x, y = p.x, p.y
        cx, cy, part, dev = (
            (x, y, a, p.X), (x, y, b, p.Y), (x, y, a, p.Y), (x, y, b, p.X),
            (1 - x, y, a, p.Y), (x, 1 - y, b, p.X), (x, y, w, p.C), (1 - x, y, a, p.C), (x, 1 - y, b, p.C),
            (x, 1 - y, a, p.C), (1 - x, 1 - y, a, p.C), (1 - x, y, b, p.C), (1 - x, 1 - y, b, p.C),
        )[k]
        ref = self.g.at[r, cx, cy, p.c, part]
        return rcopy(ref, ref, self.ps.at[r, k], self.pr.at[r, k], dev)

    def stage(self, s, r, pick):
        p = self.p
        z, x, y, nz = p.z, p.x, p.y, p.plan.nz
        if s == 0:
            for j in (0, 1):
                if r < nz - 1:
                    when(z == r, pick(r, x, y))(lambda: self.zcopy(r, j, True).start())
                if r > 0:
                    when(z == r, pick(r, x, y))(lambda: self.zcopy(r, j, False).start())
        if s == 1:
            for j in (0, 1):
                when(z != r, pick(r, x, y))(lambda: self.zcopy(r, j, True).wait_recv())
                if 0 < r < nz - 1 or r == 0:
                    when(z > r, z < nz - 1, pick(r, x, y))(lambda: self.zcopy(r, j, True).start())
                if r > 0:
                    when(z < r, z > 0, pick(r, x, y))(lambda: self.zcopy(r, j, False).start())
                when(pick(r, x, y))(lambda: self.cp(r, j).start())

            def rest():
                for k in (2, 3, 6):
                    self.cp(r, k).start()

            when(pick(r, x, y))(rest)
        if s == 2:
            for k, a, b, cx, cy in ((0, 4, 7, 1 - x, y), (1, 5, 8, x, 1 - y)):
                def go():
                    self.cp(r, k).wait_recv()
                    self.cp(r, a).start()
                    self.cp(r, b).start()

                when(pick(r, cx, cy))(go)
        if s == 3:
            for k, a, cx, cy in ((2, 9, x, 1 - y), (4, 10, 1 - x, 1 - y), (3, 11, 1 - x, y), (5, 12, 1 - x, 1 - y)):
                def go():
                    self.cp(r, k).wait_recv()
                    self.cp(r, a).start()

                when(pick(r, cx, cy))(go)
        if s == 4:
            for ks, cx, cy in (((6,), x, y), ((7, 11), 1 - x, y), ((8, 9), x, 1 - y), ((10, 12), 1 - x, 1 - y)):
                def go():
                    for k in ks:
                        self.cp(r, k).wait_recv()

                when(pick(r, cx, cy))(go)

    def drain(self):
        z, nz = self.p.z, self.p.plan.nz
        for r in range(nz):
            for j in (0, 1):
                if r < nz - 1:
                    when(z >= r, z < nz - 1)(lambda: self.zcopy(r, j, True).wait_send())
                if r > 0:
                    when(z <= r, z > 0)(lambda: self.zcopy(r, j, False).wait_send())
            for k in range(AG_KINDS):
                self.cp(r, k).wait_send()


class Reduce:
    def __init__(self, p, src, g, cs, cr, ps, pr, zs, zr):
        self.p, self.src, self.g = p, src, g
        self.cs, self.cr, self.ps, self.pr, self.zs, self.zr = cs, cr, ps, pr, zs, zr
        self.h, self.n = p.plan.half, p.plan.rows
        self.a, self.b, self.w = pl.ds(0, self.h), pl.ds(self.h, self.n - self.h), pl.ds(0, self.n)

    def cols(self, j):
        return pl.ds(0, ROW) if j is None else pl.ds(128 * j, 128)

    def rows(self, r, xx, yy, cc):
        plan = self.p.plan
        i = ((r * 2 + xx) * 2 + yy) * 2 + cc
        return pl.ds(pl.multiple_of(lax.div(i * plan.share, jnp.int32(ROW * TILE)) * TILE, TILE), self.n)

    def cb(self, u, xx, yy, part):
        r, j = self.p.plan.units[u]
        return self.g.at[r, xx, yy, 0, part, self.cols(j)]

    def pa(self, u, xx):
        r, j = self.p.plan.units[u]
        return self.g.at[r, 0, xx, 1, self.a, self.cols(j)]

    def pb(self, u, yy):
        r, j = self.p.plan.units[u]
        return self.g.at[r, 0, yy, 1, self.b, self.cols(j)]

    def p2(self, u, part):
        r, j = self.p.plan.units[u]
        return self.g.at[r, 1, 0, 1, part, self.cols(j)]

    def ccopy(self, u, xx, yy):
        p = self.p
        r, j = p.plan.units[u]
        return rcopy(
            self.src.at[self.rows(r, xx, yy, 1 - p.c), self.cols(j)], self.cb(u, xx, yy, self.w),
            self.cs.at[u, xx, yy], self.cr.at[u, xx, yy], p.C,
        )

    def cp(self, u, k):
        p = self.p
        x, y = p.x, p.y
        s, d, dev = (
            (self.cb(u, 0, 1 - y, self.a), self.pa(u, 0), p.Y),
            (self.cb(u, 1, 1 - y, self.a), self.pa(u, 1), p.Y),
            (self.cb(u, 1 - x, 0, self.b), self.pb(u, 0), p.X),
            (self.cb(u, 1 - x, 1, self.b), self.pb(u, 1), p.X),
            (self.pa(u, 1 - x), self.p2(u, self.a), p.X),
            (self.pb(u, 1 - y), self.p2(u, self.b), p.Y),
        )[k]
        return rcopy(s, d, self.ps.at[u, k], self.pr.at[u, k], dev)

    def zcopy(self, u):
        p = self.p
        r, j = p.plan.units[u]
        k = j or 0
        return rcopy(
            self.p2(u, self.w), self.g.at[p.z, 1, 1, 1, self.w, self.cols(j)],
            self.zs.at[u], self.zr.at[k, p.z], p.dev(z=r),
        )

    def zwait(self, j, s):
        ref = self.g.at[s, 1, 1, 1, self.w, self.cols(j)]
        rcopy(ref, ref, self.zs.at[0], self.zr.at[j or 0, s], self.p.dev(z=s)).wait_recv()

    def stage(self, s, u):
        p = self.p
        z, x, y = p.z, p.x, p.y
        r, j = p.plan.units[u]
        both = [(xx, yy) for xx in (0, 1) for yy in (0, 1)]
        if s == 0:
            for xx, yy in both:
                self.ccopy(u, xx, yy).start()
        if s == 1:
            for xx, yy in both:
                self.ccopy(u, xx, yy).wait_recv()
                ref = self.cb(u, xx, yy, self.w)
                ref[...] = ref[...] + self.src[self.rows(r, xx, yy, p.c), self.cols(j)]
            for q in (0, 1):
                self.cp(u, q).start()
                self.cp(u, 2 + q).start()
        if s == 2:
            for q in (0, 1):
                self.cp(u, q).wait_recv()
                ref = self.pa(u, q)
                ref[...] = ref[...] + self.cb(u, q, y, self.a)[...]
            self.cp(u, 4).start()
            for q in (0, 1):
                self.cp(u, 2 + q).wait_recv()
                ref = self.pb(u, q)
                ref[...] = ref[...] + self.cb(u, x, q, self.b)[...]
            self.cp(u, 5).start()
        if s == 3:
            self.cp(u, 4).wait_recv()
            ref = self.p2(u, self.a)
            ref[...] = ref[...] + self.pa(u, x)[...]
            self.cp(u, 5).wait_recv()
            ref = self.p2(u, self.b)
            ref[...] = ref[...] + self.pb(u, y)[...]
            when(z != r)(lambda: self.zcopy(u).start())

    def finish(self, out):
        z, plan = self.p.z, self.p.plan
        out[...] = self.g[z, 1, 0, 1].astype(F32)
        for s in range(plan.nz):
            def go():
                @pl.when(z >= plan.lo)
                def _():
                    self.zwait(None, s)

                @pl.when(z < plan.lo)
                def _():
                    for j in range(plan.slices):
                        self.zwait(None if plan.slices == 1 else j, s)

                out[...] += self.g[s, 1, 1, 1].astype(F32)

            when(z != s)(go)

    def drain(self):
        for u, (r, _) in enumerate(self.p.plan.units):
            for xx in (0, 1):
                for yy in (0, 1):
                    self.ccopy(u, xx, yy).wait_send()
            for k in range(RS_KINDS):
                self.cp(u, k).wait_send()
            when(self.p.z != r)(lambda: self.zcopy(u).wait_send())


class Corner:
    def __init__(self, p, t, rx, zt, ss, rs, zs, zr):
        self.p, self.t, self.rx, self.zt = p, t, rx, zt
        self.ss, self.rs, self.zs, self.zr = ss, rs, zs, zr

    def copy(self, k):
        p = self.p
        return rcopy(self.t.at[k], self.rx.at[k], self.ss.at[k], self.rs.at[k], (p.C, p.Y, p.X)[k])

    def zcopy(self, m):
        p = self.p
        return rcopy(
            self.t.at[3], self.zt.at[p.z], self.zs.at[m], self.zr.at[p.z], p.dev(z=p.plan.ends[m])
        )

    def senders(self, m):
        p = self.p
        return when(p.z != p.plan.ends[m], p.plan.early_pick(p.plan.ends[m], p.x, p.y))

    def start(self):
        self.copy(0).start()

    def step(self, k):
        self.copy(k).wait_recv()
        self.t[k + 1] = self.t[k] + self.rx[k]
        if k < 2:
            self.copy(k + 1).start()
        else:
            for m in range(len(self.p.plan.ends)):
                self.senders(m)(lambda: self.zcopy(m).start())

    def finish(self, r):
        p = self.p
        self.zt[r] = self.t[3]
        for s in range(p.plan.nz):
            if s != r:
                ref = self.zt.at[s]
                rcopy(ref, ref, self.zs.at[0], self.zr.at[s], p.dev(z=s)).wait_recv()

    def drain(self):
        for k in range(3):
            self.copy(k).wait_send()
        for m in range(len(self.p.plan.ends)):
            self.senders(m)(lambda: self.zcopy(m).wait_send())


def assemble(plan, g, lo, hi, store):
    for i in range(plan.count):
        at = lambda k: (k // 8, (k // 4) % 2, (k // 2) % 2, k % 2)
        s = plan.starts[i]
        e = plan.starts[i + 1] if i + 1 < plan.count else plan.padded
        if lo <= s < hi:
            head = g[at(i) + (slice(0, TILE),)]
            if i and s - plan.starts[i - 1] < plan.rows:
                d = s - plan.starts[i - 1]
                head = head + g[at(i - 1) + (slice(d, d + TILE),)]
            store(s, s + TILE, head)
        a, b = max(s + TILE, lo), min(e, hi, s + plan.rows)
        if b > a:
            store(a, b, g[at(i) + (slice(a - s, b - s),)])


def mm(a, b):
    return lax.dot_general(a, b, (((1,), (0,)), ((), ())), preferred_element_type=F32)


def mm_nt(a, b):
    return lax.dot_general(a, b, (((1,), (1,)), ((), ())), preferred_element_type=F32)


def mm_tn(a, b):
    return lax.dot_general(a, b, (((0,), (0,)), ((), ())), preferred_element_type=F32)


def norm(h):
    mean = jnp.mean(h, axis=-1, keepdims=True)
    cen = h - mean
    inv = lax.rsqrt(jnp.mean(cen * cen, axis=-1, keepdims=True) + EPSILON)
    return cen * inv, inv


def norm_back(dn, n, inv):
    return (dn - jnp.mean(dn, axis=-1, keepdims=True) - n * jnp.mean(dn * n, axis=-1, keepdims=True)) * inv


def valid_len(lens, b):
    long = lens[0, 1] == 0
    short = lens[0, 0]
    for k in range(1, NB):
        short = jnp.where(b == k, lens[0, k], short)
    return jnp.where(long, lens[0, 0] - b * BLK, short)


def lane_half(par):
    lane = lax.broadcasted_iota(jnp.int32, (1, 128), 1)
    return (lane >= 64) if par else (lane < 64)


def key_bias(lens, qb):
    long = lens[0, 1] == 0
    cols = []
    it = lax.broadcasted_iota(jnp.int32, (BLK, 1), 0)
    for kb in range(NB):
        thr = jnp.where(long | (qb == kb), valid_len(lens, kb), 0)
        cols.append(jnp.where(it < thr, 0.0, -1e30).astype(F32))
    return jnp.concatenate(cols, axis=0)


def lanes(j):
    return slice(128 * j, 128 * j + 128)


def spread(wf, base):
    def store(a, b, val):
        for j in range(4):
            wf[j, a - base:b - base, :] = val[:, lanes(j)].astype(F32)
    return store


def regroup(wf, n, to):
    for c in range(n):
        for j in range(4):
            to[c, :, lanes(j)] = wf[j, pl.ds(c, 512, stride=n), :].astype(BF)


def put(wf, c, n, val):
    for j in range(4):
        wf[j, pl.ds(c, 512, stride=n), :] = val[:, lanes(j)]


def take(wf, n, out, base):
    for j in range(4):
        out[base:base + 512 * n, lanes(j)] = wf[j, 0:512 * n, :].astype(BF)


def phi_parts(v):
    cdf = 0.5 * (1.0 + lax.erf(v * (2.0 ** -0.5)))
    pdf = jnp.exp(v * v * -0.5) * (1.0 / math.sqrt(2.0 * math.pi))
    return cdf, pdf


def block_rows(b):
    return pl.ds(pl.multiple_of(b * BLK, BLK), BLK)


def body(plan, lens, ids, feat, x_hbm, cot_hbm, chunk_hbm, out_hbm, gin_hbm, own,
         g, src, wf, wq, wu, wo, wd, vec, xs, cs, resid0, attn_in, qkv, attended, lse, ft,
         act, dpre, fin, dff, dbr, dres, datt, dqkv, accv, slots, small, cacc,
         ct, crx, czt, ht, hrx, hzt, tg,
         zs, zr, ps, pr, rcs, rcr, rps, rpr, rzs, rzr,
         css, crs, czs, czr, hss, hrs, hzs, hzr, ready, ins, outs, gins):
    p = Place(plan)
    nz = plan.nz
    corner = Corner(p, ct, crx, czt, css, crs, czs, czr)
    hints = Corner(p, ht, hrx, hzt, hss, hrs, hzs, hzr)
    place = lax.div(lax.broadcasted_iota(jnp.int32, (32, 1), 0), jnp.int32(4)) == (p.x * 2 + p.y) * 2 + p.c
    gather = Gather(p, g, zs, zr, ps, pr)
    loads = [
        pltpu.make_async_copy(chunk_hbm, g.at[p.z, p.x, p.y, p.c], ins.at[0]),
        pltpu.make_async_copy(x_hbm, xs, ins.at[1]),
        pltpu.make_async_copy(cot_hbm, cs, ins.at[2]),
    ]
    for cpy in loads:
        cpy.start()
    bar = pltpu.get_barrier_semaphore()
    signal_all(p, bar)
    wait_all(p, bar)
    loads[0].wait()

    for r in plan.early:
        gather.stage(0, r, plan.early_pick)
    for t in range(nz + 3):
        for s in (4, 3, 2, 1):
            for r in plan.early:
                if 0 <= t - (s - 1) < nz:
                    when(p.far(r) == t - (s - 1))(lambda: gather.stage(s, r, plan.early_pick))
    for r in plan.late:
        gather.stage(0, r, plan.late_pick)
    ht[0] = jnp.where(place, jnp.concatenate([feat[...].astype(F32)] * 4, axis=0), 0.0).astype(BF)
    hints.start()

    def gather_hook(i):
        for s in (1, 2, 3, 4):
            for r in plan.late:
                start = lax.div(9 * p.far(r) + 2, jnp.int32(2)) + (0, 0, 3, 6, 7)[s]
                when(i == jnp.minimum(start, HOOKS))(lambda: gather.stage(s, r, plan.late_pick))

    assemble(plan, g, 0, ROW_O, spread(wf, 0))
    regroup(wf, 3, wq)

    def tail_store(a, b, val):
        vec[a - ROW_T:b - ROW_T, :] = val

    assemble(plan, g, ROW_T, ROW_C + TAIL, tail_store)
    ctab = vec[256:288, :]
    vecs = vec[272:304, :].astype(F32)
    v0 = ROW_V - ROW_C - 16
    g1, b1, g2, b2, bq, bv, bo, bd = (vecs[v0 + k:v0 + k + 1] for k in range(8))
    ft[...] = mm(feat[...], vec[0:256, :])
    long = lens[0, 1] == 0
    loads[1].wait()

    def embed(b, _):
        gather_hook(b)
        rows = block_rows(b)
        oh = (lax.broadcasted_iota(jnp.int32, (32, BLK), 0) == ids[0:1, rows]).astype(F32).astype(BF)
        side = mm_tn(oh, ctab)
        slot = jnp.where(long, 0, b)
        h = xs[rows, :].astype(F32) + (side + ft[pl.ds(slot, 1), :])
        resid0[rows, :] = h
        n, _i = norm(h)
        a = (n * g1 + b1).astype(BF)
        attn_in[rows, :] = a
        for c in range(3):
            pr_ = mm(a, wq[c])
            if c == 0:
                pr_ = pr_ + bq
            if c == 2:
                pr_ = pr_ + bv
            pr_ = pr_.astype(BF)
            for j in range(4):
                qkv[4 * c + j, rows, :] = pr_[:, lanes(j)]
        return 0

    lax.fori_loop(0, NB, embed, 0)
    ones = jnp.ones((T, 128), BF)

    def attend(i, _):
        gather_hook(i + NB)
        pair, qb = lax.div(i, NB), lax.rem(i, NB)
        rows = block_rows(qb)
        q = qkv[pair, rows, :] * jnp.asarray(SCALE, BF)
        k = qkv[PAIRS + pair]
        va = jnp.concatenate([qkv[2 * PAIRS + pair], ones], axis=1)
        bias = key_bias(lens, qb)
        heads = []
        for par in (0, 1):
            qm = jnp.where(lane_half(par), q, jnp.zeros_like(q))
            s = mm_nt(k, qm) + bias
            m = jnp.max(s, axis=0, keepdims=True)
            e = jnp.exp(s - m)
            l = jnp.sum(e, axis=0, keepdims=True)
            lse[pl.ds(2 * pair + par, 1), rows] = m + jnp.log(l)
            oa = mm_tn(e.astype(BF), va)
            heads.append(oa[:, :128] / oa[:, 128:])
        attended[pair, rows, :] = jnp.where(lane_half(0), heads[0], heads[1]).astype(BF)
        return 0

    lax.fori_loop(0, PAIRS * NB, attend, 0)
    gather_hook(HOOKS)

    def wo_store(a, b, val):
        wo[a - ROW_O:b - ROW_O, :] = val

    def wd_store(a, b, val):
        wd[a - ROW_DOWN:b - ROW_DOWN, :] = val

    assemble(plan, g, ROW_O, ROW_UP, wo_store)
    assemble(plan, g, ROW_UP, ROW_DOWN, spread(wf, ROW_UP))
    assemble(plan, g, ROW_DOWN, ROW_T, wd_store)
    regroup(wf, 4, wu)
    hints.step(0)
    gather.drain()
    signal_all(p, ready)
    small[...] = jnp.zeros_like(small)
    loads[2].wait()

    def feed(b, _):
        rows = block_rows(b)
        att = jnp.concatenate([attended[j, rows, :] for j in range(PAIRS)], axis=1)
        h = resid0[rows, :] + (mm(att, wo[...]) + bo)
        n, inv = norm(h)
        f = (n * g2 + b2).astype(BF)
        fin[rows, :] = f
        ok = lax.broadcasted_iota(jnp.int32, (BLK, 1), 0) < valid_len(lens, b)
        do = jnp.where(ok, cs[rows, :].astype(F32), 0.0)
        d = do.astype(BF)
        dff[rows, :] = d
        small[0:1, :] += jnp.sum(do, axis=0, keepdims=True)
        acc = h + bd
        e2 = jnp.zeros((BLK, D), F32)
        for c in range(4):
            pre = mm(f, wu[c]) + vecs[v0 + 8 + c:v0 + 9 + c]
            cdf, pdf = phi_parts(pre)
            a = (pre * cdf).astype(BF)
            wdc = wd[512 * c:512 * c + 512, :]
            dp = (mm_nt(d, wdc) * (cdf + pre * pdf)).astype(BF)
            act[c, rows, :] = a
            dpre[c, rows, :] = dp
            small[4 + c:5 + c, :] += jnp.sum(dp.astype(F32), axis=0, keepdims=True)
            acc = acc + mm(a, wdc)
            e2 = e2 + mm_nt(dp, wu[c])
        xs[rows, :] = acc.astype(BF)
        pltpu.make_async_copy(xs.at[rows], out_hbm.at[rows], outs.at[b]).start()
        small[1:2, :] += jnp.sum(e2 * n, axis=0, keepdims=True)
        small[2:3, :] += jnp.sum(e2, axis=0, keepdims=True)
        dr = do + norm_back(e2 * g2, n, inv)
        dres[rows, :] = dr
        db = dr.astype(BF)
        dbr[rows, :] = db
        small[3:4, :] += jnp.sum(db.astype(F32), axis=0, keepdims=True)
        da = mm_nt(db, wo[...]).astype(BF)
        for j in range(PAIRS):
            datt[j, rows, :] = da[:, lanes(j)]
        return 0

    lax.fori_loop(0, NB, feed, 0)
    hints.step(1)
    src[ROW_T:plan.padded, :] = jnp.zeros((plan.padded - ROW_T, ROW), BF)
    for c in range(4):
        src[ROW_DOWN + 512 * c:ROW_DOWN + 512 * c + 512, :] = mm_tn(act[c], dff[...]).astype(BF)
        put(wf, c, 4, mm_tn(fin[...], dpre[c]))
    take(wf, 4, src, ROW_UP)
    for j in range(PAIRS):
        src[ROW_O + 128 * j:ROW_O + 128 * j + 128, :] = mm_tn(attended[j], dbr[...]).astype(BF)

    reduce = Reduce(p, src, g, rcs, rcr, rps, rpr, rzs, rzr)
    hints.step(2)
    wait_all(p, ready)
    for u in range(plan.body_units):
        reduce.stage(0, u)

    def qkv_grad(j):
        dq = jnp.concatenate([dqkv[4 * c + j] for c in range(3)], axis=1)
        gq = mm_tn(attn_in[...], dq)
        for c in range(3):
            wf[j, pl.ds(c, 512, stride=3), :] = gq[:, lanes(c)]
        src[0:ROW_O, lanes(j)] = wf[j, 0:ROW_O, :].astype(BF)
        for c in (0, 2):
            slots[10 + c // 2:11 + c // 2, lanes(j)] = jnp.sum(dqkv[4 * c + j].astype(F32), axis=0, keepdims=True)

    def slice_start(j):
        qkv_grad(j)
        if plan.slices > 1:
            for u in plan.slice_units(j):
                reduce.stage(0, u)

    def reduce_at(s, u):
        return lambda: reduce.stage(s, u)

    steps = []
    for k in range(plan.body_units):
        for s, at in ((1, 1 + 3 * k), (2, 4 + 3 * k), (3, 6 + 3 * k)):
            steps.append((at, -s, reduce_at(s, k)))
    for j in range(PAIRS - 1):
        steps.append((NB * (j + 1), 0, lambda j=j: slice_start(j)))
        if plan.slices > 1:
            for s, at in ((1, (10, 11, 14)[j]), (2, (12, 13, 15)[j]), (3, (14, 15, 16)[j])):
                for u in plan.slice_units(j):
                    steps.append((at, -s, reduce_at(s, u)))
    steps.sort(key=lambda e: e[:2])

    def reduce_hook(i):
        for at, _, run in steps:
            if at < PAIRS * NB:
                pl.when(i == at)(run)

    def attend_back(i, _):
        reduce_hook(i)
        pair, qb = lax.div(i, NB), lax.rem(i, NB)
        rows = block_rows(qb)
        q = qkv[pair, rows, :] * jnp.asarray(SCALE, BF)
        k = qkv[PAIRS + pair]
        v = qkv[2 * PAIRS + pair]
        do = datt[pair, rows, :]
        bias = key_bias(lens, qb)
        dqs = []

        @pl.when(qb == 0)
        def _():
            accv[...] = jnp.zeros_like(accv)

        for par in (0, 1):
            half = lane_half(par)
            qm = jnp.where(half, q, jnp.zeros_like(q))
            dm = jnp.where(half, do, jnp.zeros_like(do))
            pp = jnp.exp(mm_nt(k, qm) + bias - lse[pl.ds(2 * pair + par, 1), rows])
            dp = mm_nt(v, dm)
            delta = jnp.sum(pp * dp, axis=0, keepdims=True)
            ds = (pp * (dp - delta)).astype(BF)
            accv[1] += mm(pp.astype(BF), dm)
            accv[0] += mm(ds, qm)
            dqs.append(mm_tn(ds, k))
        dqkv[pair, rows, :] = (jnp.where(lane_half(0), dqs[0], dqs[1]) * SCALE).astype(BF)

        @pl.when(qb == NB - 1)
        def _():
            dqkv[PAIRS + pair] = accv[0].astype(BF)
            dqkv[2 * PAIRS + pair] = accv[1].astype(BF)
        return 0

    lax.fori_loop(0, PAIRS * NB, attend_back, 0)
    slice_start(PAIRS - 1)
    last = plan.slice_units(plan.slices - 1)
    if plan.slices == 1:
        for u in last:
            reduce.stage(0, u)
    for at, _, run in steps:
        if at >= PAIRS * NB:
            run()
    slots[0:10, :] = jnp.zeros((10, D), F32)
    cacc[...] = jnp.zeros_like(cacc)

    def embed_back(b, _):
        rows = block_rows(b)

        @pl.when(b == 1)
        def _():
            for u in last:
                reduce.stage(1, u)

        @pl.when(b == 3)
        def _():
            for u in last:
                reduce.stage(2, u)

        e1 = jnp.zeros((BLK, D), F32)
        for c in range(3):
            dq = jnp.concatenate([dqkv[4 * c + j, rows, :] for j in range(4)], axis=1)
            e1 = e1 + mm_nt(dq, wq[c])
        n, inv = norm(resid0[rows, :])
        slots[8:9, :] += jnp.sum(e1 * n, axis=0, keepdims=True)
        slots[9:10, :] += jnp.sum(e1, axis=0, keepdims=True)
        gi = dres[rows, :] + norm_back(e1 * g1, n, inv)
        resid0[rows, :] = gi
        pltpu.make_async_copy(resid0.at[rows], gin_hbm.at[rows], gins.at[b]).start()
        ds = gi.astype(BF)
        oh = (lax.broadcasted_iota(jnp.int32, (32, BLK), 0) == ids[0:1, rows]).astype(F32).astype(BF)
        cacc[0:32, :] += mm(oh, ds)
        total = jnp.sum(ds.astype(F32), axis=0, keepdims=True)
        slots[pl.ds(b, 1), :] = total
        slots[pl.ds(b + NB, 1), :] = total
        return 0

    lax.fori_loop(0, NB, embed_back, 0)
    per = slots[0:8, :]
    total = 0.5 * jnp.sum(per, axis=0, keepdims=True)
    first = lax.rem(lax.broadcasted_iota(jnp.int32, (8, 1), 0), jnp.int32(NB)) == 0
    per = jnp.where(long, jnp.where(first, total, 0.0), per)
    ct[0, 0:32, :] = jnp.where(place, jnp.concatenate([per] * 4, axis=0), 0.0).astype(BF)
    o = ROW_V - ROW_C
    cacc[o:o + 2, :] = slots[8:10, :]
    cacc[o + 2:o + 4, :] = small[1:3, :]
    cacc[o + 4:o + 5, :] = slots[10:11, :]
    cacc[o + 5:o + 6, :] = slots[11:12, :]
    cacc[o + 6:o + 7, :] = small[3:4, :]
    cacc[o + 7:o + 8, :] = small[0:1, :]
    cacc[o + 8:o + 12, :] = small[4:8, :]
    ct[0, 32:32 + TAIL, :] = cacc[...].astype(BF)
    corner.start()
    for u in last:
        reduce.stage(3, u)
    for k in range(3):
        corner.step(k)
    reduce.finish(own)
    for r in plan.ends:
        def tail():
            hints.finish(r)
            corner.finish(r)
            tg[0:256, :] = mm_tn(
                jnp.concatenate([hzt[s] for s in range(nz)], axis=0),
                jnp.concatenate([czt[s, 0:32, :] for s in range(nz)], axis=0),
            )
            rest = czt[0, 32:32 + TAIL, :].astype(F32)
            for s in range(1, nz):
                rest = rest + czt[s, 32:32 + TAIL, :].astype(F32)
            tg[256:256 + TAIL, :] = rest

        when(p.z == r, plan.early_pick(r, p.x, p.y))(tail)
    for i in plan.owners:
        @pl.when(p.here() == i)
        def _():
            at = plan.starts[i]
            a, b = max(at, ROW_T), min(at + plan.rows, ROW_C + TAIL)
            own[a - at:b - at, :] += tg[a - ROW_T:b - ROW_T, :]
    hints.drain()
    corner.drain()
    reduce.drain()
    for b in range(NB):
        rows = pl.ds(b * BLK, BLK)
        pltpu.make_async_copy(xs.at[rows], out_hbm.at[rows], outs.at[b]).wait()
        pltpu.make_async_copy(resid0.at[rows], gin_hbm.at[rows], gins.at[b]).wait()


def layer(plan, lens, ids, feat, x, cot, chunk):
    S = jax.ShapeDtypeStruct
    V = pltpu.VMEM
    DM = pltpu.SemaphoreType.DMA
    nz, n, nu, ne = plan.nz, plan.rows, len(plan.units), len(plan.ends)
    vm = pl.BlockSpec(memory_space=pltpu.VMEM)
    hb = pl.BlockSpec(memory_space=pl.ANY)

    def kernel(*refs):
        body(plan, *refs)

    return pl.pallas_call(
        kernel,
        out_shape=[S((T, D), BF), S((T, D), F32), S((n, ROW), F32)],
        in_specs=[pl.BlockSpec(memory_space=pltpu.SMEM), vm, vm, hb, hb, hb],
        out_specs=[hb, hb, vm],
        scratch_shapes=[
            V((nz, 2, 2, 2, n, ROW), BF), V((plan.padded, ROW), BF), V((4, 2048, 128), F32),
            V((3, D, D), BF), V((4, D, D), BF), V((D, D), BF), V((2048, D), BF), V((256 + TAIL, D), BF),
            V((T, D), BF), V((T, D), BF), V((T, D), F32), V((T, D), BF), V((12, T, 128), BF),
            V((PAIRS, T, 128), BF), V((8, T), F32), V((8, D), F32),
            V((4, T, D), BF), V((4, T, D), BF), V((T, D), BF), V((T, D), BF), V((T, D), BF), V((T, D), F32),
            V((PAIRS, T, 128), BF), V((12, T, 128), BF), V((2, T, 128), F32), V((16, D), F32), V((8, D), F32),
            V((TAIL, D), F32),
            V((4, 32 + TAIL, D), BF), V((3, 32 + TAIL, D), BF), V((nz, 32 + TAIL, D), BF),
            V((4, 32, 256), BF), V((3, 32, 256), BF), V((nz, 32, 256), BF), V((256 + TAIL, D), F32),
            DM((nz, 2, 2)), DM((nz, 2)), DM((nz, AG_KINDS)), DM((nz, AG_KINDS)),
            DM((nu, 2, 2)), DM((nu, 2, 2)), DM((nu, RS_KINDS)), DM((nu, RS_KINDS)), DM((nu,)), DM((PAIRS, nz)),
            DM((3,)), DM((3,)), DM((ne,)), DM((nz,)), DM((3,)), DM((3,)), DM((ne,)), DM((nz,)),
            pltpu.SemaphoreType.REGULAR, DM((3,)), DM((NB,)), DM((NB,)),
        ],
        compiler_params=pltpu.CompilerParams(
            collective_id=0, has_side_effects=True, vmem_limit_bytes=67043328
        ),
        name="layer",
    )(lens, ids, feat, x, cot, chunk)


def time_features(steps):
    half = 128
    freqs = jnp.exp(-math.log(10000.0) * jnp.arange(half, dtype=F32) / half)
    ang = steps.astype(F32).reshape(4, 1) * freqs
    f = jnp.concatenate([jnp.sin(ang), jnp.cos(ang)], axis=-1).astype(BF)
    return jnp.concatenate([f, f], axis=0)


def shards(inputs, noisy_ids, timesteps, doc_lens, cotangent, params, momentum, average):
    ndp, nfs = lax.axis_size("dp"), lax.axis_size("fsdp")
    device_count = ndp * nfs
    row_count, seq_len, model_width = inputs.shape
    plan = Plan(ndp, nfs, params.shape[0] * device_count)
    i = lax.axis_index("dp") * nfs + lax.axis_index("fsdp")
    offset = lax.rem(i * plan.share, ROW * TILE)
    chunk = lax.dynamic_update_slice(
        jnp.zeros((plan.rows * ROW,), BF), params.astype(BF), (offset,)
    ).reshape(plan.rows, ROW)
    output, input_grad, owned = layer(
        plan, doc_lens, noisy_ids, time_features(timesteps),
        inputs.reshape(T, D), cotangent.reshape(T, D), chunk,
    )
    owned_grad = lax.dynamic_slice(owned.reshape(-1), (offset,), (plan.share,))
    gradient = owned_grad * (1.0 / math.sqrt(row_count * seq_len * device_count))
    new_momentum = MOMENTUM_RATE * momentum + gradient
    new_params = params - LEARN_RATE * (gradient + MOMENTUM_RATE * new_momentum)
    new_average = AVERAGE_RATE * average + (1.0 - AVERAGE_RATE) * new_params
    return (
        output.reshape(row_count, seq_len, model_width),
        input_grad.reshape(row_count, seq_len, model_width),
        new_params,
        new_momentum,
        new_average,
        new_params.astype(BF),
    )


def solution(mesh):
    rows = ("dp", "fsdp")
    in_specs = (
        P(rows, None, None), P(rows, None), P(rows, None), P(rows, None), P(rows, None, None),
        P(rows), P(rows), P(rows),
    )
    out_specs = (P(rows, None, None), P(rows, None, None), P(rows), P(rows), P(rows), P(rows))
    return jax.shard_map(shards, mesh=mesh, in_specs=in_specs, out_specs=out_specs, check_vma=False)
```

```python
import math

import jax
import jax.numpy as jnp
from jax import lax
from jax.experimental import pallas as pl
from jax.experimental.pallas import tpu as pltpu
from jax.sharding import PartitionSpec as P

MOMENTUM_RATE = 0.9
LEARN_RATE = 0.02
AVERAGE_RATE = 0.8
EPSILON = 1e-5
MESH = pl.DeviceIdType.MESH
BF = jnp.bfloat16
F32 = jnp.float32
ROW = 512
TILE = 16
T = 1024
D = 512
BLK = 256
NB = T // BLK
PAIRS = 4
SCALE = 0.125
LOG2E = math.log2(math.e)
ROW_O, ROW_UP, ROW_DOWN, ROW_T, ROW_C, ROW_V = 1536, 2048, 4096, 6144, 6400, 6427
TAIL = 48
AG_KINDS = 13
RS_KINDS = 6
HOOKS = NB + PAIRS * NB


class Plan:
    def __init__(self, ndp, nfs, total):
        self.nx, self.ny, self.nc = 2, 2, nfs // 2
        self.nz = ndp // 2
        self.count = ndp * nfs
        self.share = total // self.count
        self.starts = [((i * self.share) // (ROW * TILE)) * TILE for i in range(self.count)]
        ends = [-(-((i + 1) * self.share) // ROW) for i in range(self.count)]
        need = max(e - s for e, s in zip(ends, self.starts))
        self.rows = max(2, -(-need // TILE)) * TILE
        self.half = -(-self.rows // (2 * TILE)) * TILE
        self.padded = max(max(self.starts) + self.rows, ROW_C + TAIL)
        layer = self.count // self.nz
        last = self.nz - 1
        self.lo = next(r for r in range(self.nz) if self.starts[r * layer] >= ROW_O)
        first = next(i for i in range(self.count) if self.starts[i] + self.rows > ROW_T)
        self.only = first >= self.count - self.nc
        self.hi = last if self.only else first // layer - 1
        self.early = list(range(self.lo)) + list(range(last if self.only else self.hi + 1, self.nz))
        self.late = list(range(self.lo, self.hi + 1))
        self.ends = [r for r in self.early if r >= self.lo]
        self.owners = [i for i in range(self.count) if self.starts[i] + self.rows > ROW_T]
        self.flat = -(-self.share // 1024) * 8
        self.slices = PAIRS if self.lo == 1 else 1
        self.units = [(r, None) for r in range(self.lo, self.nz)]
        self.body_units = len(self.units)
        for j in range(self.slices):
            self.units += [(r, None if self.slices == 1 else j) for r in range(self.lo)]

    def slice_units(self, j):
        return range(self.body_units + j * self.lo, self.body_units + (j + 1) * self.lo)

    def early_pick(self, r, cx, cy):
        if self.only and r == self.nz - 1:
            return cx * cy == 1
        return True

    def late_pick(self, r, cx, cy):
        if self.only and r == self.nz - 1:
            return cx * cy == 0
        return True


class Place:
    def __init__(self, plan):
        d = lax.axis_index("dp")
        f = lax.axis_index("fsdp")
        self.plan = plan
        two = jnp.int32(2)
        self.z, self.x = lax.div(d, two), lax.rem(d, two)
        self.y, self.c = lax.div(f, two), lax.rem(f, two)
        self.X = self.dev(x=1 - self.x)
        self.Y = self.dev(y=1 - self.y)
        self.C = self.dev(c=1 - self.c)

    def dev(self, z=None, x=None, y=None, c=None):
        z = self.z if z is None else z
        x = self.x if x is None else x
        y = self.y if y is None else y
        c = self.c if c is None else c
        return (z * 2 + x, y * 2 + c)

    def here(self):
        return ((self.z * 2 + self.x) * 2 + self.y) * 2 + self.c

    def partners(self):
        nz = self.plan.nz
        others = [self.dev(z=lax.rem(self.z + s, jnp.int32(nz))) for s in range(1, nz)]
        return [self.X, self.Y, self.C] + others

    def far(self, r):
        return jnp.abs(self.z - r)


def signal_all(place, sem):
    for dev in place.partners():
        pl.semaphore_signal(sem, inc=1, device_id=dev, device_id_type=MESH)


def wait_all(place, sem):
    pl.semaphore_wait(sem, 3 + place.plan.nz - 1)


def rcopy(src, dst, ss, rs, dev):
    return pltpu.make_async_remote_copy(
        src_ref=src, dst_ref=dst, send_sem=ss, recv_sem=rs, device_id=dev, device_id_type=MESH
    )


def when(*conds):
    real = [c for c in conds if c is not True]

    def run(f):
        if not real:
            return f()
        c = real[0]
        for other in real[1:]:
            c = c & other
        return pl.when(c)(f)

    return run


class Gather:
    def __init__(self, p, g, zs, zr, ps, pr):
        self.p, self.g, self.zs, self.zr, self.ps, self.pr = p, g, zs, zr, ps, pr
        h, n = p.plan.half, p.plan.rows
        self.parts = (pl.ds(0, h), pl.ds(h, n - h), pl.ds(0, n))

    def zcopy(self, r, j, up):
        p = self.p
        ref = self.g.at[r, p.x, p.y, p.c, self.parts[j]]
        return rcopy(ref, ref, self.zs.at[r, j, 0 if up else 1], self.zr.at[r, j], p.dev(z=p.z + 1 if up else p.z - 1))

    def cp(self, r, k):
        p = self.p
        a, b, w = self.parts
        x, y = p.x, p.y
        cx, cy, part, dev = (
            (x, y, a, p.X), (x, y, b, p.Y), (x, y, a, p.Y), (x, y, b, p.X),
            (1 - x, y, a, p.Y), (x, 1 - y, b, p.X), (x, y, w, p.C), (1 - x, y, a, p.C), (x, 1 - y, b, p.C),
            (x, 1 - y, a, p.C), (1 - x, 1 - y, a, p.C), (1 - x, y, b, p.C), (1 - x, 1 - y, b, p.C),
        )[k]
        ref = self.g.at[r, cx, cy, p.c, part]
        return rcopy(ref, ref, self.ps.at[r, k], self.pr.at[r, k], dev)

    def stage(self, s, r, pick):
        p = self.p
        z, x, y, nz = p.z, p.x, p.y, p.plan.nz
        if s == 0:
            for j in (0, 1):
                if r < nz - 1:
                    when(z == r, pick(r, x, y))(lambda: self.zcopy(r, j, True).start())
                if r > 0:
                    when(z == r, pick(r, x, y))(lambda: self.zcopy(r, j, False).start())
        if s == 1:
            for j in (0, 1):
                when(z != r, pick(r, x, y))(lambda: self.zcopy(r, j, True).wait_recv())
                if 0 < r < nz - 1 or r == 0:
                    when(z > r, z < nz - 1, pick(r, x, y))(lambda: self.zcopy(r, j, True).start())
                if r > 0:
                    when(z < r, z > 0, pick(r, x, y))(lambda: self.zcopy(r, j, False).start())
                when(pick(r, x, y))(lambda: self.cp(r, j).start())

            def rest():
                for k in (2, 3, 6):
                    self.cp(r, k).start()

            when(pick(r, x, y))(rest)
        if s == 2:
            for k, a, b, cx, cy in ((0, 4, 7, 1 - x, y), (1, 5, 8, x, 1 - y)):
                def go():
                    self.cp(r, k).wait_recv()
                    self.cp(r, a).start()
                    self.cp(r, b).start()

                when(pick(r, cx, cy))(go)
        if s == 3:
            for k, a, cx, cy in ((2, 9, x, 1 - y), (4, 10, 1 - x, 1 - y), (3, 11, 1 - x, y), (5, 12, 1 - x, 1 - y)):
                def go():
                    self.cp(r, k).wait_recv()
                    self.cp(r, a).start()

                when(pick(r, cx, cy))(go)
        if s == 4:
            for ks, cx, cy in (((6,), x, y), ((7, 11), 1 - x, y), ((8, 9), x, 1 - y), ((10, 12), 1 - x, 1 - y)):
                def go():
                    for k in ks:
                        self.cp(r, k).wait_recv()

                when(pick(r, cx, cy))(go)

    def drain(self):
        z, nz = self.p.z, self.p.plan.nz
        for r in range(nz):
            for j in (0, 1):
                if r < nz - 1:
                    when(z >= r, z < nz - 1)(lambda: self.zcopy(r, j, True).wait_send())
                if r > 0:
                    when(z <= r, z > 0)(lambda: self.zcopy(r, j, False).wait_send())
            for k in range(AG_KINDS):
                self.cp(r, k).wait_send()


class Reduce:
    def __init__(self, p, src, g, cs, cr, ps, pr, zs, zr):
        self.p, self.src, self.g = p, src, g
        self.cs, self.cr, self.ps, self.pr, self.zs, self.zr = cs, cr, ps, pr, zs, zr
        self.h, self.n = p.plan.half, p.plan.rows
        self.a, self.b, self.w = pl.ds(0, self.h), pl.ds(self.h, self.n - self.h), pl.ds(0, self.n)

    def cols(self, j):
        return pl.ds(0, ROW) if j is None else pl.ds(128 * j, 128)

    def rows(self, r, xx, yy, cc):
        plan = self.p.plan
        i = ((r * 2 + xx) * 2 + yy) * 2 + cc
        return pl.ds(pl.multiple_of(lax.div(i * plan.share, jnp.int32(ROW * TILE)) * TILE, TILE), self.n)

    def cb(self, u, xx, yy, part):
        r, j = self.p.plan.units[u]
        return self.g.at[r, xx, yy, 0, part, self.cols(j)]

    def pa(self, u, xx):
        r, j = self.p.plan.units[u]
        return self.g.at[r, 0, xx, 1, self.a, self.cols(j)]

    def pb(self, u, yy):
        r, j = self.p.plan.units[u]
        return self.g.at[r, 0, yy, 1, self.b, self.cols(j)]

    def p2(self, u, part):
        r, j = self.p.plan.units[u]
        return self.g.at[r, 1, 0, 1, part, self.cols(j)]

    def ccopy(self, u, xx, yy):
        p = self.p
        r, j = p.plan.units[u]
        return rcopy(
            self.src.at[self.rows(r, xx, yy, 1 - p.c), self.cols(j)], self.cb(u, xx, yy, self.w),
            self.cs.at[u, xx, yy], self.cr.at[u, xx, yy], p.C,
        )

    def cp(self, u, k):
        p = self.p
        x, y = p.x, p.y
        s, d, dev = (
            (self.cb(u, 0, 1 - y, self.a), self.pa(u, 0), p.Y),
            (self.cb(u, 1, 1 - y, self.a), self.pa(u, 1), p.Y),
            (self.cb(u, 1 - x, 0, self.b), self.pb(u, 0), p.X),
            (self.cb(u, 1 - x, 1, self.b), self.pb(u, 1), p.X),
            (self.pa(u, 1 - x), self.p2(u, self.a), p.X),
            (self.pb(u, 1 - y), self.p2(u, self.b), p.Y),
        )[k]
        return rcopy(s, d, self.ps.at[u, k], self.pr.at[u, k], dev)

    def zcopy(self, u):
        p = self.p
        r, j = p.plan.units[u]
        k = j or 0
        return rcopy(
            self.p2(u, self.w), self.g.at[p.z, 1, 1, 1, self.w, self.cols(j)],
            self.zs.at[u], self.zr.at[k, p.z], p.dev(z=r),
        )

    def zwait(self, j, s):
        ref = self.g.at[s, 1, 1, 1, self.w, self.cols(j)]
        rcopy(ref, ref, self.zs.at[0], self.zr.at[j or 0, s], self.p.dev(z=s)).wait_recv()

    def stage(self, s, u):
        p = self.p
        z, x, y = p.z, p.x, p.y
        r, j = p.plan.units[u]
        both = [(xx, yy) for xx in (0, 1) for yy in (0, 1)]
        if s == 0:
            for xx, yy in both:
                self.ccopy(u, xx, yy).start()
        if s == 1:
            for xx, yy in both:
                self.ccopy(u, xx, yy).wait_recv()
                ref = self.cb(u, xx, yy, self.w)
                ref[...] = ref[...] + self.src[self.rows(r, xx, yy, p.c), self.cols(j)]
            for q in (0, 1):
                self.cp(u, q).start()
                self.cp(u, 2 + q).start()
        if s == 2:
            for q in (0, 1):
                self.cp(u, q).wait_recv()
                ref = self.pa(u, q)
                ref[...] = ref[...] + self.cb(u, q, y, self.a)[...]
            self.cp(u, 4).start()
            for q in (0, 1):
                self.cp(u, 2 + q).wait_recv()
                ref = self.pb(u, q)
                ref[...] = ref[...] + self.cb(u, x, q, self.b)[...]
            self.cp(u, 5).start()
        if s == 3:
            self.cp(u, 4).wait_recv()
            ref = self.p2(u, self.a)
            ref[...] = ref[...] + self.pa(u, x)[...]
            self.cp(u, 5).wait_recv()
            ref = self.p2(u, self.b)
            ref[...] = ref[...] + self.pb(u, y)[...]
            when(z != r)(lambda: self.zcopy(u).start())

    def finish(self, out):
        z, plan = self.p.z, self.p.plan
        out[...] = self.g[z, 1, 0, 1].astype(F32)
        for s in range(plan.nz):
            def go():
                @pl.when(z >= plan.lo)
                def _():
                    self.zwait(None, s)

                @pl.when(z < plan.lo)
                def _():
                    for j in range(plan.slices):
                        self.zwait(None if plan.slices == 1 else j, s)

                out[...] += self.g[s, 1, 1, 1].astype(F32)

            when(z != s)(go)

    def drain(self):
        for u, (r, _) in enumerate(self.p.plan.units):
            for xx in (0, 1):
                for yy in (0, 1):
                    self.ccopy(u, xx, yy).wait_send()
            for k in range(RS_KINDS):
                self.cp(u, k).wait_send()
            when(self.p.z != r)(lambda: self.zcopy(u).wait_send())


class Corner:
    def __init__(self, p, t, rx, zt, ss, rs, zs, zr):
        self.p, self.t, self.rx, self.zt = p, t, rx, zt
        self.ss, self.rs, self.zs, self.zr = ss, rs, zs, zr

    def copy(self, k):
        p = self.p
        return rcopy(self.t.at[k], self.rx.at[k], self.ss.at[k], self.rs.at[k], (p.C, p.Y, p.X)[k])

    def zcopy(self, m):
        p = self.p
        return rcopy(
            self.t.at[3], self.zt.at[p.z], self.zs.at[m], self.zr.at[p.z], p.dev(z=p.plan.ends[m])
        )

    def senders(self, m):
        p = self.p
        return when(p.z != p.plan.ends[m], p.plan.early_pick(p.plan.ends[m], p.x, p.y))

    def start(self):
        self.copy(0).start()

    def step(self, k):
        self.copy(k).wait_recv()
        self.t[k + 1] = self.t[k] + self.rx[k]
        if k < 2:
            self.copy(k + 1).start()
        else:
            for m in range(len(self.p.plan.ends)):
                self.senders(m)(lambda: self.zcopy(m).start())

    def finish(self, r):
        p = self.p
        self.zt[r] = self.t[3]
        for s in range(p.plan.nz):
            if s != r:
                ref = self.zt.at[s]
                rcopy(ref, ref, self.zs.at[0], self.zr.at[s], p.dev(z=s)).wait_recv()

    def drain(self):
        for k in range(3):
            self.copy(k).wait_send()
        for m in range(len(self.p.plan.ends)):
            self.senders(m)(lambda: self.zcopy(m).wait_send())


def assemble(plan, g, lo, hi, store):
    for i in range(plan.count):
        at = lambda k: (k // 8, (k // 4) % 2, (k // 2) % 2, k % 2)
        s = plan.starts[i]
        e = plan.starts[i + 1] if i + 1 < plan.count else plan.padded
        if lo <= s < hi:
            head = g[at(i) + (slice(0, TILE),)]
            if i and s - plan.starts[i - 1] < plan.rows:
                d = s - plan.starts[i - 1]
                head = head + g[at(i - 1) + (slice(d, d + TILE),)]
            store(s, s + TILE, head)
        a, b = max(s + TILE, lo), min(e, hi, s + plan.rows)
        if b > a:
            store(a, b, g[at(i) + (slice(a - s, b - s),)])


class Shift:
    def __init__(self, plan, p):
        self.p, self.n, self.flat = p, plan.rows, plan.flat
        at = lax.rem(p.here() * plan.share, jnp.int32(ROW * TILE))
        self.q, self.s = lax.div(at, jnp.int32(128)), lax.rem(at, jnp.int32(128))
        self.high = lax.broadcasted_iota(jnp.int32, (1, 128), 1) >= self.s

    def load(self, wf, g):
        p, n, f = self.p, self.n, self.flat
        wf[0, 0:72, :] = jnp.zeros((72, 128), F32)
        wf[0, 72:72 + f, :] = pltpu.roll(wf[1, 0:f, :], self.s, 1)
        if 4 * n > f:
            wf[0, 72 + f:72 + 4 * n, :] = jnp.zeros((4 * n - f, 128), F32)
        a = wf[0, pl.ds(72 - self.q, 4 * n), :]
        b = wf[0, pl.ds(71 - self.q, 4 * n), :]
        wf[2, 0:4 * n, :] = jnp.where(self.high, a, b)
        for j in range(4):
            g[p.z, p.x, p.y, p.c, :, lanes(j)] = wf[2, pl.ds(j, n, stride=4), :].astype(BF)

    def store(self, wf, own, out):
        n, f = self.n, self.flat
        for j in range(4):
            wf[0, pl.ds(j, n, stride=4), :] = own[:, lanes(j)]
        wf[0, 4 * n:4 * n + 16, :] = jnp.zeros((16, 128), F32)
        a = wf[0, pl.ds(self.q, f), :]
        b = wf[0, pl.ds(self.q + 1, f), :]
        out[...] = pltpu.roll(jnp.where(self.high, a, b), lax.rem(128 - self.s, jnp.int32(128)), 1)


def mm(a, b):
    return lax.dot_general(a, b, (((1,), (0,)), ((), ())), preferred_element_type=F32)


def mm_nt(a, b):
    return lax.dot_general(a, b, (((1,), (1,)), ((), ())), preferred_element_type=F32)


def mm_tn(a, b):
    return lax.dot_general(a, b, (((0,), (0,)), ((), ())), preferred_element_type=F32)


def norm(h):
    mean = jnp.mean(h, axis=-1, keepdims=True)
    cen = h - mean
    inv = lax.rsqrt(jnp.mean(cen * cen, axis=-1, keepdims=True) + EPSILON)
    return cen * inv, inv


def norm_back(dn, n, inv):
    return (dn - jnp.mean(dn, axis=-1, keepdims=True) - n * jnp.mean(dn * n, axis=-1, keepdims=True)) * inv


def valid_len(lens, b):
    long = lens[0, 1] == 0
    short = lens[0, 0]
    for k in range(1, NB):
        short = jnp.where(b == k, lens[0, k], short)
    return jnp.where(long, lens[0, 0] - b * BLK, short)


def lane_half(par):
    lane = lax.broadcasted_iota(jnp.int32, (1, 128), 1)
    return (lane >= 64) if par else (lane < 64)


def key_bias(lens, qb):
    long = lens[0, 1] == 0
    cols = []
    it = lax.broadcasted_iota(jnp.int32, (BLK, 1), 0)
    for kb in range(NB):
        thr = jnp.where(long | (qb == kb), valid_len(lens, kb), 0)
        cols.append(jnp.where(it < thr, 0.0, -1e30).astype(F32))
    return jnp.concatenate(cols, axis=0)


def lanes(j):
    return slice(128 * j, 128 * j + 128)


def spread(wf, base):
    def store(a, b, val):
        for j in range(4):
            wf[j, a - base:b - base, :] = val[:, lanes(j)].astype(F32)
    return store


def regroup(wf, n, to):
    for c in range(n):
        for j in range(4):
            to[c, :, lanes(j)] = wf[j, pl.ds(c, 512, stride=n), :].astype(BF)


def put(wf, c, n, val):
    for j in range(4):
        wf[j, pl.ds(c, 512, stride=n), :] = val[:, lanes(j)]


def take(wf, n, out, base):
    for j in range(4):
        out[base:base + 512 * n, lanes(j)] = wf[j, 0:512 * n, :].astype(BF)


def phi_parts(v):
    cdf = 0.5 * (1.0 + lax.erf(v * (2.0 ** -0.5)))
    pdf = jnp.exp(v * v * -0.5) * (1.0 / math.sqrt(2.0 * math.pi))
    return cdf, pdf


def block_rows(b):
    return pl.ds(pl.multiple_of(b * BLK, BLK), BLK)


def body(plan, lens, ids, feat, x_hbm, cot_hbm, chunk_hbm, out_hbm, gin_hbm, own_flat,
         g, src, wf, wq, wu, wo, wd, vec, xs, cs, resid0, attn_in, qkv, attended, lse, ft,
         act, dpre, fin, dff, dbr, dres, datt, dqkv, accv, slots, small, cacc,
         ct, crx, czt, ht, hrx, hzt, tg, own,
         zs, zr, ps, pr, rcs, rcr, rps, rpr, rzs, rzr,
         css, crs, czs, czr, hss, hrs, hzs, hzr, ready, ins, outs, gins):
    p = Place(plan)
    nz = plan.nz
    corner = Corner(p, ct, crx, czt, css, crs, czs, czr)
    hints = Corner(p, ht, hrx, hzt, hss, hrs, hzs, hzr)
    place = lax.div(lax.broadcasted_iota(jnp.int32, (32, 1), 0), jnp.int32(4)) == (p.x * 2 + p.y) * 2 + p.c
    gather = Gather(p, g, zs, zr, ps, pr)
    loads = [
        pltpu.make_async_copy(chunk_hbm, wf.at[1, pl.ds(0, plan.flat)], ins.at[0]),
        pltpu.make_async_copy(x_hbm, xs, ins.at[1]),
        pltpu.make_async_copy(cot_hbm, cs, ins.at[2]),
    ]
    for cpy in loads:
        cpy.start()
    bar = pltpu.get_barrier_semaphore()
    signal_all(p, bar)
    shift = Shift(plan, p)
    loads[0].wait()
    shift.load(wf, g)
    wait_all(p, bar)

    for r in plan.early:
        gather.stage(0, r, plan.early_pick)
    for t in range(nz + 3):
        for s in (4, 3, 2, 1):
            for r in plan.early:
                if 0 <= t - (s - 1) < nz:
                    when(p.far(r) == t - (s - 1))(lambda: gather.stage(s, r, plan.early_pick))
    for r in plan.late:
        gather.stage(0, r, plan.late_pick)
    ht[0] = jnp.where(place, jnp.concatenate([feat[...].astype(F32)] * 4, axis=0), 0.0).astype(BF)
    hints.start()

    def gather_hook(i):
        for s in (1, 2, 3, 4):
            for r in plan.late:
                start = lax.div(9 * p.far(r) + 2, jnp.int32(2)) + (0, 0, 3, 6, 7)[s]
                when(i == jnp.minimum(start, HOOKS))(lambda: gather.stage(s, r, plan.late_pick))

    assemble(plan, g, 0, ROW_O, spread(wf, 0))
    regroup(wf, 3, wq)

    def tail_store(a, b, val):
        vec[a - ROW_T:b - ROW_T, :] = val

    assemble(plan, g, ROW_T, ROW_C + TAIL, tail_store)
    ctab = vec[256:288, :]
    vecs = vec[272:304, :].astype(F32)
    v0 = ROW_V - ROW_C - 16
    g1, b1, g2, b2, bq, bv, bo, bd = (vecs[v0 + k:v0 + k + 1] for k in range(8))
    ft[...] = mm(feat[...], vec[0:256, :])
    long = lens[0, 1] == 0
    loads[1].wait()

    def embed(b, _):
        gather_hook(b)
        rows = block_rows(b)
        oh = (lax.broadcasted_iota(jnp.int32, (32, BLK), 0) == ids[0:1, rows]).astype(F32).astype(BF)
        side = mm_tn(oh, ctab)
        slot = jnp.where(long, 0, b)
        h = xs[rows, :].astype(F32) + (side + ft[pl.ds(slot, 1), :])
        resid0[rows, :] = h
        n, _i = norm(h)
        a = (n * g1 + b1).astype(BF)
        attn_in[rows, :] = a
        for c in range(3):
            pr_ = mm(a, wq[c])
            if c == 0:
                pr_ = (pr_ + bq) * (SCALE * LOG2E)
            if c == 2:
                pr_ = pr_ + bv
            pr_ = pr_.astype(BF)
            for j in range(4):
                qkv[4 * c + j, rows, :] = pr_[:, lanes(j)]
        return 0

    lax.fori_loop(0, NB, embed, 0)
    ones = jnp.ones((T, 128), BF)

    def attend(i, _):
        gather_hook(i + NB)
        pair, qb = lax.div(i, NB), lax.rem(i, NB)
        rows = block_rows(qb)
        q = qkv[pair, rows, :]
        k = qkv[PAIRS + pair]
        va = jnp.concatenate([qkv[2 * PAIRS + pair], ones], axis=1)
        bias = key_bias(lens, qb)
        heads = []
        for par in (0, 1):
            qm = jnp.where(lane_half(par), q, jnp.zeros_like(q))
            s = mm_nt(k, qm) + bias
            m = jnp.max(s, axis=0, keepdims=True)
            e = jnp.exp2(s - m)
            l = jnp.sum(e, axis=0, keepdims=True)
            lse[pl.ds(2 * pair + par, 1), rows] = m + jnp.log(l) * LOG2E
            oa = mm_tn(e.astype(BF), va)
            heads.append(oa[:, :128] / oa[:, 128:])
        attended[pair, rows, :] = jnp.where(lane_half(0), heads[0], heads[1]).astype(BF)
        return 0

    lax.fori_loop(0, PAIRS * NB, attend, 0)
    gather_hook(HOOKS)

    def wo_store(a, b, val):
        wo[a - ROW_O:b - ROW_O, :] = val

    def wd_store(a, b, val):
        wd[a - ROW_DOWN:b - ROW_DOWN, :] = val

    assemble(plan, g, ROW_O, ROW_UP, wo_store)
    assemble(plan, g, ROW_UP, ROW_DOWN, spread(wf, ROW_UP))
    assemble(plan, g, ROW_DOWN, ROW_T, wd_store)
    regroup(wf, 4, wu)
    hints.step(0)
    gather.drain()
    signal_all(p, ready)
    small[...] = jnp.zeros_like(small)
    loads[2].wait()

    def feed(b, _):
        rows = block_rows(b)
        att = jnp.concatenate([attended[j, rows, :] for j in range(PAIRS)], axis=1)
        h = resid0[rows, :] + (mm(att, wo[...]) + bo)
        n, inv = norm(h)
        f = (n * g2 + b2).astype(BF)
        fin[rows, :] = f
        ok = lax.broadcasted_iota(jnp.int32, (BLK, 1), 0) < valid_len(lens, b)
        do = jnp.where(ok, cs[rows, :].astype(F32), 0.0)
        d = do.astype(BF)
        dff[rows, :] = d
        small[0:1, :] += jnp.sum(do, axis=0, keepdims=True)
        acc = h + bd
        e2 = jnp.zeros((BLK, D), F32)
        for c in range(4):
            pre = mm(f, wu[c]) + vecs[v0 + 8 + c:v0 + 9 + c]
            cdf, pdf = phi_parts(pre)
            a = (pre * cdf).astype(BF)
            wdc = wd[512 * c:512 * c + 512, :]
            dp = (mm_nt(d, wdc) * (cdf + pre * pdf)).astype(BF)
            act[c, rows, :] = a
            dpre[c, rows, :] = dp
            small[4 + c:5 + c, :] += jnp.sum(dp.astype(F32), axis=0, keepdims=True)
            acc = acc + mm(a, wdc)
            e2 = e2 + mm_nt(dp, wu[c])
        xs[rows, :] = acc.astype(BF)
        pltpu.make_async_copy(xs.at[rows], out_hbm.at[0, rows], outs.at[b]).start()
        small[1:2, :] += jnp.sum(e2 * n, axis=0, keepdims=True)
        small[2:3, :] += jnp.sum(e2, axis=0, keepdims=True)
        dr = do + norm_back(e2 * g2, n, inv)
        dres[rows, :] = dr
        db = dr.astype(BF)
        dbr[rows, :] = db
        small[3:4, :] += jnp.sum(db.astype(F32), axis=0, keepdims=True)
        da = mm_nt(db, wo[...]).astype(BF)
        for j in range(PAIRS):
            datt[j, rows, :] = da[:, lanes(j)]
        return 0

    lax.fori_loop(0, NB, feed, 0)
    hints.step(1)
    src[ROW_T:plan.padded, :] = jnp.zeros((plan.padded - ROW_T, ROW), BF)
    for c in range(4):
        src[ROW_DOWN + 512 * c:ROW_DOWN + 512 * c + 512, :] = mm_tn(act[c], dff[...]).astype(BF)
        put(wf, c, 4, mm_tn(fin[...], dpre[c]))
    take(wf, 4, src, ROW_UP)
    for j in range(PAIRS):
        src[ROW_O + 128 * j:ROW_O + 128 * j + 128, :] = mm_tn(attended[j], dbr[...]).astype(BF)

    reduce = Reduce(p, src, g, rcs, rcr, rps, rpr, rzs, rzr)
    hints.step(2)
    wait_all(p, ready)
    for u in range(plan.body_units):
        reduce.stage(0, u)

    def qkv_grad(j):
        dq = jnp.concatenate([dqkv[4 * c + j] for c in range(3)], axis=1)
        gq = mm_tn(attn_in[...], dq)
        for c in range(3):
            wf[j, pl.ds(c, 512, stride=3), :] = gq[:, lanes(c)]
        src[0:ROW_O, lanes(j)] = wf[j, 0:ROW_O, :].astype(BF)
        for c in (0, 2):
            slots[10 + c // 2:11 + c // 2, lanes(j)] = jnp.sum(dqkv[4 * c + j].astype(F32), axis=0, keepdims=True)

    def slice_start(j):
        qkv_grad(j)
        if plan.slices > 1:
            for u in plan.slice_units(j):
                reduce.stage(0, u)

    def reduce_at(s, u):
        return lambda: reduce.stage(s, u)

    steps = []
    for k in range(plan.body_units):
        for s, at in ((1, 1 + 3 * k), (2, 4 + 3 * k), (3, 6 + 3 * k)):
            steps.append((at, -s, reduce_at(s, k)))
    for j in range(PAIRS - 1):
        steps.append((NB * (j + 1), 0, lambda j=j: slice_start(j)))
        if plan.slices > 1:
            for s, at in ((1, (10, 11, 14)[j]), (2, (12, 13, 15)[j]), (3, (14, 15, 16)[j])):
                for u in plan.slice_units(j):
                    steps.append((at, -s, reduce_at(s, u)))
    steps.sort(key=lambda e: e[:2])

    def reduce_hook(i):
        for at, _, run in steps:
            if at < PAIRS * NB:
                pl.when(i == at)(run)

    head = lax.broadcasted_iota(jnp.int32, (8, 128), 1) // 64
    both = jnp.where(head == lax.broadcasted_iota(jnp.int32, (8, 128), 0), 1.0, 0.0).astype(BF)

    def attend_back(i, _):
        reduce_hook(i)
        pair, qb = lax.div(i, NB), lax.rem(i, NB)
        rows = block_rows(qb)
        q = qkv[pair, rows, :]
        k = qkv[PAIRS + pair]
        v = qkv[2 * PAIRS + pair]
        do = datt[pair, rows, :]
        bias = key_bias(lens, qb)
        prod = attended[pair, rows, :].astype(F32) * do.astype(F32)
        high = prod.astype(BF)
        delta = mm_nt(both, high) + mm_nt(both, (prod - high.astype(F32)).astype(BF))
        dqs = []

        @pl.when(qb == 0)
        def _():
            accv[...] = jnp.zeros_like(accv)

        for par in (0, 1):
            half = lane_half(par)
            qm = jnp.where(half, q, jnp.zeros_like(q))
            dm = jnp.where(half, do, jnp.zeros_like(do))
            pp = jnp.exp2(mm_nt(k, qm) + bias - lse[pl.ds(2 * pair + par, 1), rows])
            dp = mm_nt(v, dm)
            ds = (pp * (dp - delta[par:par + 1])).astype(BF)
            accv[1] += mm(pp.astype(BF), dm)
            accv[0] += mm(ds, qm)
            dqs.append(mm_tn(ds, k))
        dqkv[pair, rows, :] = (jnp.where(lane_half(0), dqs[0], dqs[1]) * SCALE).astype(BF)

        @pl.when(qb == NB - 1)
        def _():
            dqkv[PAIRS + pair] = (accv[0] * (1.0 / LOG2E)).astype(BF)
            dqkv[2 * PAIRS + pair] = accv[1].astype(BF)
        return 0

    lax.fori_loop(0, PAIRS * NB, attend_back, 0)
    slice_start(PAIRS - 1)
    last = plan.slice_units(plan.slices - 1)
    if plan.slices == 1:
        for u in last:
            reduce.stage(0, u)
    for at, _, run in steps:
        if at >= PAIRS * NB:
            run()
    slots[0:10, :] = jnp.zeros((10, D), F32)
    cacc[...] = jnp.zeros_like(cacc)

    def embed_back(b, _):
        rows = block_rows(b)

        @pl.when(b == 1)
        def _():
            for u in last:
                reduce.stage(1, u)

        @pl.when(b == 3)
        def _():
            for u in last:
                reduce.stage(2, u)

        e1 = jnp.zeros((BLK, D), F32)
        for c in range(3):
            dq = jnp.concatenate([dqkv[4 * c + j, rows, :] for j in range(4)], axis=1)
            e1 = e1 + mm_nt(dq, wq[c])
        n, inv = norm(resid0[rows, :])
        slots[8:9, :] += jnp.sum(e1 * n, axis=0, keepdims=True)
        slots[9:10, :] += jnp.sum(e1, axis=0, keepdims=True)
        gi = dres[rows, :] + norm_back(e1 * g1, n, inv)
        resid0[rows, :] = gi
        pltpu.make_async_copy(resid0.at[rows], gin_hbm.at[0, rows], gins.at[b]).start()
        ds = gi.astype(BF)
        oh = (lax.broadcasted_iota(jnp.int32, (32, BLK), 0) == ids[0:1, rows]).astype(F32).astype(BF)
        cacc[0:32, :] += mm(oh, ds)
        total = jnp.sum(ds.astype(F32), axis=0, keepdims=True)
        slots[pl.ds(b, 1), :] = total
        slots[pl.ds(b + NB, 1), :] = total
        return 0

    lax.fori_loop(0, NB, embed_back, 0)
    per = slots[0:8, :]
    total = 0.5 * jnp.sum(per, axis=0, keepdims=True)
    first = lax.rem(lax.broadcasted_iota(jnp.int32, (8, 1), 0), jnp.int32(NB)) == 0
    per = jnp.where(long, jnp.where(first, total, 0.0), per)
    ct[0, 0:32, :] = jnp.where(place, jnp.concatenate([per] * 4, axis=0), 0.0).astype(BF)
    o = ROW_V - ROW_C
    cacc[o:o + 2, :] = slots[8:10, :]
    cacc[o + 2:o + 4, :] = small[1:3, :]
    cacc[o + 4:o + 5, :] = slots[10:11, :]
    cacc[o + 5:o + 6, :] = slots[11:12, :]
    cacc[o + 6:o + 7, :] = small[3:4, :]
    cacc[o + 7:o + 8, :] = small[0:1, :]
    cacc[o + 8:o + 12, :] = small[4:8, :]
    ct[0, 32:32 + TAIL, :] = cacc[...].astype(BF)
    corner.start()
    for u in last:
        reduce.stage(3, u)
    for k in range(3):
        corner.step(k)
    reduce.finish(own)
    for r in plan.ends:
        def tail():
            hints.finish(r)
            corner.finish(r)
            tg[0:256, :] = mm_tn(
                jnp.concatenate([hzt[s] for s in range(nz)], axis=0),
                jnp.concatenate([czt[s, 0:32, :] for s in range(nz)], axis=0),
            )
            rest = czt[0, 32:32 + TAIL, :].astype(F32)
            for s in range(1, nz):
                rest = rest + czt[s, 32:32 + TAIL, :].astype(F32)
            tg[256:256 + TAIL, :] = rest

        when(p.z == r, plan.early_pick(r, p.x, p.y))(tail)
    for i in plan.owners:
        @pl.when(p.here() == i)
        def _():
            at = plan.starts[i]
            a, b = max(at, ROW_T), min(at + plan.rows, ROW_C + TAIL)
            own[a - at:b - at, :] += tg[a - ROW_T:b - ROW_T, :]
    shift.store(wf, own, own_flat)
    hints.drain()
    corner.drain()
    reduce.drain()
    for b in range(NB):
        rows = pl.ds(b * BLK, BLK)
        pltpu.make_async_copy(xs.at[rows], out_hbm.at[0, rows], outs.at[b]).wait()
        pltpu.make_async_copy(resid0.at[rows], gin_hbm.at[0, rows], gins.at[b]).wait()


def layer(plan, lens, ids, feat, x, cot, chunk):
    S = jax.ShapeDtypeStruct
    V = pltpu.VMEM
    DM = pltpu.SemaphoreType.DMA
    nz, n, nu, ne = plan.nz, plan.rows, len(plan.units), len(plan.ends)
    vm = pl.BlockSpec(memory_space=pltpu.VMEM)
    hb = pl.BlockSpec(memory_space=pl.ANY)

    def kernel(*refs):
        body(plan, *refs)

    return pl.pallas_call(
        kernel,
        out_shape=[S((1, T, D), BF), S((1, T, D), F32), S((plan.flat, 128), F32)],
        in_specs=[pl.BlockSpec(memory_space=pltpu.SMEM), vm, vm, hb, hb, hb],
        out_specs=[hb, hb, vm],
        scratch_shapes=[
            V((nz, 2, 2, 2, n, ROW), BF), V((plan.padded, ROW), BF), V((4, 2048, 128), F32),
            V((3, D, D), BF), V((4, D, D), BF), V((D, D), BF), V((2048, D), BF), V((256 + TAIL, D), BF),
            V((T, D), BF), V((T, D), BF), V((T, D), F32), V((T, D), BF), V((12, T, 128), BF),
            V((PAIRS, T, 128), BF), V((8, T), F32), V((8, D), F32),
            V((4, T, D), BF), V((4, T, D), BF), V((T, D), BF), V((T, D), BF), V((T, D), BF), V((T, D), F32),
            V((PAIRS, T, 128), BF), V((12, T, 128), BF), V((2, T, 128), F32), V((16, D), F32), V((8, D), F32),
            V((TAIL, D), F32),
            V((4, 32 + TAIL, D), BF), V((3, 32 + TAIL, D), BF), V((nz, 32 + TAIL, D), BF),
            V((4, 32, 256), BF), V((3, 32, 256), BF), V((nz, 32, 256), BF), V((256 + TAIL, D), F32), V((n, ROW), F32),
            DM((nz, 2, 2)), DM((nz, 2)), DM((nz, AG_KINDS)), DM((nz, AG_KINDS)),
            DM((nu, 2, 2)), DM((nu, 2, 2)), DM((nu, RS_KINDS)), DM((nu, RS_KINDS)), DM((nu,)), DM((PAIRS, nz)),
            DM((3,)), DM((3,)), DM((ne,)), DM((nz,)), DM((3,)), DM((3,)), DM((ne,)), DM((nz,)),
            pltpu.SemaphoreType.REGULAR, DM((3,)), DM((NB,)), DM((NB,)),
        ],
        compiler_params=pltpu.CompilerParams(
            collective_id=0, has_side_effects=True, vmem_limit_bytes=67043328
        ),
        name="layer",
    )(lens, ids, feat, x, cot, chunk)


def time_features(steps):
    half = 128
    freqs = jnp.exp(-math.log(10000.0) * jnp.arange(half, dtype=F32) / half)
    ang = steps.astype(F32).reshape(4, 1) * freqs
    f = jnp.concatenate([jnp.sin(ang), jnp.cos(ang)], axis=-1).astype(BF)
    return jnp.concatenate([f, f], axis=0)


def shards(inputs, noisy_ids, timesteps, doc_lens, cotangent, params, momentum, average):
    ndp, nfs = lax.axis_size("dp"), lax.axis_size("fsdp")
    device_count = ndp * nfs
    row_count, seq_len, model_width = inputs.shape
    plan = Plan(ndp, nfs, params.shape[0] * device_count)
    chunk = jnp.pad(params, (0, plan.flat * 128 - plan.share)).reshape(plan.flat, 128)
    output, input_grad, owned = layer(
        plan, doc_lens, noisy_ids, time_features(timesteps),
        inputs.reshape(T, D), cotangent.reshape(T, D), chunk,
    )
    owned_grad = owned.reshape(-1)[:plan.share]
    gradient = owned_grad * (1.0 / math.sqrt(row_count * seq_len * device_count))
    new_momentum = MOMENTUM_RATE * momentum + gradient
    new_params = params - LEARN_RATE * (gradient + MOMENTUM_RATE * new_momentum)
    new_average = AVERAGE_RATE * average + (1.0 - AVERAGE_RATE) * new_params
    return (
        output,
        input_grad,
        new_params,
        new_momentum,
        new_average,
        new_params.astype(BF),
    )


def solution(mesh):
    rows = ("dp", "fsdp")
    in_specs = (
        P(rows, None, None), P(rows, None), P(rows, None), P(rows, None), P(rows, None, None),
        P(rows), P(rows), P(rows),
    )
    out_specs = (P(rows, None, None), P(rows, None, None), P(rows), P(rows), P(rows), P(rows))
    return jax.shard_map(shards, mesh=mesh, in_specs=in_specs, out_specs=out_specs, check_vma=False)
```

```python
import math

import jax
import jax.numpy as jnp
from jax import lax
from jax.experimental import pallas as pl
from jax.experimental.pallas import tpu as pltpu
from jax.sharding import PartitionSpec as P

MOMENTUM_RATE = 0.9
LEARN_RATE = 0.02
AVERAGE_RATE = 0.8
EPSILON = 1e-5
MESH = pl.DeviceIdType.MESH
BF = jnp.bfloat16
F32 = jnp.float32
ROW = 512
TILE = 16
T = 1024
D = 512
BLK = 256
NB = T // BLK
PAIRS = 4
SCALE = 0.125
LOG2E = math.log2(math.e)
ROW_O, ROW_UP, ROW_DOWN, ROW_T, ROW_C, ROW_V = 1536, 2048, 4096, 6144, 6400, 6427
TAIL = 48
AG_KINDS = 13
RS_KINDS = 6
HOOKS = NB + PAIRS * NB


class Plan:
    def __init__(self, ndp, nfs, total):
        self.nx, self.ny, self.nc = 2, 2, nfs // 2
        self.nz = ndp // 2
        self.count = ndp * nfs
        self.share = total // self.count
        self.starts = [((i * self.share) // (ROW * TILE)) * TILE for i in range(self.count)]
        ends = [-(-((i + 1) * self.share) // ROW) for i in range(self.count)]
        need = max(e - s for e, s in zip(ends, self.starts))
        self.rows = max(2, -(-need // TILE)) * TILE
        self.half = -(-self.rows // (2 * TILE)) * TILE
        self.padded = max(max(self.starts) + self.rows, ROW_C + TAIL)
        layer = self.count // self.nz
        last = self.nz - 1
        self.lo = next(r for r in range(self.nz) if self.starts[r * layer] >= ROW_O)
        first = next(i for i in range(self.count) if self.starts[i] + self.rows > ROW_T)
        self.only = first >= self.count - self.nc
        self.hi = last if self.only else first // layer - 1
        self.early = list(range(self.lo)) + list(range(last if self.only else self.hi + 1, self.nz))
        self.late = list(range(self.lo, self.hi + 1))
        self.ends = [r for r in self.early if r >= self.lo]
        self.owners = [i for i in range(self.count) if self.starts[i] + self.rows > ROW_T]
        self.flat = -(-self.share // 1024) * 8
        self.slices = PAIRS if self.lo == 1 else 1
        self.units = [(r, None) for r in range(self.lo, self.nz)]
        self.body_units = len(self.units)
        for j in range(self.slices):
            self.units += [(r, None if self.slices == 1 else j) for r in range(self.lo)]

    def slice_units(self, j):
        return range(self.body_units + j * self.lo, self.body_units + (j + 1) * self.lo)

    def early_pick(self, r, cx, cy):
        if self.only and r == self.nz - 1:
            return cx * cy == 1
        return True

    def late_pick(self, r, cx, cy):
        if self.only and r == self.nz - 1:
            return cx * cy == 0
        return True


class Place:
    def __init__(self, plan):
        d = lax.axis_index("dp")
        f = lax.axis_index("fsdp")
        self.plan = plan
        two = jnp.int32(2)
        self.z, self.x = lax.div(d, two), lax.rem(d, two)
        self.y, self.c = lax.div(f, two), lax.rem(f, two)
        self.X = self.dev(x=1 - self.x)
        self.Y = self.dev(y=1 - self.y)
        self.C = self.dev(c=1 - self.c)

    def dev(self, z=None, x=None, y=None, c=None):
        z = self.z if z is None else z
        x = self.x if x is None else x
        y = self.y if y is None else y
        c = self.c if c is None else c
        return (z * 2 + x, y * 2 + c)

    def here(self):
        return ((self.z * 2 + self.x) * 2 + self.y) * 2 + self.c

    def partners(self):
        nz = self.plan.nz
        others = [self.dev(z=lax.rem(self.z + s, jnp.int32(nz))) for s in range(1, nz)]
        return [self.X, self.Y, self.C] + others

    def far(self, r):
        return jnp.abs(self.z - r)


def signal_all(place, sem):
    for dev in place.partners():
        pl.semaphore_signal(sem, inc=1, device_id=dev, device_id_type=MESH)


def wait_all(place, sem):
    pl.semaphore_wait(sem, 3 + place.plan.nz - 1)


def rcopy(src, dst, ss, rs, dev):
    return pltpu.make_async_remote_copy(
        src_ref=src, dst_ref=dst, send_sem=ss, recv_sem=rs, device_id=dev, device_id_type=MESH
    )


def when(*conds):
    real = [c for c in conds if c is not True]

    def run(f):
        if not real:
            return f()
        c = real[0]
        for other in real[1:]:
            c = c & other
        return pl.when(c)(f)

    return run


class Gather:
    def __init__(self, p, g, zs, zr, ps, pr):
        self.p, self.g, self.zs, self.zr, self.ps, self.pr = p, g, zs, zr, ps, pr
        h, n = p.plan.half, p.plan.rows
        self.parts = (pl.ds(0, h), pl.ds(h, n - h), pl.ds(0, n))

    def zcopy(self, r, j, up):
        p = self.p
        ref = self.g.at[r, p.x, p.y, p.c, self.parts[j]]
        return rcopy(ref, ref, self.zs.at[r, j, 0 if up else 1], self.zr.at[r, j], p.dev(z=p.z + 1 if up else p.z - 1))

    def cp(self, r, k):
        p = self.p
        a, b, w = self.parts
        x, y = p.x, p.y
        cx, cy, part, dev = (
            (x, y, a, p.X), (x, y, b, p.Y), (x, y, a, p.Y), (x, y, b, p.X),
            (1 - x, y, a, p.Y), (x, 1 - y, b, p.X), (x, y, w, p.C), (1 - x, y, a, p.C), (x, 1 - y, b, p.C),
            (x, 1 - y, a, p.C), (1 - x, 1 - y, a, p.C), (1 - x, y, b, p.C), (1 - x, 1 - y, b, p.C),
        )[k]
        ref = self.g.at[r, cx, cy, p.c, part]
        return rcopy(ref, ref, self.ps.at[r, k], self.pr.at[r, k], dev)

    def stage(self, s, r, pick):
        p = self.p
        z, x, y, nz = p.z, p.x, p.y, p.plan.nz
        if s == 0:
            for j in (0, 1):
                if r < nz - 1:
                    when(z == r, pick(r, x, y))(lambda: self.zcopy(r, j, True).start())
                if r > 0:
                    when(z == r, pick(r, x, y))(lambda: self.zcopy(r, j, False).start())
        if s == 1:
            for j in (0, 1):
                when(z != r, pick(r, x, y))(lambda: self.zcopy(r, j, True).wait_recv())
                if 0 < r < nz - 1 or r == 0:
                    when(z > r, z < nz - 1, pick(r, x, y))(lambda: self.zcopy(r, j, True).start())
                if r > 0:
                    when(z < r, z > 0, pick(r, x, y))(lambda: self.zcopy(r, j, False).start())
                when(pick(r, x, y))(lambda: self.cp(r, j).start())

            def rest():
                for k in (2, 3, 6):
                    self.cp(r, k).start()

            when(pick(r, x, y))(rest)
        if s == 2:
            for k, a, b, cx, cy in ((0, 4, 7, 1 - x, y), (1, 5, 8, x, 1 - y)):
                def go():
                    self.cp(r, k).wait_recv()
                    self.cp(r, a).start()
                    self.cp(r, b).start()

                when(pick(r, cx, cy))(go)
        if s == 3:
            for k, a, cx, cy in ((2, 9, x, 1 - y), (4, 10, 1 - x, 1 - y), (3, 11, 1 - x, y), (5, 12, 1 - x, 1 - y)):
                def go():
                    self.cp(r, k).wait_recv()
                    self.cp(r, a).start()

                when(pick(r, cx, cy))(go)
        if s == 4:
            for ks, cx, cy in (((6,), x, y), ((7, 11), 1 - x, y), ((8, 9), x, 1 - y), ((10, 12), 1 - x, 1 - y)):
                def go():
                    for k in ks:
                        self.cp(r, k).wait_recv()

                when(pick(r, cx, cy))(go)

    def drain(self):
        z, nz = self.p.z, self.p.plan.nz
        for r in range(nz):
            for j in (0, 1):
                if r < nz - 1:
                    when(z >= r, z < nz - 1)(lambda: self.zcopy(r, j, True).wait_send())
                if r > 0:
                    when(z <= r, z > 0)(lambda: self.zcopy(r, j, False).wait_send())
            for k in range(AG_KINDS):
                self.cp(r, k).wait_send()


class Reduce:
    def __init__(self, p, src, g, cs, cr, ps, pr, zs, zr):
        self.p, self.src, self.g = p, src, g
        self.cs, self.cr, self.ps, self.pr, self.zs, self.zr = cs, cr, ps, pr, zs, zr
        self.h, self.n = p.plan.half, p.plan.rows
        self.a, self.b, self.w = pl.ds(0, self.h), pl.ds(self.h, self.n - self.h), pl.ds(0, self.n)

    def cols(self, j):
        return pl.ds(0, ROW) if j is None else pl.ds(128 * j, 128)

    def rows(self, r, xx, yy, cc):
        plan = self.p.plan
        i = ((r * 2 + xx) * 2 + yy) * 2 + cc
        return pl.ds(pl.multiple_of(lax.div(i * plan.share, jnp.int32(ROW * TILE)) * TILE, TILE), self.n)

    def cb(self, u, xx, yy, part):
        r, j = self.p.plan.units[u]
        return self.g.at[r, xx, yy, 0, part, self.cols(j)]

    def pa(self, u, xx):
        r, j = self.p.plan.units[u]
        return self.g.at[r, 0, xx, 1, self.a, self.cols(j)]

    def pb(self, u, yy):
        r, j = self.p.plan.units[u]
        return self.g.at[r, 0, yy, 1, self.b, self.cols(j)]

    def p2(self, u, part):
        r, j = self.p.plan.units[u]
        return self.g.at[r, 1, 0, 1, part, self.cols(j)]

    def ccopy(self, u, xx, yy):
        p = self.p
        r, j = p.plan.units[u]
        return rcopy(
            self.src.at[self.rows(r, xx, yy, 1 - p.c), self.cols(j)], self.cb(u, xx, yy, self.w),
            self.cs.at[u, xx, yy], self.cr.at[u, xx, yy], p.C,
        )

    def cp(self, u, k):
        p = self.p
        x, y = p.x, p.y
        s, d, dev = (
            (self.cb(u, 0, 1 - y, self.a), self.pa(u, 0), p.Y),
            (self.cb(u, 1, 1 - y, self.a), self.pa(u, 1), p.Y),
            (self.cb(u, 1 - x, 0, self.b), self.pb(u, 0), p.X),
            (self.cb(u, 1 - x, 1, self.b), self.pb(u, 1), p.X),
            (self.pa(u, 1 - x), self.p2(u, self.a), p.X),
            (self.pb(u, 1 - y), self.p2(u, self.b), p.Y),
        )[k]
        return rcopy(s, d, self.ps.at[u, k], self.pr.at[u, k], dev)

    def zcopy(self, u):
        p = self.p
        r, j = p.plan.units[u]
        k = j or 0
        return rcopy(
            self.p2(u, self.w), self.g.at[p.z, 1, 1, 1, self.w, self.cols(j)],
            self.zs.at[u], self.zr.at[k, p.z], p.dev(z=r),
        )

    def zwait(self, j, s):
        ref = self.g.at[s, 1, 1, 1, self.w, self.cols(j)]
        rcopy(ref, ref, self.zs.at[0], self.zr.at[j or 0, s], self.p.dev(z=s)).wait_recv()

    def stage(self, s, u):
        p = self.p
        z, x, y = p.z, p.x, p.y
        r, j = p.plan.units[u]
        both = [(xx, yy) for xx in (0, 1) for yy in (0, 1)]
        if s == 0:
            for xx, yy in both:
                self.ccopy(u, xx, yy).start()
        if s == 1:
            for xx, yy in both:
                self.ccopy(u, xx, yy).wait_recv()
                ref = self.cb(u, xx, yy, self.w)
                ref[...] = ref[...] + self.src[self.rows(r, xx, yy, p.c), self.cols(j)]
            for q in (0, 1):
                self.cp(u, q).start()
                self.cp(u, 2 + q).start()
        if s == 2:
            for q in (0, 1):
                self.cp(u, q).wait_recv()
                ref = self.pa(u, q)
                ref[...] = ref[...] + self.cb(u, q, y, self.a)[...]
            self.cp(u, 4).start()
            for q in (0, 1):
                self.cp(u, 2 + q).wait_recv()
                ref = self.pb(u, q)
                ref[...] = ref[...] + self.cb(u, x, q, self.b)[...]
            self.cp(u, 5).start()
        if s == 3:
            self.cp(u, 4).wait_recv()
            ref = self.p2(u, self.a)
            ref[...] = ref[...] + self.pa(u, x)[...]
            self.cp(u, 5).wait_recv()
            ref = self.p2(u, self.b)
            ref[...] = ref[...] + self.pb(u, y)[...]
            when(z != r)(lambda: self.zcopy(u).start())

    def finish(self, out):
        z, plan = self.p.z, self.p.plan
        out[...] = self.g[z, 1, 0, 1].astype(F32)
        for s in range(plan.nz):
            def go():
                @pl.when(z >= plan.lo)
                def _():
                    self.zwait(None, s)

                @pl.when(z < plan.lo)
                def _():
                    for j in range(plan.slices):
                        self.zwait(None if plan.slices == 1 else j, s)

                out[...] += self.g[s, 1, 1, 1].astype(F32)

            when(z != s)(go)

    def drain(self):
        for u, (r, _) in enumerate(self.p.plan.units):
            for xx in (0, 1):
                for yy in (0, 1):
                    self.ccopy(u, xx, yy).wait_send()
            for k in range(RS_KINDS):
                self.cp(u, k).wait_send()
            when(self.p.z != r)(lambda: self.zcopy(u).wait_send())


class Corner:
    def __init__(self, p, t, rx, zt, ss, rs, zs, zr):
        self.p, self.t, self.rx, self.zt = p, t, rx, zt
        self.ss, self.rs, self.zs, self.zr = ss, rs, zs, zr

    def copy(self, k):
        p = self.p
        return rcopy(self.t.at[k], self.rx.at[k], self.ss.at[k], self.rs.at[k], (p.C, p.Y, p.X)[k])

    def zcopy(self, m):
        p = self.p
        return rcopy(
            self.t.at[3], self.zt.at[p.z], self.zs.at[m], self.zr.at[p.z], p.dev(z=p.plan.ends[m])
        )

    def senders(self, m):
        p = self.p
        return when(p.z != p.plan.ends[m], p.plan.early_pick(p.plan.ends[m], p.x, p.y))

    def start(self):
        self.copy(0).start()

    def step(self, k):
        self.copy(k).wait_recv()
        self.t[k + 1] = self.t[k] + self.rx[k]
        if k < 2:
            self.copy(k + 1).start()
        else:
            for m in range(len(self.p.plan.ends)):
                self.senders(m)(lambda: self.zcopy(m).start())

    def finish(self, r):
        p = self.p
        self.zt[r] = self.t[3]
        for s in range(p.plan.nz):
            if s != r:
                ref = self.zt.at[s]
                rcopy(ref, ref, self.zs.at[0], self.zr.at[s], p.dev(z=s)).wait_recv()

    def drain(self):
        for k in range(3):
            self.copy(k).wait_send()
        for m in range(len(self.p.plan.ends)):
            self.senders(m)(lambda: self.zcopy(m).wait_send())


def assemble(plan, g, lo, hi, store):
    for i in range(plan.count):
        at = lambda k: (k // 8, (k // 4) % 2, (k // 2) % 2, k % 2)
        s = plan.starts[i]
        e = plan.starts[i + 1] if i + 1 < plan.count else plan.padded
        if lo <= s < hi:
            head = g[at(i) + (slice(0, TILE),)]
            if i and s - plan.starts[i - 1] < plan.rows:
                d = s - plan.starts[i - 1]
                head = head + g[at(i - 1) + (slice(d, d + TILE),)]
            store(s, s + TILE, head)
        a, b = max(s + TILE, lo), min(e, hi, s + plan.rows)
        if b > a:
            store(a, b, g[at(i) + (slice(a - s, b - s),)])


class Shift:
    def __init__(self, plan, p):
        self.p, self.n, self.flat = p, plan.rows, plan.flat
        at = lax.rem(p.here() * plan.share, jnp.int32(ROW * TILE))
        self.q, self.s = lax.div(at, jnp.int32(128)), lax.rem(at, jnp.int32(128))
        self.high = lax.broadcasted_iota(jnp.int32, (1, 128), 1) >= self.s

    def load(self, wf, g):
        p, n, f = self.p, self.n, self.flat
        wf[0, 0:72, :] = jnp.zeros((72, 128), F32)
        wf[0, 72:72 + f, :] = pltpu.roll(wf[1, 0:f, :], self.s, 1)
        if 4 * n > f:
            wf[0, 72 + f:72 + 4 * n, :] = jnp.zeros((4 * n - f, 128), F32)
        a = wf[0, pl.ds(72 - self.q, 4 * n), :]
        b = wf[0, pl.ds(71 - self.q, 4 * n), :]
        wf[2, 0:4 * n, :] = jnp.where(self.high, a, b)
        for j in range(4):
            g[p.z, p.x, p.y, p.c, :, lanes(j)] = wf[2, pl.ds(j, n, stride=4), :].astype(BF)

    def store(self, wf, own, out):
        n, f = self.n, self.flat
        for j in range(4):
            wf[0, pl.ds(j, n, stride=4), :] = own[:, lanes(j)]
        wf[0, 4 * n:4 * n + 16, :] = jnp.zeros((16, 128), F32)
        a = wf[0, pl.ds(self.q, f), :]
        b = wf[0, pl.ds(self.q + 1, f), :]
        out[...] = pltpu.roll(jnp.where(self.high, a, b), lax.rem(128 - self.s, jnp.int32(128)), 1)


def mm(a, b):
    return lax.dot_general(a, b, (((1,), (0,)), ((), ())), preferred_element_type=F32)


def mm_nt(a, b):
    return lax.dot_general(a, b, (((1,), (1,)), ((), ())), preferred_element_type=F32)


def mm_tn(a, b):
    return lax.dot_general(a, b, (((0,), (0,)), ((), ())), preferred_element_type=F32)


def norm(h):
    mean = jnp.mean(h, axis=-1, keepdims=True)
    cen = h - mean
    inv = lax.rsqrt(jnp.mean(cen * cen, axis=-1, keepdims=True) + EPSILON)
    return cen * inv, inv


def norm_back(dn, n, inv):
    return (dn - jnp.mean(dn, axis=-1, keepdims=True) - n * jnp.mean(dn * n, axis=-1, keepdims=True)) * inv


def valid_len(lens, b):
    long = lens[0, 1] == 0
    short = lens[0, 0]
    for k in range(1, NB):
        short = jnp.where(b == k, lens[0, k], short)
    return jnp.where(long, lens[0, 0] - b * BLK, short)


def lane_half(par):
    lane = lax.broadcasted_iota(jnp.int32, (1, 128), 1)
    return (lane >= 64) if par else (lane < 64)


def key_bias(lens, qb):
    long = lens[0, 1] == 0
    cols = []
    it = lax.broadcasted_iota(jnp.int32, (BLK, 1), 0)
    for kb in range(NB):
        thr = jnp.where(long | (qb == kb), valid_len(lens, kb), 0)
        cols.append(jnp.where(it < thr, 0.0, -1e30).astype(F32))
    return jnp.concatenate(cols, axis=0)


def lanes(j):
    return slice(128 * j, 128 * j + 128)


def spread(wf, base):
    def store(a, b, val):
        for j in range(4):
            wf[j, a - base:b - base, :] = val[:, lanes(j)].astype(F32)
    return store


def regroup(wf, n, to):
    for c in range(n):
        for j in range(4):
            to[c, :, lanes(j)] = wf[j, pl.ds(c, 512, stride=n), :].astype(BF)


def put(wf, c, n, val):
    for j in range(4):
        wf[j, pl.ds(c, 512, stride=n), :] = val[:, lanes(j)]


def take(wf, n, out, base):
    for j in range(4):
        out[base:base + 512 * n, lanes(j)] = wf[j, 0:512 * n, :].astype(BF)


def phi_parts(v):
    cdf = 0.5 * (1.0 + lax.erf(v * (2.0 ** -0.5)))
    pdf = jnp.exp(v * v * -0.5) * (1.0 / math.sqrt(2.0 * math.pi))
    return cdf, pdf


def block_rows(b):
    return pl.ds(pl.multiple_of(b * BLK, BLK), BLK)


def body(plan, lens, ids, feat, x_hbm, cot_hbm, chunk_hbm, out_hbm, gin_hbm, own_flat,
         g, src, wf, wq, wu, wo, wd, vec, xs, cs, resid0, attn_in, qkv, attended, lse, ft,
         act, dpre, fin, dff, dbr, dres, datt, dqkv, accv, slots, small, cacc,
         ct, crx, czt, ht, hrx, hzt, tg, own,
         zs, zr, ps, pr, rcs, rcr, rps, rpr, rzs, rzr,
         css, crs, czs, czr, hss, hrs, hzs, hzr, ready, ins, outs, gins):
    p = Place(plan)
    nz = plan.nz
    corner = Corner(p, ct, crx, czt, css, crs, czs, czr)
    hints = Corner(p, ht, hrx, hzt, hss, hrs, hzs, hzr)
    place = lax.div(lax.broadcasted_iota(jnp.int32, (32, 1), 0), jnp.int32(4)) == (p.x * 2 + p.y) * 2 + p.c
    gather = Gather(p, g, zs, zr, ps, pr)
    loads = [
        pltpu.make_async_copy(chunk_hbm, wf.at[1, pl.ds(0, plan.flat)], ins.at[0]),
        pltpu.make_async_copy(x_hbm, xs, ins.at[1]),
        pltpu.make_async_copy(cot_hbm, cs, ins.at[2]),
    ]
    for cpy in loads:
        cpy.start()
    bar = pltpu.get_barrier_semaphore()
    signal_all(p, bar)
    shift = Shift(plan, p)
    loads[0].wait()
    shift.load(wf, g)
    wait_all(p, bar)

    for r in plan.early:
        gather.stage(0, r, plan.early_pick)
    for t in range(nz + 3):
        for s in (4, 3, 2, 1):
            for r in plan.early:
                if 0 <= t - (s - 1) < nz:
                    when(p.far(r) == t - (s - 1))(lambda: gather.stage(s, r, plan.early_pick))
    for r in plan.late:
        gather.stage(0, r, plan.late_pick)
    ht[0] = jnp.where(place, jnp.concatenate([feat[...].astype(F32)] * 4, axis=0), 0.0).astype(BF)
    hints.start()

    def gather_hook(i):
        for s in (1, 2, 3, 4):
            for r in plan.late:
                start = lax.div(9 * p.far(r) + 2, jnp.int32(2)) + (0, 0, 3, 6, 7)[s]
                when(i == jnp.minimum(start, HOOKS))(lambda: gather.stage(s, r, plan.late_pick))

    assemble(plan, g, 0, ROW_O, spread(wf, 0))
    regroup(wf, 3, wq)

    def tail_store(a, b, val):
        vec[a - ROW_T:b - ROW_T, :] = val

    assemble(plan, g, ROW_T, ROW_C + TAIL, tail_store)
    ctab = vec[256:288, :]
    vecs = vec[272:304, :].astype(F32)
    v0 = ROW_V - ROW_C - 16
    g1, b1, g2, b2, bq, bv, bo, bd = (vecs[v0 + k:v0 + k + 1] for k in range(8))
    ft[...] = mm(feat[...], vec[0:256, :])
    long = lens[0, 1] == 0
    loads[1].wait()

    def embed(b, _):
        gather_hook(b)
        rows = block_rows(b)
        oh = (lax.broadcasted_iota(jnp.int32, (32, BLK), 0) == ids[0:1, rows]).astype(F32).astype(BF)
        side = mm_tn(oh, ctab)
        slot = jnp.where(long, 0, b)
        h = xs[rows, :].astype(F32) + (side + ft[pl.ds(slot, 1), :])
        resid0[rows, :] = h
        n, _i = norm(h)
        a = (n * g1 + b1).astype(BF)
        attn_in[rows, :] = a
        for c in range(3):
            pr_ = mm(a, wq[c])
            if c == 0:
                pr_ = (pr_ + bq) * (SCALE * LOG2E)
            if c == 2:
                pr_ = pr_ + bv
            pr_ = pr_.astype(BF)
            for j in range(4):
                qkv[4 * c + j, rows, :] = pr_[:, lanes(j)]
        return 0

    lax.fori_loop(0, NB, embed, 0)
    ones = jnp.ones((T, 128), BF)

    def attend(i, _):
        gather_hook(i + NB)
        pair, qb = lax.div(i, NB), lax.rem(i, NB)
        rows = block_rows(qb)
        q = qkv[pair, rows, :]
        k = qkv[PAIRS + pair]
        va = jnp.concatenate([qkv[2 * PAIRS + pair], ones], axis=1)
        bias = key_bias(lens, qb)
        heads = []
        for par in (0, 1):
            qm = jnp.where(lane_half(par), q, jnp.zeros_like(q))
            s = mm_nt(k, qm) + bias
            m = jnp.max(s, axis=0, keepdims=True)
            e = jnp.exp2(s - m)
            l = jnp.sum(e, axis=0, keepdims=True)
            lse[pl.ds(2 * pair + par, 1), rows] = m + jnp.log(l) * LOG2E
            oa = mm_tn(e.astype(BF), va)
            heads.append(oa[:, :128] / oa[:, 128:])
        attended[pair, rows, :] = jnp.where(lane_half(0), heads[0], heads[1]).astype(BF)
        return 0

    lax.fori_loop(0, PAIRS * NB, attend, 0)
    gather_hook(HOOKS)

    def wo_store(a, b, val):
        wo[a - ROW_O:b - ROW_O, :] = val

    def wd_store(a, b, val):
        wd[a - ROW_DOWN:b - ROW_DOWN, :] = val

    assemble(plan, g, ROW_O, ROW_UP, wo_store)
    assemble(plan, g, ROW_UP, ROW_DOWN, spread(wf, ROW_UP))
    assemble(plan, g, ROW_DOWN, ROW_T, wd_store)
    regroup(wf, 4, wu)
    hints.step(0)
    gather.drain()
    signal_all(p, ready)
    small[...] = jnp.zeros_like(small)
    loads[2].wait()

    def feed(b, _):
        rows = block_rows(b)
        att = jnp.concatenate([attended[j, rows, :] for j in range(PAIRS)], axis=1)
        h = resid0[rows, :] + (mm(att, wo[...]) + bo)
        n, inv = norm(h)
        f = (n * g2 + b2).astype(BF)
        fin[rows, :] = f
        ok = lax.broadcasted_iota(jnp.int32, (BLK, 1), 0) < valid_len(lens, b)
        do = jnp.where(ok, cs[rows, :].astype(F32), 0.0)
        d = do.astype(BF)
        dff[rows, :] = d
        small[0:1, :] += jnp.sum(do, axis=0, keepdims=True)
        acc = h + bd
        e2 = jnp.zeros((BLK, D), F32)
        for c in range(4):
            pre = mm(f, wu[c]) + vecs[v0 + 8 + c:v0 + 9 + c]
            cdf, pdf = phi_parts(pre)
            a = (pre * cdf).astype(BF)
            wdc = wd[512 * c:512 * c + 512, :]
            dp = (mm_nt(d, wdc) * (cdf + pre * pdf)).astype(BF)
            act[c, rows, :] = a
            dpre[c, rows, :] = dp
            small[4 + c:5 + c, :] += jnp.sum(dp.astype(F32), axis=0, keepdims=True)
            acc = acc + mm(a, wdc)
            e2 = e2 + mm_nt(dp, wu[c])
        xs[rows, :] = acc.astype(BF)
        pltpu.make_async_copy(xs.at[rows], out_hbm.at[0, rows], outs.at[b]).start()
        small[1:2, :] += jnp.sum(e2 * n, axis=0, keepdims=True)
        small[2:3, :] += jnp.sum(e2, axis=0, keepdims=True)
        dr = do + norm_back(e2 * g2, n, inv)
        dres[rows, :] = dr
        db = dr.astype(BF)
        dbr[rows, :] = db
        small[3:4, :] += jnp.sum(db.astype(F32), axis=0, keepdims=True)
        da = mm_nt(db, wo[...]).astype(BF)
        for j in range(PAIRS):
            datt[j, rows, :] = da[:, lanes(j)]
        return 0

    lax.fori_loop(0, NB, feed, 0)
    hints.step(1)
    src[ROW_T:plan.padded, :] = jnp.zeros((plan.padded - ROW_T, ROW), BF)
    for c in range(4):
        src[ROW_DOWN + 512 * c:ROW_DOWN + 512 * c + 512, :] = mm_tn(act[c], dff[...]).astype(BF)
        put(wf, c, 4, mm_tn(fin[...], dpre[c]))
    take(wf, 4, src, ROW_UP)
    for j in range(PAIRS):
        src[ROW_O + 128 * j:ROW_O + 128 * j + 128, :] = mm_tn(attended[j], dbr[...]).astype(BF)

    reduce = Reduce(p, src, g, rcs, rcr, rps, rpr, rzs, rzr)
    hints.step(2)
    wait_all(p, ready)
    for u in range(plan.body_units):
        reduce.stage(0, u)

    def qkv_grad(j):
        dq = jnp.concatenate([dqkv[4 * c + j] for c in range(3)], axis=1)
        gq = mm_tn(attn_in[...], dq)
        for c in range(3):
            wf[j, pl.ds(c, 512, stride=3), :] = gq[:, lanes(c)]
        src[0:ROW_O, lanes(j)] = wf[j, 0:ROW_O, :].astype(BF)
        for c in (0, 2):
            slots[10 + c // 2:11 + c // 2, lanes(j)] = jnp.sum(dqkv[4 * c + j].astype(F32), axis=0, keepdims=True)

    def slice_start(j):
        qkv_grad(j)
        if plan.slices > 1:
            for u in plan.slice_units(j):
                reduce.stage(0, u)

    def reduce_at(s, u):
        return lambda: reduce.stage(s, u)

    steps = []
    for k in range(plan.body_units):
        for s, at in ((1, 1 + 4 * k), (2, 4 + 4 * k), (3, 7 + 4 * k)):
            steps.append((at, -s, reduce_at(s, k)))
    for j in range(PAIRS - 1):
        steps.append((NB * (j + 1), 0, lambda j=j: slice_start(j)))
        if plan.slices > 1:
            for s, at in ((1, (10, 11, 14)[j]), (2, (12, 13, 15)[j]), (3, (14, 15, 16)[j])):
                for u in plan.slice_units(j):
                    steps.append((at, -s, reduce_at(s, u)))
    steps.sort(key=lambda e: e[:2])

    def reduce_hook(i):
        for at, _, run in steps:
            if at < PAIRS * NB:
                pl.when(i == at)(run)

    head = lax.broadcasted_iota(jnp.int32, (8, 128), 1) // 64
    both = jnp.where(head == lax.broadcasted_iota(jnp.int32, (8, 128), 0), 1.0, 0.0).astype(BF)

    def attend_back(i, _):
        reduce_hook(i)
        pair, qb = lax.div(i, NB), lax.rem(i, NB)
        rows = block_rows(qb)
        q = qkv[pair, rows, :]
        k = qkv[PAIRS + pair]
        v = qkv[2 * PAIRS + pair]
        do = datt[pair, rows, :]
        bias = key_bias(lens, qb)
        prod = attended[pair, rows, :].astype(F32) * do.astype(F32)
        high = prod.astype(BF)
        delta = mm_nt(both, high) + mm_nt(both, (prod - high.astype(F32)).astype(BF))
        dqs = []

        @pl.when(qb == 0)
        def _():
            accv[...] = jnp.zeros_like(accv)

        for par in (0, 1):
            half = lane_half(par)
            qm = jnp.where(half, q, jnp.zeros_like(q))
            dm = jnp.where(half, do, jnp.zeros_like(do))
            pp = jnp.exp2(mm_nt(k, qm) + bias - lse[pl.ds(2 * pair + par, 1), rows])
            dp = mm_nt(v, dm)
            ds = (pp * (dp - delta[par:par + 1])).astype(BF)
            accv[1] += mm(pp.astype(BF), dm)
            accv[0] += mm(ds, qm)
            dqs.append(mm_tn(ds, k))
        dqkv[pair, rows, :] = (jnp.where(lane_half(0), dqs[0], dqs[1]) * SCALE).astype(BF)

        @pl.when(qb == NB - 1)
        def _():
            dqkv[PAIRS + pair] = (accv[0] * (1.0 / LOG2E)).astype(BF)
            dqkv[2 * PAIRS + pair] = accv[1].astype(BF)
        return 0

    lax.fori_loop(0, PAIRS * NB, attend_back, 0)
    slice_start(PAIRS - 1)
    last = plan.slice_units(plan.slices - 1)
    if plan.slices == 1:
        for u in last:
            reduce.stage(0, u)
    for at, _, run in steps:
        if at >= PAIRS * NB:
            run()
    slots[0:10, :] = jnp.zeros((10, D), F32)
    cacc[...] = jnp.zeros_like(cacc)

    def embed_back(b, _):
        rows = block_rows(b)

        @pl.when(b == 1)
        def _():
            for u in last:
                reduce.stage(1, u)

        @pl.when(b == 3)
        def _():
            for u in last:
                reduce.stage(2, u)

        e1 = jnp.zeros((BLK, D), F32)
        for c in range(3):
            dq = jnp.concatenate([dqkv[4 * c + j, rows, :] for j in range(4)], axis=1)
            e1 = e1 + mm_nt(dq, wq[c])
        n, inv = norm(resid0[rows, :])
        slots[8:9, :] += jnp.sum(e1 * n, axis=0, keepdims=True)
        slots[9:10, :] += jnp.sum(e1, axis=0, keepdims=True)
        gi = dres[rows, :] + norm_back(e1 * g1, n, inv)
        resid0[rows, :] = gi
        pltpu.make_async_copy(resid0.at[rows], gin_hbm.at[0, rows], gins.at[b]).start()
        ds = gi.astype(BF)
        oh = (lax.broadcasted_iota(jnp.int32, (32, BLK), 0) == ids[0:1, rows]).astype(F32).astype(BF)
        cacc[0:32, :] += mm(oh, ds)
        total = jnp.sum(ds.astype(F32), axis=0, keepdims=True)
        slots[pl.ds(b, 1), :] = total
        slots[pl.ds(b + NB, 1), :] = total
        return 0

    lax.fori_loop(0, NB, embed_back, 0)
    per = slots[0:8, :]
    total = 0.5 * jnp.sum(per, axis=0, keepdims=True)
    first = lax.rem(lax.broadcasted_iota(jnp.int32, (8, 1), 0), jnp.int32(NB)) == 0
    per = jnp.where(long, jnp.where(first, total, 0.0), per)
    ct[0, 0:32, :] = jnp.where(place, jnp.concatenate([per] * 4, axis=0), 0.0).astype(BF)
    o = ROW_V - ROW_C
    cacc[o:o + 2, :] = slots[8:10, :]
    cacc[o + 2:o + 4, :] = small[1:3, :]
    cacc[o + 4:o + 5, :] = slots[10:11, :]
    cacc[o + 5:o + 6, :] = slots[11:12, :]
    cacc[o + 6:o + 7, :] = small[3:4, :]
    cacc[o + 7:o + 8, :] = small[0:1, :]
    cacc[o + 8:o + 12, :] = small[4:8, :]
    ct[0, 32:32 + TAIL, :] = cacc[...].astype(BF)
    corner.start()
    for u in last:
        reduce.stage(3, u)
    for k in range(3):
        corner.step(k)
    reduce.finish(own)
    for r in plan.ends:
        def tail():
            hints.finish(r)
            corner.finish(r)
            tg[0:256, :] = mm_tn(
                jnp.concatenate([hzt[s] for s in range(nz)], axis=0),
                jnp.concatenate([czt[s, 0:32, :] for s in range(nz)], axis=0),
            )
            rest = czt[0, 32:32 + TAIL, :].astype(F32)
            for s in range(1, nz):
                rest = rest + czt[s, 32:32 + TAIL, :].astype(F32)
            tg[256:256 + TAIL, :] = rest

        when(p.z == r, plan.early_pick(r, p.x, p.y))(tail)
    for i in plan.owners:
        @pl.when(p.here() == i)
        def _():
            at = plan.starts[i]
            a, b = max(at, ROW_T), min(at + plan.rows, ROW_C + TAIL)
            own[a - at:b - at, :] += tg[a - ROW_T:b - ROW_T, :]
    shift.store(wf, own, own_flat)
    hints.drain()
    corner.drain()
    reduce.drain()
    for b in range(NB):
        rows = pl.ds(b * BLK, BLK)
        pltpu.make_async_copy(xs.at[rows], out_hbm.at[0, rows], outs.at[b]).wait()
        pltpu.make_async_copy(resid0.at[rows], gin_hbm.at[0, rows], gins.at[b]).wait()


def layer(plan, lens, ids, feat, x, cot, chunk):
    S = jax.ShapeDtypeStruct
    V = pltpu.VMEM
    DM = pltpu.SemaphoreType.DMA
    nz, n, nu, ne = plan.nz, plan.rows, len(plan.units), len(plan.ends)
    vm = pl.BlockSpec(memory_space=pltpu.VMEM)
    hb = pl.BlockSpec(memory_space=pl.ANY)

    def kernel(*refs):
        body(plan, *refs)

    return pl.pallas_call(
        kernel,
        out_shape=[S((1, T, D), BF), S((1, T, D), F32), S((plan.flat, 128), F32)],
        in_specs=[pl.BlockSpec(memory_space=pltpu.SMEM), vm, vm, hb, hb, hb],
        out_specs=[hb, hb, vm],
        scratch_shapes=[
            V((nz, 2, 2, 2, n, ROW), BF), V((plan.padded, ROW), BF), V((4, 2048, 128), F32),
            V((3, D, D), BF), V((4, D, D), BF), V((D, D), BF), V((2048, D), BF), V((256 + TAIL, D), BF),
            V((T, D), BF), V((T, D), BF), V((T, D), F32), V((T, D), BF), V((12, T, 128), BF),
            V((PAIRS, T, 128), BF), V((8, T), F32), V((8, D), F32),
            V((4, T, D), BF), V((4, T, D), BF), V((T, D), BF), V((T, D), BF), V((T, D), BF), V((T, D), F32),
            V((PAIRS, T, 128), BF), V((12, T, 128), BF), V((2, T, 128), F32), V((16, D), F32), V((8, D), F32),
            V((TAIL, D), F32),
            V((4, 32 + TAIL, D), BF), V((3, 32 + TAIL, D), BF), V((nz, 32 + TAIL, D), BF),
            V((4, 32, 256), BF), V((3, 32, 256), BF), V((nz, 32, 256), BF), V((256 + TAIL, D), F32), V((n, ROW), F32),
            DM((nz, 2, 2)), DM((nz, 2)), DM((nz, AG_KINDS)), DM((nz, AG_KINDS)),
            DM((nu, 2, 2)), DM((nu, 2, 2)), DM((nu, RS_KINDS)), DM((nu, RS_KINDS)), DM((nu,)), DM((PAIRS, nz)),
            DM((3,)), DM((3,)), DM((ne,)), DM((nz,)), DM((3,)), DM((3,)), DM((ne,)), DM((nz,)),
            pltpu.SemaphoreType.REGULAR, DM((3,)), DM((NB,)), DM((NB,)),
        ],
        compiler_params=pltpu.CompilerParams(
            collective_id=0, has_side_effects=True, vmem_limit_bytes=67043328
        ),
        name="layer",
    )(lens, ids, feat, x, cot, chunk)


def time_features(steps):
    half = 128
    freqs = jnp.exp(-math.log(10000.0) * jnp.arange(half, dtype=F32) / half)
    ang = steps.astype(F32).reshape(4, 1) * freqs
    f = jnp.concatenate([jnp.sin(ang), jnp.cos(ang)], axis=-1).astype(BF)
    return jnp.concatenate([f, f], axis=0)


def shards(inputs, noisy_ids, timesteps, doc_lens, cotangent, params, momentum, average):
    ndp, nfs = lax.axis_size("dp"), lax.axis_size("fsdp")
    device_count = ndp * nfs
    row_count, seq_len, model_width = inputs.shape
    plan = Plan(ndp, nfs, params.shape[0] * device_count)
    chunk = jnp.pad(params, (0, plan.flat * 128 - plan.share)).reshape(plan.flat, 128)
    output, input_grad, owned = layer(
        plan, doc_lens, noisy_ids, time_features(timesteps),
        inputs.reshape(T, D), cotangent.reshape(T, D), chunk,
    )
    owned_grad = owned.reshape(-1)[:plan.share]
    gradient = owned_grad * (1.0 / math.sqrt(row_count * seq_len * device_count))
    new_momentum = MOMENTUM_RATE * momentum + gradient
    new_params = params - LEARN_RATE * (gradient + MOMENTUM_RATE * new_momentum)
    new_average = AVERAGE_RATE * average + (1.0 - AVERAGE_RATE) * new_params
    return (
        output,
        input_grad,
        new_params,
        new_momentum,
        new_average,
        new_params.astype(BF),
    )


def solution(mesh):
    rows = ("dp", "fsdp")
    in_specs = (
        P(rows, None, None), P(rows, None), P(rows, None), P(rows, None), P(rows, None, None),
        P(rows), P(rows), P(rows),
    )
    out_specs = (P(rows, None, None), P(rows, None, None), P(rows), P(rows), P(rows), P(rows))
    return jax.shard_map(shards, mesh=mesh, in_specs=in_specs, out_specs=out_specs, check_vma=False)
```
